32 devices in a mesh: dp: 8 (over y, x, core), section: 4 (over z).
Axes of the slice: x: 2, y: 2, z: 4, core: 2. Of those that a mesh axis runs over, the one named last changes fastest.
Arguments:
- features: bfloat16 [4, 4096, 768], P(None, ('dp', 'section')), may hold values from -6 to 6
- packing: int32 [4, 8, 512], P(None, 'dp'), may hold values from 0 to 511, each once within a row
- segment_ids: int32 [4, 8, 512], P(None, 'dp'), may hold values from 0 to 5, never falling along the last dimension, each value on 1 to 196 neighbouring positions
- norm1_gain: float32 [768], replicated, may hold values from 0.5 to 1.5
- norm1_shift: float32 [768], replicated, may hold values from -1.5 to 1.5
- project_weight: bfloat16 [3, 768, 768], P(None, 'dp', 'section'), may hold values from -0.21875 to 0.21875
- project_bias: float32 [2, 768], replicated, may hold values from -2.5 to 2.5
- merge_weight: bfloat16 [768, 768], P('section', 'dp'), may hold values from -0.875 to 0.875
- merge_bias: float32 [768], replicated, may hold values from -1.5 to 1.5
- norm2_gain: float32 [768], replicated, may hold values from 0.5 to 1.5
- norm2_shift: float32 [768], replicated, may hold values from -1.5 to 1.5
- expand_weight: bfloat16 [768, 3072], P('dp', 'section'), may hold values from -0.21875 to 0.21875
- expand_bias: float32 [3072], replicated, may hold values from -2.5 to 2.5
- reduce_weight: bfloat16 [3072, 768], P('section', 'dp'), may hold values from -0.109375 to 0.109375
- reduce_bias: float32 [768], replicated, may hold values from -1.5 to 1.5
- cotangent: bfloat16 [4, 4096, 768], P(None, ('dp', 'section')), may hold values from -6 to 6
Outputs:
- output: bfloat16 [4, 4096, 768], P(None, ('dp', 'section'))
- features_grad: float32 [4, 4096, 768], P(None, ('dp', 'section'))
- norm1_gain_grad: float32 [768], replicated
- norm1_shift_grad: float32 [768], replicated
- project_weight_grad: float32 [3, 768, 768], P(None, 'dp', 'section')
- project_bias_grad: float32 [2, 768], replicated
- merge_weight_grad: float32 [768, 768], P('section', 'dp')
- merge_bias_grad: float32 [768], replicated
- norm2_gain_grad: float32 [768], replicated
- norm2_shift_grad: float32 [768], replicated
- expand_weight_grad: float32 [768, 3072], P('dp', 'section')
- expand_bias_grad: float32 [3072], replicated
- reduce_weight_grad: float32 [3072, 768], P('section', 'dp')
- reduce_bias_grad: float32 [768], replicated
The draws below stay inside these ranges and needn't reach their ends.
Inputs may be any that keep to these rules, and one draw needn't show every extreme that they name: packing[b, g] lists each of the 512 token positions of its group once. `segment_ids`: along a row segment numbers never fall; a segment spans 1 to 196 consecutive packed positions, one exactly 196.
All inputs are finite; a program needn't handle non-finite values.
Results may differ from the reference program's by a relative error of at most 0.012.
Values may be sent and summed in bfloat16 or wider, within the bound.
A program may use at most 128 MiB of HBM per device.

```python
import math
import jax
import jax.numpy as jnp
import numpy as np
from jax import lax

D = 768
HEADS = 12
HEAD_DIM = 64
FF = 3072
TOK = 512
MB = 4
SEGLEN = 196
GROUPS = 8
TOKENS = 4096


def block_scale(own_key, extent, cuts, smallest, high):
    def one(dim, parts):
        heights = jax.random.uniform(jax.random.fold_in(jax.random.fold_in(own_key, 6), dim), (parts,), jnp.float32, smallest / len(cuts), high / len(cuts))
        return jnp.repeat(jnp.exp(heights), extent[dim] // parts).reshape((-1,) + (1,) * (len(extent) - dim - 1))

    level = one(*cuts[0])
    for cut in cuts[1:]:
        level = level * one(*cut)
    return level


def profile(count, total, reach, skew):
    loads = [(1 << 20) // math.isqrt(grade ** skew) + 1 for grade in range(2, count + 1)]
    rest, counts = total - reach - (count - 1), [1] * (count - 1)
    while rest > 0:
        candidates = [i for i in range(count - 1) if counts[i] < reach]
        mass, budget = sum([loads[i] for i in candidates]), rest
        for i in candidates:
            extra = min(reach - counts[i], max(1, budget * loads[i] // mass), rest)
            counts[i] = counts[i] + extra
            rest = rest - extra
    return np.array([reach] + counts)


def ragged_sizes(stream_key, amount, total, reach, lean):
    if amount == 2:
        one = jax.random.randint(stream_key, (), max(1, total - reach), min(reach, total - 1) + 1)
        return jnp.stack([one, total - one])
    sizes = jnp.asarray(profile(amount, total, reach, lean), jnp.int32)
    twos = (amount - 1) // 2
    donor, receiver = sizes[1:1 + 2 * twos:2], sizes[2:2 + 2 * twos:2]
    margin = jnp.minimum(donor - 1, reach - receiver)
    moved = jax.random.randint(jax.random.fold_in(stream_key, 1), (twos,), 0, 1 << 20) % (margin + 1)
    sizes = sizes.at[1:1 + 2 * twos:2].set(donor - moved).at[2:2 + 2 * twos:2].set(receiver + moved)
    return sizes[jax.random.permutation(jax.random.fold_in(stream_key, 2), amount)]


def normal_values(key, extent, scale, most, shards=(), kind=jnp.bfloat16):
    values = jax.random.normal(key, extent, jnp.float32) * scale
    if len(shards) > 0:
        values = block_scale(key, extent, shards, -0.22, 0.18) * values
    return jnp.clip(values, min=-most, max=most).astype(kind)


def setup_inputs(seed: int = 0) -> dict:
    seeds = jax.random.split(jax.random.key(seed), 17)
    return {
        "features": normal_values(seeds[0], (MB, TOKENS, D), 1.0, 6.0, ((1, 32),)),
        "packing": jax.vmap(lambda own: jax.random.permutation(own, TOK))(jax.random.split(seeds[1], MB * GROUPS)).reshape((MB, GROUPS, TOK)).astype(jnp.int32),
        "segment_ids": jax.vmap(lambda own: jnp.searchsorted(jnp.cumsum(ragged_sizes(own, TOK // (SEGLEN // 2) + 1, TOK, SEGLEN, 1)), jnp.arange(TOK), side="right"))(jax.random.split(seeds[2], MB * GROUPS)).reshape((MB, GROUPS, TOK)).astype(jnp.int32),
        "norm1_gain": jnp.clip(1.0 + 0.1 * jax.random.normal(seeds[3], (D,), jnp.float32), 0.5, 1.5),
        "norm1_shift": normal_values(seeds[4], (D,), 0.3, 1.5, (), jnp.float32),
        "project_weight": normal_values(seeds[5], (3, D, D), D ** -0.5, 0.21875, ((1, 8), (2, 4))),
        "project_bias": normal_values(seeds[6], (2, D), 0.5, 2.5, (), jnp.float32),
        "merge_weight": normal_values(seeds[7], (D, D), (D // 16) ** -0.5, 0.875, ((0, 4), (1, 8))),
        "merge_bias": normal_values(seeds[8], (D,), 0.3, 1.5, (), jnp.float32),
        "norm2_gain": jnp.clip(1.0 + 0.1 * jax.random.normal(seeds[9], (D,), jnp.float32), 0.5, 1.5),
        "norm2_shift": normal_values(seeds[10], (D,), 0.3, 1.5, (), jnp.float32),
        "expand_weight": normal_values(seeds[11], (D, FF), D ** -0.5, 0.21875, ((0, 8), (1, 4))),
        "expand_bias": normal_values(seeds[12], (FF,), 0.5, 2.5, (), jnp.float32),
        "reduce_weight": normal_values(seeds[13], (FF, D), FF ** -0.5, 0.109375, ((0, 4), (1, 8))),
        "reduce_bias": normal_values(seeds[14], (D,), 0.3, 1.5, (), jnp.float32),
        "cotangent": normal_values(seeds[15], (MB, TOKENS, D), 1.0, 6.0, ((1, 32),)),
    }


EPSILON = 1e-06
MASKED = -1000000000.0

@jax.custom_vjp
def low(v):
    return lax.optimization_barrier(v.astype(jnp.bfloat16)).astype(jnp.float32)

@jax.custom_vjp
def low_back(v):
    return v

def low_keep(v):
    return (low(v), None)

def low_pass(kept, grad):
    return (grad,)

def back_keep(v):
    return (v, None)

def back_low(kept, grad):
    return (low(grad),)
low.defvjp(low_keep, low_pass)
low_back.defvjp(back_keep, back_low)

def norm_rows(values, gain, shift):
    center = values - lax.optimization_barrier(jnp.mean(values, axis=-1, keepdims=True))
    spread = lax.optimization_barrier(jnp.mean(center * center, axis=-1, keepdims=True))
    return center * lax.rsqrt(spread + EPSILON) * gain + shift

def matmul(left, right):
    return jnp.dot(left, right, precision=lax.Precision.HIGHEST)

def sequence(tokens, order, labels, params):
    norm1_gain, norm1_shift, project_weight, project_bias, merge_weight, merge_bias, norm2_gain, norm2_shift, expand_weight, expand_bias, reduce_weight, reduce_bias = params
    length = tokens.shape[0]
    normed = low(norm_rows(tokens, norm1_gain, norm1_shift))
    packed = normed[order]
    queries = low_back(low(matmul(packed, project_weight[0]) + project_bias[0]))
    keys = low_back(low(matmul(packed, project_weight[1])))
    values = low_back(low(matmul(packed, project_weight[2]) + project_bias[1]))
    queries = queries.reshape(length, HEADS, HEAD_DIM)
    keys = keys.reshape(length, HEADS, HEAD_DIM)
    values = values.reshape(length, HEADS, HEAD_DIM)
    scores = jnp.einsum('qhd,khd->hqk', queries, keys, precision=lax.Precision.HIGHEST) * HEAD_DIM ** (-0.5)
    scores = low_back(scores)
    allowed = labels[:, None] == labels[None, :]
    scores = jnp.where(allowed[None], scores, MASKED)
    peak = lax.optimization_barrier(jnp.max(scores, axis=-1, keepdims=True))
    weights = jnp.exp(scores - peak)
    probs = low(weights / lax.optimization_barrier(jnp.sum(weights, axis=-1, keepdims=True)))
    mixed = jnp.einsum('hqk,khd->qhd', probs, values, precision=lax.Precision.HIGHEST).reshape(length, D)
    mixed = low_back(low(mixed))
    inverse = jnp.zeros((length,), jnp.int32).at[order].set(jnp.arange(length, dtype=jnp.int32))
    branch = low_back(matmul(mixed[inverse], merge_weight) + merge_bias)
    middle = tokens + branch
    normed_two = low(norm_rows(middle, norm2_gain, norm2_shift))
    hidden = low_back(matmul(normed_two, expand_weight) + expand_bias)
    active = low(jax.nn.gelu(hidden, approximate=False))
    second = low_back(matmul(active, reduce_weight) + reduce_bias)
    return middle + second

def reference(features, packing, segment_ids, norm1_gain, norm1_shift, project_weight, project_bias, merge_weight, merge_bias, norm2_gain, norm2_shift, expand_weight, expand_bias, reduce_weight, reduce_bias, cotangent):
    params = tuple((item.astype(jnp.float32) for item in (norm1_gain, norm1_shift, project_weight, project_bias, merge_weight, merge_bias, norm2_gain, norm2_shift, expand_weight, expand_bias, reduce_weight, reduce_bias)))
    orders = packing.reshape(MB * GROUPS, TOK).astype(jnp.int32)
    labels = segment_ids.reshape(MB * GROUPS, TOK).astype(jnp.int32)

    def forward(tokens, *weights):
        pieces = tokens.reshape(MB * GROUPS, TOK, D)
        checked = jax.checkpoint(lambda item: sequence(item[0], item[1], item[2], weights))
        results = lax.map(checked, (pieces, orders, labels))
        return results.reshape(MB, TOKENS, D)
    result, pullback = jax.vjp(forward, features.astype(jnp.float32), *params)
    grads = pullback(cotangent.astype(jnp.float32))
    return (result.astype(jnp.bfloat16), grads[0], grads[1], grads[2], grads[3], grads[4], grads[5], grads[6], grads[7], grads[8], grads[9], grads[10], grads[11], grads[12])
```

```python
import functools

import jax
import jax.numpy as jnp
from jax import lax
from jax.experimental import pallas as pl
from jax.experimental.pallas import tpu as pltpu
from jax.sharding import PartitionSpec as P

HEAD_DIM = 64
EPSILON = 1e-06
MASKED = -1000000000.0
F32 = jnp.float32
BF16 = jnp.bfloat16
MESH_ID = pl.DeviceIdType.MESH

NS = 4
D = 768
TOK = 512
ROWS = 96
HALF = 48
SEC = 192
NT_DIMS = (((1,), (1,)), ((), ()))
TN_DIMS = (((0,), (0,)), ((), ()))
CORE, XOWN, YOWN, XFWD, YFWD = range(5)
CHUNK = 128


def norm_stats(values):
    center = values - jnp.mean(values, axis=-1, keepdims=True)
    spread = jnp.mean(center * center, axis=-1, keepdims=True)
    scale = lax.rsqrt(spread + EPSILON)
    return center * scale, scale


def norm_grad(normal, scale, grad, gain):
    scaled = grad * gain
    first = jnp.mean(scaled, axis=-1, keepdims=True)
    second = jnp.mean(scaled * normal, axis=-1, keepdims=True)
    return scale * (scaled - first - normal * second)


def dot(left, right, dims=(((1,), (0,)), ((), ()))):
    return lax.dot_general(left, right, dims, preferred_element_type=F32)


def column_sum(values):
    return jnp.sum(values, axis=0, keepdims=True)


def block_kernel(
    features, packing, segments, gain1, shift1, project, project_bias, merge, merge_bias, gain2, shift2,
    expand, expand_bias, reduce, reduce_bias, cotangent,
    out, features_grad, gain1_grad, shift1_grad, project_grad, project_bias_grad, merge_grad, merge_bias_grad,
    gain2_grad, shift2_grad, expand_grad, expand_bias_grad, reduce_grad, reduce_bias_grad,
    W, G, RC, RD, RE, RZ, X, U, UT, N1, N1T, N2, N2T, QA, MID, ACC1, ACC2, AC, GH, GA, MASK, LSE, PB, SG, SGR, FS, FR, TB,
    z_send, z_recv, g_send, g_recv, r_send, r_recv, rz_send, rz_recv, in_send, in_recv, out_send, out_recv, sg_send, sg_recv,
    local_sem, credit, fw_sem,
):
    dp = lax.axis_index("dp")
    z = lax.axis_index("section")
    c = dp % 2
    k = dp // 2
    xi = k % 2
    yi = k // 2
    kx = 2 * yi + (1 - xi)
    ky = 2 * (1 - yi) + xi
    kd = 3 - k
    x_dev = {"dp": 2 * kx + c, "section": z}
    y_dev = {"dp": 2 * ky + c, "section": z}
    c_dev = {"dp": 2 * k + (1 - c), "section": z}

    def z_dev(other):
        return {"dp": dp, "section": other}

    half = z // 2
    start = (1 - half) * (z % 2) + half * (1 - z % 2)

    def s_of(t):
        base = (t // 2) * t + (1 - t // 2) * ((start + t) % 2)
        return half * 3 + (1 - 2 * half) * base

    def remote(src, dst, send, recv, device):
        return pltpu.make_async_remote_copy(
            src_ref=src, dst_ref=dst, send_sem=send, recv_sem=recv, device_id=device, device_id_type=MESH_ID
        )

    barrier = pltpu.get_barrier_semaphore()
    for device in (x_dev, y_dev, c_dev):
        pl.semaphore_signal(barrier, inc=1, device_id=device, device_id_type=MESH_ID)
    for step in range(1, NS):
        pl.semaphore_signal(barrier, inc=1, device_id=z_dev((z + step) % NS), device_id_type=MESH_ID)

    for piece in range(3):
        TB[:, piece * SEC : (piece + 1) * SEC] = project[piece].astype(F32)
    TB[:, 3 * SEC :] = merge[...].astype(F32).T
    W[0, pl.ds(z, 1), pl.ds(k, 1), pl.ds(c, 1)] = TB[...].astype(BF16)[None, None, None]
    W[1, pl.ds(z, 1), pl.ds(k, 1), pl.ds(c, 1)] = expand[...][None, None, None]
    W[2, pl.ds(z, 1), pl.ds(k, 1), pl.ds(c, 1)] = reduce[...][None, None, None]
    pl.semaphore_wait(barrier, 6)

    def z_copy(m, s, up):
        place = W.at[m, s, k, c]
        return remote(place, place, z_send.at[up, m, s], z_recv.at[m, s], z_dev(z + 2 * up - 1))

    def z_pass(m, s):
        @pl.when((s <= z) & (z < NS - 1))
        def _():
            z_copy(m, s, 1).start()

        @pl.when((s >= z) & (z > 0))
        def _():
            z_copy(m, s, 0).start()

    def plane_copy(kind, m, s, receive=False):
        rows = slice(None)
        if kind == CORE:
            place = W.at[m, s, :, (1 - c) if receive else c]
            return remote(place, place, g_send.at[kind, m, s], g_recv.at[kind, m, s], c_dev)
        if kind == XOWN:
            place = W.at[m, s, kx if receive else k, c]
            return remote(place, place, g_send.at[kind, m, s], g_recv.at[kind, m, s], x_dev)
        if kind == YOWN:
            place = W.at[m, s, ky if receive else k, c]
            return remote(place, place, g_send.at[kind, m, s], g_recv.at[kind, m, s], y_dev)
        if kind == XFWD:
            place = W.at[m, s, kd if receive else ky, c, pl.ds(0, HALF)]
            return remote(place, place, g_send.at[kind, m, s], g_recv.at[kind, m, s], x_dev)
        place = W.at[m, s, kd if receive else kx, c, pl.ds(HALF, HALF)]
        return remote(place, place, g_send.at[kind, m, s], g_recv.at[kind, m, s], y_dev)

    def place_of(i):
        if i < 3:
            return i, 0
        if i < 6:
            return 0, i - 2
        return 1 + (i - 6) % 2, (i - 6) // 2 + 1

    def gather_a(i):
        if i > 11:
            return
        m, t = place_of(i)
        s = s_of(t)
        if t > 0:
            z_copy(m, s, 0).wait_recv()
            z_pass(m, s)
        plane_copy(XOWN, m, s).start()
        plane_copy(YOWN, m, s).start()

    def gather_b(i):
        if i > 11:
            return
        m, t = place_of(i)
        s = s_of(t)
        plane_copy(YOWN, m, s, True).wait_recv()
        plane_copy(XFWD, m, s).start()
        plane_copy(XOWN, m, s, True).wait_recv()
        plane_copy(YFWD, m, s).start()

    def gather_c(i):
        m, t = place_of(i)
        s = s_of(t)
        plane_copy(XFWD, m, s, True).wait_recv()
        plane_copy(YFWD, m, s, True).wait_recv()
        plane_copy(CORE, m, s).start()

    def gather_d(m, t):
        plane_copy(CORE, m, s_of(t), True).wait_recv()

    def pump(i):
        if i > 11:
            return
        gather_a(i + 3)
        gather_b(i + 1)
        gather_c(i)

    def row_copy(which, source, target, there):
        return remote(source.at[there], target.at[z], in_send.at[which, there], in_recv.at[which, z], z_dev(there))

    def rows_send(which, source, target):
        for there in range(NS):

            @pl.when(there != z)
            def _():
                row_copy(which, source, target, there).start()

        pltpu.make_async_copy(source.at[z], target.at[z], local_sem.at[which]).start()

    def rows_wait(which, source, target):
        for origin in range(NS):

            @pl.when(origin != z)
            def _():
                remote(
                    source.at[origin], target.at[origin], in_send.at[which, origin], in_recv.at[which, origin], z_dev(origin)
                ).wait_recv()

        pltpu.make_async_copy(source.at[z], target.at[z], local_sem.at[which]).wait()

    z_pass(0, z)
    rows_send(0, features, X)
    for i in range(3):
        gather_a(i)
    z_pass(1, z)
    z_pass(2, z)
    rows_send(1, cotangent, U)

    order = packing[pl.ds(z, 1), :]
    labels = segments[pl.ds(z, 1), :].astype(F32)
    token = lax.broadcasted_iota(jnp.int32, (TOK, TOK), 0)
    token_labels = jnp.sum(jnp.where(token == order, labels, 0.0), axis=1, keepdims=True)
    kinds = lax.broadcasted_iota(jnp.int32, (TOK, 128), 1).astype(F32)
    one_hot = jnp.where(token_labels == kinds, 1.0, 0.0).astype(BF16)
    MASK[...] = dot(one_hot, one_hot, NT_DIMS)
    SG[...] = jnp.zeros_like(SG)
    PB[...] = jnp.zeros_like(PB)
    for s in range(NS):
        PB[s : s + 1, 0:SEC] = project_bias[0:1, s * SEC : (s + 1) * SEC]
        PB[s : s + 1, 2 * SEC : 3 * SEC] = project_bias[1:2, s * SEC : (s + 1) * SEC]

    gather_b(0)
    pump(0)
    pump(1)
    pump(2)

    rows_wait(0, features, X)
    for i in range(NS):
        normal, _ = norm_stats(X[i].astype(F32))
        normed = normal * gain1[...] + shift1[...]
        N1[i * CHUNK : (i + 1) * CHUNK, :] = normed.astype(BF16)
        N1T[:, i * CHUNK : (i + 1) * CHUNK] = normed.T.astype(BF16)

    def weight(m, s):
        return W[m, s].reshape(D, D)

    def weight_tile(m, s, n):
        return W[m, s, :, :, :, pl.ds(pl.multiple_of(n * 256, 256), 256)].reshape(D, 256)

    def last_quarter(value):
        lane = lax.broadcasted_iota(jnp.int32, value.shape, 1)
        return jnp.where(lane >= 64, value, jnp.zeros_like(value))

    def attend(s):
        def project_tile(n, carry):
            lanes = pl.ds(pl.multiple_of(n * 256, 256), 256)
            QA[s, :, lanes] = (dot(N1[...], weight_tile(0, s, n)) + PB[pl.ds(s, 1), lanes]).astype(BF16)
            return carry

        lax.fori_loop(0, 3, project_tile, 0)
        for j in range(3):
            keys = QA[s, :, SEC + 64 * j : SEC + 64 * j + 64]
            values = QA[s, :, 2 * SEC + 64 * j : 2 * SEC + 64 * j + 64]
            for tile in range(2):
                rows = slice(tile * 256, tile * 256 + 256)
                queries = QA[s, rows, 64 * j : 64 * j + 64] * 0.125
                scores = dot(keys, queries, NT_DIMS)
                scores = jnp.where(MASK[:, rows] > 0.5, scores, MASKED)
                peak = jnp.max(scores, axis=0, keepdims=True)
                weights = jnp.exp(scores - peak)
                total = jnp.sum(weights, axis=0, keepdims=True)
                probs = (weights * (1.0 / total)).astype(BF16)
                LSE[pl.ds(s * 3 + j, 1), rows] = peak + jnp.log(total)
                mixed = dot(values, probs, TN_DIMS)
                QA[s, rows, 3 * SEC + 64 * j : 3 * SEC + 64 * j + 64] = mixed.T.astype(BF16)
        mixed = last_quarter(QA[s, :, 512:768])
        return dot(mixed, W[0, s, :, :, :, 512:768].reshape(D, 256), NT_DIMS)

    gather_d(0, 0)
    pump(3)
    ACC1[...] = attend(s_of(0))
    for t in range(1, 4):
        gather_d(0, t)
        pump(3 + t)
        ACC1[...] += attend(s_of(t))

    for i in range(NS):
        rows = slice(i * CHUNK, (i + 1) * CHUNK)
        middle = X[i].astype(F32) + (ACC1[rows, :] + merge_bias[...])
        MID[rows, :] = middle
        normal, _ = norm_stats(middle)
        normed = normal * gain2[...] + shift2[...]
        N2[i] = normed.astype(BF16)
        N2T[:, rows] = normed.T.astype(BF16)
    pump(7)
    rows_wait(1, cotangent, U)
    for i in range(NS):
        upstream = U[i].astype(F32)
        UT[:, i * CHUNK : (i + 1) * CHUNK] = upstream.T.astype(BF16)
        SG[5:6, :] += column_sum(upstream)
    ACC1[...] = jnp.zeros_like(ACC1)
    ACC2[...] = jnp.zeros_like(ACC2)
    pump(8)

    def slot(m):
        return 2 - m if m > 0 else 0

    def rs_core(m, s, receive=False):
        if receive:
            place = RC.at[slot(m), s]
            return remote(place, place, r_send.at[CORE, m, s], r_recv.at[CORE, m, s], c_dev)
        return remote(G.at[m, s, :, 1 - c], RC.at[slot(m), s], r_send.at[CORE, m, s], r_recv.at[CORE, m, s], c_dev)

    def rs_diag(kind, m, s):
        which, device = (0, x_dev) if kind == XFWD else (1, y_dev)
        return remote(
            G.at[m, s, kd, c, pl.ds(which * HALF, HALF)], RD.at[slot(m), s, which],
            r_send.at[kind, m, s], r_recv.at[kind, m, s], device,
        )

    def rs_side(kind, m, s):
        which, device, block = (0, x_dev, kx) if kind == XOWN else (1, y_dev, ky)
        return remote(
            G.at[m, s, block, c], RE.at[slot(m), s, which], r_send.at[kind, m, s], r_recv.at[kind, m, s], device
        )

    def rs_z(m, s):
        return remote(G.at[m, s, k, c], RZ.at[m, z], rz_send.at[m, s], rz_recv.at[m, z], z_dev(s))

    def add_into(place, other):
        place[...] = (place[...].astype(F32) + other[...].astype(F32)).astype(BF16)

    def scatter_p(m, s):
        rs_core(m, s).start()

    def scatter_place(r):
        if r < 8:
            return 2 - r % 2, r // 2
        return 0, r - 8

    def scatter_q(r):
        if not 0 <= r <= 11:
            return
        m, t = scatter_place(r)
        s = s_of(t)
        rs_core(m, s, True).wait_recv()
        for block in range(4):
            add_into(G.at[m, s, block, c], RC.at[slot(m), s, block])
        rs_diag(XFWD, m, s).start()
        rs_diag(YFWD, m, s).start()

    def scatter_r(r):
        if not 0 <= r <= 11:
            return
        m, t = scatter_place(r)
        s = s_of(t)
        rs_diag(XFWD, m, s).wait_recv()
        add_into(G.at[m, s, ky, c, pl.ds(0, HALF)], RD.at[slot(m), s, 0])
        rs_side(YOWN, m, s).start()
        rs_diag(YFWD, m, s).wait_recv()
        add_into(G.at[m, s, kx, c, pl.ds(HALF, HALF)], RD.at[slot(m), s, 1])
        rs_side(XOWN, m, s).start()

    def scatter_t(r):
        if not 0 <= r <= 11:
            return
        m, t = scatter_place(r)
        s = s_of(t)
        rs_side(XOWN, m, s).wait_recv()
        rs_side(YOWN, m, s).wait_recv()
        total = G[m, s, k, c].astype(F32) + (RE[slot(m), s, 0].astype(F32) + RE[slot(m), s, 1].astype(F32))
        G[m, pl.ds(s, 1), pl.ds(k, 1), pl.ds(c, 1)] = total.astype(BF16)[None, None, None]
        if t > 0:
            rs_z(m, s).start()

    def scatter_pump(r):
        scatter_q(r)
        scatter_r(r - 1)
        scatter_t(r - 2)

    def scatter_sum(m):
        total = G[m, z, k, c].astype(F32)
        for step in range(1, NS):
            origin = (z + step) % NS
            remote(RZ.at[m, origin], RZ.at[m, origin], rz_send.at[m, origin], rz_recv.at[m, origin], z_dev(origin)).wait_recv()
            total = total + RZ[m, origin].astype(F32)
        return total

    def feed(s):
        def tile_step(n, carry):
            lanes = pl.ds(pl.multiple_of(n * 256, 256), 256)
            hidden = dot(N2[...].reshape(TOK, D), weight_tile(1, s, n)) + expand_bias[pl.ds(s, 1), lanes]
            gate = 0.5 + 0.5 * lax.erf(hidden * 0.7071067811865476)
            active = (hidden * gate).astype(BF16)
            AC[:, lanes] = active
            slope = gate + hidden * (jnp.exp(-0.5 * hidden * hidden) * 0.3989422804014327)
            G[2, s, :, :, :, lanes] = dot(UT[...], active).astype(BF16).reshape(4, 2, ROWS, 256)
            grad_active = dot(U[...].reshape(TOK, D), weight_tile(2, s, n))
            grad_hidden = (grad_active * slope).astype(BF16)
            GH[:, lanes] = grad_hidden
            SG[pl.ds(6 + s, 1), lanes] = column_sum(grad_hidden.astype(F32))
            G[1, s, :, :, :, lanes] = dot(N2T[...], grad_hidden).astype(BF16).reshape(4, 2, ROWS, 256)
            return carry

        lax.fori_loop(0, 3, tile_step, 0)
        ACC1[...] += dot(AC[...], weight(2, s), NT_DIMS)
        ACC2[...] += dot(GH[...], weight(1, s), NT_DIMS)

    for t in range(4):
        s = s_of(t)
        gather_d(1, t)
        gather_d(2, t)
        pump(9 + t)
        feed(s)
        scatter_p(2, s)
        scatter_p(1, s)
        if t > 0:
            scatter_pump(2 * t - 2)
            scatter_pump(2 * t - 1)

    def wide_copy(i):
        return pltpu.make_async_copy(ACC2.at[pl.ds(i * CHUNK, CHUNK)], features_grad.at[i], fw_sem.at[i])

    def back_copy(which, source, target, there, origin):
        return remote(source.at[there], target.at[origin], out_send.at[which, there], out_recv.at[which, origin], z_dev(there))

    def rows_back(which, source, target):
        for there in range(NS):

            @pl.when(there != z)
            def _():
                back_copy(which, source, target, there, z).start()

        pltpu.make_async_copy(source.at[z], target.at[z], local_sem.at[2 + which]).start()

    def back_wait(which, source, target):
        for other in range(NS):

            @pl.when(other != z)
            def _():
                back_copy(which, source, target, other, other).wait()

        pltpu.make_async_copy(source.at[z], target.at[z], local_sem.at[2 + which]).wait()

    for i in range(NS):
        rows = slice(i * CHUNK, (i + 1) * CHUNK)
        middle = MID[rows, :]
        FS[i] = (middle + (ACC1[rows, :] + reduce_bias[...])).astype(BF16)
    rows_back(0, FS, out)

    for i in range(NS):
        rows = slice(i * CHUNK, (i + 1) * CHUNK)
        normal, scale = norm_stats(MID[rows, :])
        grad = ACC2[rows, :]
        grad_middle = U[i].astype(F32) + norm_grad(normal, scale, grad, gain2[...])
        SG[2:3, :] += column_sum(grad * normal)
        SG[3:4, :] += column_sum(grad)
        grad_branch = grad_middle.astype(BF16)
        SG[4:5, :] += column_sum(grad_branch.astype(F32))
        MID[rows, :] = grad_middle
        AC[rows, :] = grad_branch
        UT[:, rows] = grad_branch.astype(F32).T.astype(BF16)
    ACC2[...] = jnp.zeros_like(ACC2)
    scatter_pump(6)
    scatter_pump(7)

    def attend_back(s):
        GA[...] = dot(AC[...], W[0, s, :, :, :, 512:768].reshape(D, 256)).astype(BF16)
        GH[:, 512:768] = jnp.zeros((TOK, 256), BF16)
        for j in range(3):
            keys = QA[s, :, SEC + 64 * j : SEC + 64 * j + 64]
            values = QA[s, :, 2 * SEC + 64 * j : 2 * SEC + 64 * j + 64]
            grad_keys = jnp.zeros((TOK, HEAD_DIM), F32)
            grad_values = jnp.zeros((TOK, HEAD_DIM), F32)
            for tile in range(2):
                rows = slice(tile * 256, tile * 256 + 256)
                queries = QA[s, rows, 64 * j : 64 * j + 64] * 0.125
                grad_mixed = GA[rows, 64 + 64 * j : 128 + 64 * j]
                scores = dot(keys, queries, NT_DIMS)
                scores = jnp.where(MASK[:, rows] > 0.5, scores, MASKED)
                probs = jnp.exp(scores - LSE[pl.ds(s * 3 + j, 1), rows])
                grad_probs = dot(values, grad_mixed, NT_DIMS)
                inner = jnp.sum(probs * grad_probs, axis=0, keepdims=True)
                grad_scores = (probs * (grad_probs - inner)).astype(BF16)
                grad_queries = dot(keys, grad_scores, TN_DIMS) * 0.125
                GH[rows, 64 * j : 64 * j + 64] = grad_queries.T.astype(BF16)
                grad_keys += dot(grad_scores, queries)
                grad_values += dot(probs.astype(BF16), grad_mixed)
            GH[:, SEC + 64 * j : SEC + 64 * j + 64] = grad_keys.astype(BF16)
            GH[:, 2 * SEC + 64 * j : 2 * SEC + 64 * j + 64] = grad_values.astype(BF16)
        SG[pl.ds(10 + s, 1), :] = column_sum(GH[...].astype(F32))
        for n in range(3):
            lanes = slice(n * 256, n * 256 + 256)
            part = dot(N1T[...], GH[:, lanes])
            if n == 2:
                part += dot(UT[...], last_quarter(QA[s, :, 512:768]))
            G[0, s, :, :, :, lanes] = part.astype(BF16).reshape(4, 2, ROWS, 256)
        ACC2[...] += dot(GH[...], weight(0, s), NT_DIMS)

    for t in range(4):
        s = s_of(t)
        attend_back(s)
        if t == 0:
            scatter_r(7)
            scatter_t(6)
            scatter_t(7)
            for device, which in ((c_dev, 0), (x_dev, 1), (y_dev, 2)):
                pl.semaphore_signal(credit.at[which], inc=1, device_id=device, device_id_type=MESH_ID)
            for which in range(3):
                pl.semaphore_wait(credit.at[which], 1)
        scatter_p(0, s)
        if t > 0:
            scatter_q(7 + t)
        if t > 1:
            scatter_r(6 + t)
        if t > 2:
            scatter_t(5 + t)

    for i in range(NS):
        rows = slice(i * CHUNK, (i + 1) * CHUNK)
        normal, scale = norm_stats(X[i].astype(F32))
        grad = ACC2[rows, :]
        SG[0:1, :] += column_sum(grad * normal)
        SG[1:2, :] += column_sum(grad)
        N2[i] = (MID[rows, :] + norm_grad(normal, scale, grad, gain1[...])).astype(BF16)
    rows_back(1, N2, FR)

    def sum_step(step, device):
        copy = remote(SG, SGR.at[step], sg_send.at[step], sg_recv.at[step], device)
        copy.start()
        return copy

    def sum_end(step, copy):
        copy.wait()
        SG[...] = SG[...] + SGR[step]

    copy = sum_step(0, c_dev)
    scatter_q(11)
    scatter_r(10)
    sum_end(0, copy)
    copy = sum_step(1, x_dev)
    scatter_t(9)
    scatter_r(11)
    sum_end(1, copy)
    copy = sum_step(2, y_dev)
    scatter_t(10)
    sum_end(2, copy)
    copy = sum_step(3, z_dev(z + 1 - 2 * (z % 2)))
    expand_grad[...] = scatter_sum(1)
    reduce_grad[...] = scatter_sum(2)
    sum_end(3, copy)
    copy = sum_step(4, z_dev((z + 2) % NS))
    scatter_t(11)
    sum_end(4, copy)

    gain1_grad[...] = SG[0:1, :]
    shift1_grad[...] = SG[1:2, :]
    gain2_grad[...] = SG[2:3, :]
    shift2_grad[...] = SG[3:4, :]
    merge_bias_grad[...] = SG[4:5, :]
    reduce_bias_grad[...] = SG[5:6, :]
    expand_bias_grad[...] = SG[6:10, :]
    for s in range(NS):
        project_bias_grad[0:1, s * SEC : (s + 1) * SEC] = SG[10 + s : 11 + s, 0:SEC]
        project_bias_grad[1:2, s * SEC : (s + 1) * SEC] = SG[10 + s : 11 + s, 2 * SEC : 3 * SEC]

    back_wait(1, N2, FR)
    for i in range(NS):
        ACC2[i * CHUNK : (i + 1) * CHUNK, :] = FR[i].astype(F32)
        wide_copy(i).start()
    TB[...] = scatter_sum(0)
    for piece in range(3):
        project_grad[piece] = TB[:, piece * SEC : (piece + 1) * SEC]
    merge_grad[...] = TB[:, 3 * SEC :].T
    back_wait(0, FS, out)
    for i in range(NS):
        wide_copy(i).wait()

    for m in range(3):
        for t in range(NS):
            s = s_of(t)

            @pl.when((s <= z) & (z < NS - 1))
            def _():
                z_copy(m, s, 1).wait_send()

            @pl.when((s >= z) & (z > 0))
            def _():
                z_copy(m, s, 0).wait_send()

            for kind in range(5):
                plane_copy(kind, m, s).wait_send()
            rs_core(m, s).wait_send()
            rs_diag(XFWD, m, s).wait_send()
            rs_diag(YFWD, m, s).wait_send()
            rs_side(XOWN, m, s).wait_send()
            rs_side(YOWN, m, s).wait_send()
            if t > 0:
                rs_z(m, s).wait_send()
    for which, source, target in ((0, features, X), (1, cotangent, U)):
        for there in range(NS):

            @pl.when(there != z)
            def _():
                row_copy(which, source, target, there).wait_send()


def block(features, packing, segment_ids, norm1_gain, norm1_shift, project_weight, project_bias, merge_weight, merge_bias,
          norm2_gain, norm2_shift, expand_weight, expand_bias, reduce_weight, reduce_bias, cotangent):
    def row(values):
        return values.reshape(1, -1)

    vmem = pl.BlockSpec(memory_space=pltpu.VMEM)
    anywhere = pl.BlockSpec(memory_space=pl.ANY)
    shape = jax.ShapeDtypeStruct
    wide = 4 * D
    results = pl.pallas_call(
        block_kernel,
        name="block",
        in_specs=[anywhere] + [vmem] * 14 + [anywhere],
        out_specs=[anywhere, anywhere] + [vmem] * 12,
        out_shape=[
            shape((NS, CHUNK, D), BF16),
            shape((NS, CHUNK, D), F32),
            shape((1, D), F32),
            shape((1, D), F32),
            shape((3, ROWS, SEC), F32),
            shape((2, D), F32),
            shape((SEC, ROWS), F32),
            shape((1, D), F32),
            shape((1, D), F32),
            shape((1, D), F32),
            shape((ROWS, D), F32),
            shape((4, D), F32),
            shape((ROWS, D), F32),
            shape((1, D), F32),
        ],
        scratch_shapes=[
            pltpu.VMEM((3, NS, 4, 2, ROWS, D), BF16),
            pltpu.VMEM((3, NS, 4, 2, ROWS, D), BF16),
            pltpu.VMEM((2, NS, 4, ROWS, D), BF16),
            pltpu.VMEM((2, NS, 2, HALF, D), BF16),
            pltpu.VMEM((2, NS, 2, ROWS, D), BF16),
            pltpu.VMEM((3, NS, ROWS, D), BF16),
            pltpu.VMEM((NS, CHUNK, D), BF16),
            pltpu.VMEM((NS, CHUNK, D), BF16),
            pltpu.VMEM((D, TOK), BF16),
            pltpu.VMEM((TOK, D), BF16),
            pltpu.VMEM((D, TOK), BF16),
            pltpu.VMEM((NS, CHUNK, D), BF16),
            pltpu.VMEM((D, TOK), BF16),
            pltpu.VMEM((NS, TOK, D), BF16),
            pltpu.VMEM((TOK, D), F32),
            pltpu.VMEM((TOK, D), F32),
            pltpu.VMEM((TOK, D), F32),
            pltpu.VMEM((TOK, D), BF16),
            pltpu.VMEM((TOK, D), BF16),
            pltpu.VMEM((TOK, 256), BF16),
            pltpu.VMEM((TOK, TOK), F32),
            pltpu.VMEM((16, TOK), F32),
            pltpu.VMEM((8, D), F32),
            pltpu.VMEM((16, D), F32),
            pltpu.VMEM((5, 16, D), F32),
            pltpu.VMEM((NS, CHUNK, D), BF16),
            pltpu.VMEM((NS, CHUNK, D), BF16),
            pltpu.VMEM((ROWS, D), F32),
            pltpu.SemaphoreType.DMA((2, 3, NS)),
            pltpu.SemaphoreType.DMA((3, NS)),
            pltpu.SemaphoreType.DMA((5, 3, NS)),
            pltpu.SemaphoreType.DMA((5, 3, NS)),
            pltpu.SemaphoreType.DMA((5, 3, NS)),
            pltpu.SemaphoreType.DMA((5, 3, NS)),
            pltpu.SemaphoreType.DMA((3, NS)),
            pltpu.SemaphoreType.DMA((3, NS)),
            pltpu.SemaphoreType.DMA((2, NS)),
            pltpu.SemaphoreType.DMA((2, NS)),
            pltpu.SemaphoreType.DMA((2, NS)),
            pltpu.SemaphoreType.DMA((2, NS)),
            pltpu.SemaphoreType.DMA((5,)),
            pltpu.SemaphoreType.DMA((5,)),
            pltpu.SemaphoreType.DMA((4,)),
            pltpu.SemaphoreType.REGULAR((3,)),
            pltpu.SemaphoreType.DMA((NS,)),
        ],
        compiler_params=pltpu.CompilerParams(collective_id=0, has_side_effects=True, vmem_limit_bytes=65 * 1000 * 1000),
    )(
        features,
        packing.reshape(NS, TOK),
        segment_ids.reshape(NS, TOK),
        row(norm1_gain),
        row(norm1_shift),
        project_weight,
        project_bias,
        merge_weight,
        row(merge_bias),
        row(norm2_gain),
        row(norm2_shift),
        expand_weight,
        expand_bias.reshape(4, D),
        reduce_weight.T,
        row(reduce_bias),
        cotangent,
    )
    (out, features_grad, g1, s1, pw, pb, mw, mb, g2, s2, ew, eb, rw, rb) = results
    flat = lambda values: values.reshape(-1)
    return (out, features_grad, flat(g1), flat(s1), pw, pb, mw, flat(mb), flat(g2), flat(s2), ew, flat(eb), rw.T, flat(rb))


def norm_rows(values, gain, shift):
    center = values - jnp.mean(values, axis=-1, keepdims=True)
    spread = jnp.mean(center * center, axis=-1, keepdims=True)
    return center * lax.rsqrt(spread + EPSILON) * gain + shift


def exact_gelu(values):
    return jax.nn.gelu(values, approximate=False)


def swap_rows(values):
    return lax.all_to_all(values, "section", split_axis=0, concat_axis=1, tiled=True)[0]


def swap_back(values):
    return lax.all_to_all(values[None], "section", split_axis=1, concat_axis=0, tiled=True)


def whole(values, dp_axis, section_axis):
    values = lax.all_gather(values, "dp", axis=dp_axis, tiled=True)
    return lax.all_gather(values, "section", axis=section_axis, tiled=True)


def shard(values, dp_axis, section_axis):
    values = lax.psum_scatter(values, "section", scatter_dimension=section_axis, tiled=True)
    return lax.psum_scatter(values, "dp", scatter_dimension=dp_axis, tiled=True)


def body(
    features,
    packing,
    segment_ids,
    norm1_gain,
    norm1_shift,
    project_weight,
    project_bias,
    merge_weight,
    merge_bias,
    norm2_gain,
    norm2_shift,
    expand_weight,
    expand_bias,
    reduce_weight,
    reduce_bias,
    cotangent,
):
    length = packing.shape[2]
    width = features.shape[2]
    heads = width // HEAD_DIM
    scale = HEAD_DIM ** (-0.5)
    mine = lax.axis_index("section")
    order = lax.dynamic_index_in_dim(packing[:, 0], mine, 0, keepdims=False)
    packed_labels = lax.dynamic_index_in_dim(segment_ids[:, 0], mine, 0, keepdims=False)
    labels = jnp.zeros((length,), jnp.int32).at[order].set(packed_labels)
    allowed = labels[:, None] == labels[None, :]

    tokens = swap_rows(features).astype(F32)
    upstream = swap_rows(cotangent)
    project = whole(project_weight, 1, 2)
    merge = whole(merge_weight, 1, 0)
    expand = whole(expand_weight, 0, 1)
    reduce = whole(reduce_weight, 1, 0)

    normed = norm_rows(tokens, norm1_gain, norm1_shift).astype(BF16)
    projected = jnp.einsum("td,cde->cte", normed, project, preferred_element_type=F32)
    queries = (projected[0] + project_bias[0]).astype(BF16).reshape(length, heads, HEAD_DIM)
    keys = projected[1].astype(BF16).reshape(length, heads, HEAD_DIM)
    values = (projected[2] + project_bias[1]).astype(BF16).reshape(length, heads, HEAD_DIM)
    scores = jnp.einsum("qhd,khd->hqk", queries, keys, preferred_element_type=F32) * scale
    scores = jnp.where(allowed[None], scores, MASKED)
    peak = jnp.max(scores, axis=-1, keepdims=True)
    weights = jnp.exp(scores - peak)
    probs = weights / jnp.sum(weights, axis=-1, keepdims=True)
    low_probs = probs.astype(BF16)
    mixed = jnp.einsum("hqk,khd->qhd", low_probs, values, preferred_element_type=F32)
    mixed = mixed.reshape(length, width).astype(BF16)
    middle = tokens + (jnp.dot(mixed, merge, preferred_element_type=F32) + merge_bias)
    normed_two = norm_rows(middle, norm2_gain, norm2_shift).astype(BF16)
    hidden = jnp.dot(normed_two, expand, preferred_element_type=F32) + expand_bias
    active = exact_gelu(hidden).astype(BF16)
    second = jnp.dot(active, reduce, preferred_element_type=F32)
    output = swap_back((middle + (second + reduce_bias)).astype(BF16))

    wide_upstream = upstream.astype(F32)
    reduce_bias_grad = jnp.sum(wide_upstream, axis=0)
    reduce_grad = jnp.einsum("tf,td->fd", active, upstream, preferred_element_type=F32)
    grad_active = jnp.einsum("td,fd->tf", upstream, reduce, preferred_element_type=F32)
    _, gelu_back = jax.vjp(exact_gelu, hidden)
    grad_hidden = gelu_back(grad_active)[0].astype(BF16)
    expand_bias_grad = jnp.sum(grad_hidden.astype(F32), axis=0)
    expand_grad = jnp.einsum("td,tf->df", normed_two, grad_hidden, preferred_element_type=F32)
    grad_normed_two = jnp.einsum("tf,df->td", grad_hidden, expand, preferred_element_type=F32)
    _, norm_back = jax.vjp(norm_rows, middle, norm2_gain, norm2_shift)
    grad_from_norm, gain_two, shift_two = norm_back(grad_normed_two)
    grad_middle = wide_upstream + grad_from_norm
    grad_branch = grad_middle.astype(BF16)
    merge_bias_grad = jnp.sum(grad_branch.astype(F32), axis=0)
    merge_grad = jnp.einsum("te,td->ed", mixed, grad_branch, preferred_element_type=F32)
    grad_mixed = jnp.einsum("td,ed->te", grad_branch, merge, preferred_element_type=F32)
    grad_mixed = grad_mixed.astype(BF16).reshape(length, heads, HEAD_DIM)
    grad_probs = jnp.einsum("qhd,khd->hqk", grad_mixed, values, preferred_element_type=F32)
    inner = jnp.sum(probs * grad_probs, axis=-1, keepdims=True)
    grad_scores = (probs * (grad_probs - inner)).astype(BF16)
    grad_queries = jnp.einsum("hqk,khd->qhd", grad_scores, keys, preferred_element_type=F32) * scale
    grad_keys = jnp.einsum("hqk,qhd->khd", grad_scores, queries, preferred_element_type=F32) * scale
    grad_values = jnp.einsum("hqk,qhd->khd", low_probs, grad_mixed, preferred_element_type=F32)
    stacked = jnp.stack([grad_queries, grad_keys, grad_values])
    stacked = stacked.reshape(3, length, width).astype(BF16)
    wide = stacked.astype(F32)
    project_bias_grad = jnp.stack([jnp.sum(wide[0], axis=0), jnp.sum(wide[2], axis=0)])
    project_grad = jnp.einsum("td,cte->cde", normed, stacked, preferred_element_type=F32)
    grad_normed = jnp.einsum("cte,cde->td", stacked, project, preferred_element_type=F32)
    _, first_back = jax.vjp(norm_rows, tokens, norm1_gain, norm1_shift)
    grad_tokens, gain_one, shift_one = first_back(grad_normed)
    features_grad = swap_back(grad_middle + grad_tokens)

    summed = lax.psum(
        (
            gain_one,
            shift_one,
            project_bias_grad,
            merge_bias_grad,
            gain_two,
            shift_two,
            expand_bias_grad,
            reduce_bias_grad,
        ),
        ("dp", "section"),
    )
    return (
        output,
        features_grad,
        summed[0],
        summed[1],
        shard(project_grad, 1, 2),
        summed[2],
        shard(merge_grad, 1, 0),
        summed[3],
        summed[4],
        summed[5],
        shard(expand_grad, 0, 1),
        summed[6],
        shard(reduce_grad, 1, 0),
        summed[7],
    )


def solution(mesh):
    rows = P(None, ("dp", "section"), None)
    groups = P(None, "dp", None)
    project = P(None, "dp", "section")
    inward = P("section", "dp")
    outward = P("dp", "section")
    in_specs = (rows, groups, groups, P(), P(), project, P(), inward, P(), P(), P(), outward, P(), inward, P(), rows)
    out_specs = (rows, rows, P(), P(), project, P(), inward, P(), P(), P(), outward, P(), inward, P())
    fits = mesh.shape["dp"] == 8 and mesh.shape["section"] == NS
    return jax.shard_map(block if fits else body, mesh=mesh, in_specs=in_specs, out_specs=out_specs, check_vma=False)
```

```python
import functools

import jax
import jax.numpy as jnp
from jax import lax
from jax.experimental import pallas as pl
from jax.experimental.pallas import tpu as pltpu
from jax.sharding import PartitionSpec as P

HEAD_DIM = 64
EPSILON = 1e-06
MASKED = -1000000000.0
F32 = jnp.float32
BF16 = jnp.bfloat16
MESH_ID = pl.DeviceIdType.MESH

NS = 4
D = 768
TOK = 512
ROWS = 96
HALF = 48
SEC = 192
NT_DIMS = (((1,), (1,)), ((), ()))
TN_DIMS = (((0,), (0,)), ((), ()))
CORE, XOWN, YOWN, XFWD, YFWD = range(5)
CHUNK = 128

PLAN_FEED_BEFORE = ("A10 C8 B9", "C9 B10", "C10 C11", "")
PLAN_FEED_BETWEEN = ("A11", "B11 Q0 Q1", "R0 R1 Q2 Q3", "R2 R3 Q4 Q5")
PLAN_OUT = "T0 Q6 Q7"
PLAN_NORM = "T1 R4 R5"
PLAN_BRANCH = "R6 R7 T2 Z0 Z1"
PLAN_BACK = (
    ("T3", "Q8 T4", "Q9 T6 Z4 Z5", "Q10 T7"),
    ("Z2 Z3", "T5 R8", "R9", "T8 R10 Z6 Z7"),
)


def norm_stats(values):
    center = values - jnp.mean(values, axis=-1, keepdims=True)
    spread = jnp.mean(center * center, axis=-1, keepdims=True)
    scale = lax.rsqrt(spread + EPSILON)
    return center * scale, scale


def norm_grad(normal, scale, grad, gain):
    scaled = grad * gain
    first = jnp.mean(scaled, axis=-1, keepdims=True)
    second = jnp.mean(scaled * normal, axis=-1, keepdims=True)
    return scale * (scaled - first - normal * second)


def dot(left, right, dims=(((1,), (0,)), ((), ()))):
    return lax.dot_general(left, right, dims, preferred_element_type=F32)


def row(values):
    return values[...].reshape(1, D)


def column_sum(values):
    return jnp.sum(values, axis=0, keepdims=True)


def block_kernel(
    features, packing, segments, gain1, shift1, project, project_bias, merge, merge_bias, gain2, shift2,
    expand, expand_bias, reduce, reduce_bias, cotangent,
    out, FR, weight_sums, SG,
    W, G, RC, RD, RE, RZ, RY, X, U, UT, N1, N1T, N2, N2T, QA, AT, MID, ACC1, ACC2, AC, GH, GA, MASK, LSE, PB, EB, SGR, FS, TB,
    z_send, z_recv, g_send, g_recv, r_send, r_recv, rz_send, rz_recv, ry_recv, in_send, in_recv, out_send, out_recv,
    sg_send, sg_recv, local_sem, credit,
):
    dp = lax.axis_index("dp")
    z = lax.axis_index("section")
    c = dp % 2
    k = dp // 2
    xi = k % 2
    yi = k // 2
    kx = 2 * yi + (1 - xi)
    ky = 2 * (1 - yi) + xi
    kd = 3 - k
    x_dev = {"dp": 2 * kx + c, "section": z}
    y_dev = {"dp": 2 * ky + c, "section": z}
    c_dev = {"dp": 2 * k + (1 - c), "section": z}

    def z_dev(other):
        return {"dp": dp, "section": other}

    half = z // 2
    start = (1 - half) * (z % 2) + half * (1 - z % 2)

    def s_of(t):
        base = (t // 2) * t + (1 - t // 2) * ((start + t) % 2)
        return half * 3 + (1 - 2 * half) * base

    def remote(src, dst, send, recv, device):
        return pltpu.make_async_remote_copy(
            src_ref=src, dst_ref=dst, send_sem=send, recv_sem=recv, device_id=device, device_id_type=MESH_ID
        )

    barrier = pltpu.get_barrier_semaphore()
    for device in (x_dev, y_dev, c_dev):
        pl.semaphore_signal(barrier, inc=1, device_id=device, device_id_type=MESH_ID)
    for step in range(1, NS):
        pl.semaphore_signal(barrier, inc=1, device_id=z_dev((z + step) % NS), device_id_type=MESH_ID)

    for piece in range(3):
        TB[:, piece * SEC : (piece + 1) * SEC] = project[piece].astype(F32)
    TB[:, 3 * SEC :] = merge[...].astype(F32).T
    W[0, pl.ds(z, 1), pl.ds(k, 1), pl.ds(c, 1)] = TB[...].astype(BF16)[None, None, None]
    W[1, pl.ds(z, 1), pl.ds(k, 1), pl.ds(c, 1)] = expand[...][None, None, None]
    W[2, pl.ds(z, 1), pl.ds(k, 1), pl.ds(c, 1)] = reduce[...][None, None, None]
    pl.semaphore_wait(barrier, 6)

    def z_copy(m, s, up):
        place = W.at[m, s, k, c]
        return remote(place, place, z_send.at[up, m, s], z_recv.at[m, s], z_dev(z + 2 * up - 1))

    def z_pass(m, s):
        @pl.when((s <= z) & (z < NS - 1))
        def _():
            z_copy(m, s, 1).start()

        @pl.when((s >= z) & (z > 0))
        def _():
            z_copy(m, s, 0).start()

    def plane_copy(kind, m, s, receive=False):
        rows = slice(None)
        if kind == CORE:
            place = W.at[m, s, :, (1 - c) if receive else c]
            return remote(place, place, g_send.at[kind, m, s], g_recv.at[kind, m, s], c_dev)
        if kind == XOWN:
            place = W.at[m, s, kx if receive else k, c]
            return remote(place, place, g_send.at[kind, m, s], g_recv.at[kind, m, s], x_dev)
        if kind == YOWN:
            place = W.at[m, s, ky if receive else k, c]
            return remote(place, place, g_send.at[kind, m, s], g_recv.at[kind, m, s], y_dev)
        if kind == XFWD:
            place = W.at[m, s, kd if receive else ky, c, pl.ds(0, HALF)]
            return remote(place, place, g_send.at[kind, m, s], g_recv.at[kind, m, s], x_dev)
        place = W.at[m, s, kd if receive else kx, c, pl.ds(HALF, HALF)]
        return remote(place, place, g_send.at[kind, m, s], g_recv.at[kind, m, s], y_dev)

    def guard(condition, action):
        if isinstance(condition, bool):
            if condition:
                action()
        else:
            pl.when(condition)(action)

    def place_of(i):
        if isinstance(i, int) and i < 3:
            return i, 0
        late = i // 6
        return late * (1 + i % 2), late * (i // 2 - 2) + (1 - late) * (i - 2)

    def gather_a(i):
        def action():
            m, t = place_of(i)
            s = s_of(t)
            if not isinstance(i, int) or i > 2:
                z_copy(m, s, 0).wait_recv()
                z_pass(m, s)
            plane_copy(XOWN, m, s).start()
            plane_copy(YOWN, m, s).start()

        guard(i <= 11, action)

    def gather_b(i):
        def action():
            m, t = place_of(i)
            s = s_of(t)
            plane_copy(YOWN, m, s, True).wait_recv()
            plane_copy(XFWD, m, s).start()
            plane_copy(XOWN, m, s, True).wait_recv()
            plane_copy(YFWD, m, s).start()

        guard(i <= 11, action)

    def gather_c(i):
        def action():
            m, t = place_of(i)
            s = s_of(t)
            plane_copy(XFWD, m, s, True).wait_recv()
            plane_copy(YFWD, m, s, True).wait_recv()
            plane_copy(CORE, m, s).start()

        guard(i <= 11, action)

    def gather_d(m, t):
        plane_copy(CORE, m, s_of(t), True).wait_recv()

    def pump(i):
        gather_a(i + 3)
        gather_b(i + 1)
        gather_c(i)

    def row_copy(which, source, target, there):
        return remote(source.at[there], target.at[z], in_send.at[which, there], in_recv.at[which, z], z_dev(there))

    def rows_send(which, source, target):
        for there in range(NS):

            @pl.when(there != z)
            def _():
                row_copy(which, source, target, there).start()

        pltpu.make_async_copy(source.at[z], target.at[z], local_sem.at[which]).start()

    def rows_wait(which, source, target, step):
        origin = (z + step) % NS
        if step == 0:
            pltpu.make_async_copy(source.at[z], target.at[z], local_sem.at[which]).wait()
        else:
            remote(
                source.at[origin], target.at[origin], in_send.at[which, origin], in_recv.at[which, origin], z_dev(origin)
            ).wait_recv()
        return origin

    z_pass(0, z)
    rows_send(0, features, X)
    for i in range(3):
        gather_a(i)

    order = packing[z]
    labels = segments[z].astype(F32)
    token = lax.broadcasted_iota(jnp.int32, (TOK, TOK), 0)
    token_labels = jnp.sum(jnp.where(token == order, labels, 0.0), axis=1, keepdims=True)
    kinds = lax.broadcasted_iota(jnp.int32, (TOK, 128), 1).astype(F32)
    one_hot = jnp.where(token_labels == kinds, 1.0, 0.0).astype(BF16)
    MASK[...] = (dot(one_hot, one_hot, NT_DIMS) - 1.0) * -MASKED
    AT[:, :, 0:64] = jnp.zeros((NS, TOK, 64), BF16)
    SG[...] = jnp.zeros_like(SG)
    PB[...] = jnp.zeros_like(PB)
    for s in range(NS):
        EB[s] = expand_bias[s * D : (s + 1) * D].reshape(1, D)
        PB[s, :, 0:SEC] = project_bias[0:1, s * SEC : (s + 1) * SEC]
        PB[s, :, 2 * SEC : 3 * SEC] = project_bias[1:2, s * SEC : (s + 1) * SEC]

    gather_b(0)
    gather_b(1)
    gather_c(0)
    gather_a(3)
    gather_b(2)
    gather_c(1)
    gather_a(4)
    gather_c(2)
    gather_b(3)

    for step in (0, 1, 3, 2):
        i = rows_wait(0, features, X, step)
        rows = pl.ds(pl.multiple_of(i * CHUNK, CHUNK), CHUNK)
        normal, _ = norm_stats(X[i].astype(F32))
        normed = normal * row(gain1) + row(shift1)
        N1[rows, :] = normed.astype(BF16)
        N1T[:, rows] = normed.T.astype(BF16)

    def weight(m, s):
        return W[m, s].reshape(D, D)

    def weight_tile(m, s, n):
        return W[m, s, :, :, :, pl.ds(pl.multiple_of(n * 256, 256), 256)].reshape(D, 256)

    def weight_end(s):
        return W[0, s, :, :, :, 512:768].reshape(D, 256)

    def attend(s, between):
        for first, last in ((0, 256), (256, 512), (512, 640)):
            part = dot(N1[...], W[0, s, :, :, :, first:last].reshape(D, last - first))
            QA[s, :, first:last] = (part + PB[s, :, first:last]).astype(BF16)
        between()
        for j in range(3):
            keys = QA[s, :, SEC + 64 * j : SEC + 64 * j + 64]
            values = QA[s, :, 2 * SEC + 64 * j : 2 * SEC + 64 * j + 64]
            for tile in range(2):
                rows = slice(tile * 256, tile * 256 + 256)
                queries = QA[s, rows, 64 * j : 64 * j + 64] * 0.125
                scores = dot(keys, queries, NT_DIMS) + MASK[:, rows]
                peak = jnp.max(scores, axis=0, keepdims=True)
                weights = jnp.exp(scores - peak)
                total = jnp.sum(weights, axis=0, keepdims=True)
                LSE[s * 3 + j, :, rows] = peak + jnp.log(total)
                mixed = dot(values, weights.astype(BF16), TN_DIMS) * (1.0 / total)
                AT[s, rows, 64 + 64 * j : 128 + 64 * j] = mixed.T.astype(BF16)
        ACC1[...] += dot(AT[s], weight_end(s), NT_DIMS)

    ACC1[...] = jnp.zeros_like(ACC1)
    gather_a(5)
    z_pass(1, z)
    z_pass(2, z)

    def attend_step(t, carry):
        gather_d(0, t)

        def between():
            @pl.when(t == 0)
            def _():
                gather_c(3)
                gather_b(4)

            @pl.when(t == 1)
            def _():
                gather_c(4)
                gather_b(5)
                rows_send(1, cotangent, U)

            @pl.when(t == 2)
            def _():
                gather_c(5)
                gather_a(6)
                gather_a(7)

            @pl.when(t == 3)
            def _():
                gather_b(6)
                gather_b(7)
                gather_a(8)

        attend(s_of(t), between)
        return carry

    lax.fori_loop(0, NS, attend_step, 0)

    for i in range(NS):
        rows = slice(i * CHUNK, (i + 1) * CHUNK)
        middle = X[i].astype(F32) + (ACC1[rows, :] + row(merge_bias))
        MID[rows, :] = middle
        normal, _ = norm_stats(middle)
        normed = normal * row(gain2) + row(shift2)
        N2[i] = normed.astype(BF16)
        N2T[:, rows] = normed.T.astype(BF16)
    gather_c(6)
    gather_c(7)
    gather_a(9)
    gather_b(8)
    for step in (0, 1, 3, 2):
        i = rows_wait(1, cotangent, U, step)
        upstream = U[i].astype(F32)
        UT[:, pl.ds(pl.multiple_of(i * CHUNK, CHUNK), CHUNK)] = upstream.T.astype(BF16)
        SG[5:6, :] += column_sum(upstream)
    ACC1[...] = jnp.zeros_like(ACC1)
    ACC2[...] = jnp.zeros_like(ACC2)

    def rs_core(m, s, at, receive=False):
        place = RC.at[m % 2, at]
        source = place if receive else G.at[m, s, :, 1 - c]
        return remote(source, place, r_send.at[CORE, m, s], r_recv.at[CORE, m, s], c_dev)

    def rs_diag(kind, m, s, at):
        which, device = (0, x_dev) if kind == XFWD else (1, y_dev)
        return remote(
            G.at[m, s, kd, c, pl.ds(which * HALF, HALF)], RD.at[m % 2, at, which],
            r_send.at[kind, m, s], r_recv.at[kind, m, s], device,
        )

    def rs_side(kind, m, s, at):
        which, device, block = (0, x_dev, kx) if kind == XOWN else (1, y_dev, ky)
        return remote(
            G.at[m, s, block, c], RE.at[m % 2, at, which], r_send.at[kind, m, s], r_recv.at[kind, m, s], device
        )

    outer = 1 - ((z + 1) // 2) % 2
    pair = z + 1 - 2 * (z % 2)

    def rs_near(m, s):
        near = s // 2 == z // 2
        place = G.at[m, s, k, c]

        @pl.when(near)
        def _():
            remote(place, RZ.at[m, 0], rz_send.at[m, s], rz_recv.at[m, 0], z_dev(pair)).start()

        @pl.when(jnp.logical_not(near) & (outer == 1))
        def _():
            remote(place, RY.at[m, s % 2], rz_send.at[m, s], ry_recv.at[m, s % 2], z_dev(pair)).start()

    def rs_far(m, s):
        @pl.when((s // 2 != z // 2) & (outer == 0))
        def _():
            place = G.at[m, s, k, c]
            buffer = RY.at[m, s % 2]
            remote(buffer, buffer, rz_send.at[m, s], ry_recv.at[m, s % 2], z_dev(pair)).wait_recv()
            add_into(place, buffer)
            remote(place, RZ.at[m, 1], rz_send.at[m, s], rz_recv.at[m, 1], z_dev(s)).start()

    def add_into(place, other):
        place[...] = place[...] + other[...]

    def scatter_place(r):
        if r < 8:
            return 2 - r % 2, s_of(r // 2), s_of(r // 2)
        return 0, s_of(11 - r), s_of(r - 8)

    def credit_step(give):
        for device, which in ((c_dev, 0), (x_dev, 1), (y_dev, 2)):
            if give:
                pl.semaphore_signal(credit.at[which], inc=1, device_id=device, device_id_type=MESH_ID)
            else:
                pl.semaphore_wait(credit.at[which], 1)

    def scatter_p(m, s, at):
        rs_core(m, s, at).start()

    def scatter_q(r):
        m, s, at = scatter_place(r)
        rs_core(m, s, at, True).wait_recv()
        for block in range(4):
            add_into(G.at[m, s, block, c], RC.at[m % 2, at, block])
        rs_diag(XFWD, m, s, at).start()
        rs_diag(YFWD, m, s, at).start()

    def scatter_r(r):
        m, s, at = scatter_place(r)
        rs_diag(XFWD, m, s, at).wait_recv()
        add_into(G.at[m, s, ky, c, pl.ds(0, HALF)], RD.at[m % 2, at, 0])
        rs_side(YOWN, m, s, at).start()
        rs_diag(YFWD, m, s, at).wait_recv()
        add_into(G.at[m, s, kx, c, pl.ds(HALF, HALF)], RD.at[m % 2, at, 1])
        rs_side(XOWN, m, s, at).start()

    def scatter_t(r):
        m, s, at = scatter_place(r)
        rs_side(XOWN, m, s, at).wait_recv()
        rs_side(YOWN, m, s, at).wait_recv()
        place = G.at[m, s, k, c]
        total = RE[m % 2, at, 0].astype(F32) + RE[m % 2, at, 1].astype(F32)
        place[...] = (place[...].astype(F32) + total).astype(BF16)
        if r in (0, 2, 4, 6):
            credit_step(True)
        pl.when(s != z)(lambda: rs_near(m, s))

    def scatter_z(r):
        m, s, _ = scatter_place(r)
        rs_far(m, s)

    events = {"A": gather_a, "B": gather_b, "C": gather_c, "Q": scatter_q, "R": scatter_r, "T": scatter_t, "Z": scatter_z}

    def run(plan):
        for event in plan.split():
            events[event[0]](int(event[1:]))

    def run_at(t, plans):
        for i, plan in enumerate(plans):
            if plan:
                pl.when(t == i)(lambda plan=plan: run(plan))

    def scatter_sum(m):
        total = G[m, z, k, c].astype(F32)
        for which in range(2):
            remote(RZ.at[m, which], RZ.at[m, which], rz_send.at[m, z], rz_recv.at[m, which], z_dev(pair)).wait_recv()
            total = total + RZ[m, which].astype(F32)
        return total

    def feed(s, between):
        def tile_step(n, carry):
            lanes = pl.ds(pl.multiple_of(n * 256, 256), 256)
            hidden = dot(N2[...].reshape(TOK, D), weight_tile(1, s, n)) + EB[s, :, lanes]
            gate = 0.5 + 0.5 * lax.erf(hidden * 0.7071067811865476)
            active = (hidden * gate).astype(BF16)
            AC[:, lanes] = active
            slope = gate + hidden * (jnp.exp(-0.5 * hidden * hidden) * 0.3989422804014327)
            G[2, s, :, :, :, lanes] = dot(UT[...], active).astype(BF16).reshape(4, 2, ROWS, 256)
            grad_active = dot(U[...].reshape(TOK, D), weight_tile(2, s, n))
            grad_hidden = (grad_active * slope).astype(BF16)
            GH[:, lanes] = grad_hidden
            SG[pl.ds(6 + s, 1), lanes] = column_sum(grad_hidden.astype(F32))
            G[1, s, :, :, :, lanes] = dot(N2T[...], grad_hidden).astype(BF16).reshape(4, 2, ROWS, 256)
            return carry

        lax.fori_loop(0, 3, tile_step, 0, unroll=True)
        between()
        ACC1[...] += dot(AC[...], weight(2, s), NT_DIMS)
        ACC2[...] += dot(GH[...], weight(1, s), NT_DIMS)

    def feed_step(t, carry):
        s = s_of(t)

        def before():
            run_at(t, PLAN_FEED_BEFORE)

        def between():
            scatter_p(2, s, s)
            scatter_p(1, s, s)
            run_at(t, PLAN_FEED_BETWEEN)

        before()
        gather_d(1, t)
        gather_d(2, t)
        feed(s, between)
        return carry

    lax.fori_loop(0, NS, feed_step, 0)

    def back_send(which, source, target, there):
        @pl.when(there != z)
        def _():
            remote(
                source.at[there], target.at[z], out_send.at[which, there], out_recv.at[which, z], z_dev(there)
            ).start()

        @pl.when(there == z)
        def _():
            pltpu.make_async_copy(source.at[z], target.at[z], local_sem.at[2 + which]).start()

    def back_wait(which, source, target):
        for step in range(1, NS):
            other = (z + step) % NS
            remote(
                source.at[other], target.at[other], out_send.at[which, other], out_recv.at[which, other], z_dev(other)
            ).wait()
        pltpu.make_async_copy(source.at[z], target.at[z], local_sem.at[2 + which]).wait()

    run(PLAN_OUT)
    for i in range(NS):
        rows = slice(i * CHUNK, (i + 1) * CHUNK)
        FS[i] = (MID[rows, :] + (ACC1[rows, :] + row(reduce_bias))).astype(BF16)
        back_send(0, FS, out, i)
    run(PLAN_NORM)

    for i in range(NS):
        rows = slice(i * CHUNK, (i + 1) * CHUNK)
        normal, scale = norm_stats(MID[rows, :])
        grad = ACC2[rows, :]
        grad_middle = U[i].astype(F32) + norm_grad(normal, scale, grad, row(gain2))
        SG[2:3, :] += column_sum(grad * normal)
        SG[3:4, :] += column_sum(grad)
        grad_branch = grad_middle.astype(BF16)
        SG[4:5, :] += column_sum(grad_branch.astype(F32))
        MID[rows, :] = grad_middle
        AC[rows, :] = grad_branch
        UT[:, rows] = grad_branch.astype(F32).T.astype(BF16)
    ACC2[...] = jnp.zeros_like(ACC2)
    run(PLAN_BRANCH)

    def attend_back(s, between):
        between(0)
        GA[...] = dot(AC[...], weight_end(s)).astype(BF16)
        GH[:, 512:768] = jnp.zeros((TOK, 256), BF16)
        for j in range(3):
            keys = QA[s, :, SEC + 64 * j : SEC + 64 * j + 64]
            values = QA[s, :, 2 * SEC + 64 * j : 2 * SEC + 64 * j + 64]
            grad_keys = jnp.zeros((TOK, HEAD_DIM), F32)
            grad_values = jnp.zeros((TOK, HEAD_DIM), F32)
            for tile in range(2):
                rows = slice(tile * 256, tile * 256 + 256)
                queries = QA[s, rows, 64 * j : 64 * j + 64] * 0.125
                grad_mixed = GA[rows, 64 + 64 * j : 128 + 64 * j]
                scores = dot(keys, queries, NT_DIMS) + MASK[:, rows]
                probs = jnp.exp(scores - LSE[s * 3 + j, :, rows])
                grad_probs = dot(values, grad_mixed, NT_DIMS)
                inner = jnp.sum(probs * grad_probs, axis=0, keepdims=True)
                grad_scores = (probs * (grad_probs - inner)).astype(BF16)
                grad_queries = dot(keys, grad_scores, TN_DIMS) * 0.125
                GH[rows, 64 * j : 64 * j + 64] = grad_queries.T.astype(BF16)
                grad_keys += dot(grad_scores, queries)
                grad_values += dot(probs.astype(BF16), grad_mixed)
            GH[:, SEC + 64 * j : SEC + 64 * j + 64] = grad_keys.astype(BF16)
            GH[:, 2 * SEC + 64 * j : 2 * SEC + 64 * j + 64] = grad_values.astype(BF16)
        between(1)
        SG[pl.ds(10 + s, 1), :] = column_sum(GH[...].astype(F32))
        ACC2[...] += dot(GH[...], weight(0, s), NT_DIMS)

    def attend_weight(s):
        for n in range(3):
            lanes = slice(n * 256, n * 256 + 256)
            part = dot(N1T[...], GH[:, lanes])
            if n == 2:
                part += dot(UT[...], AT[s])
            G[0, s, :, :, :, lanes] = part.astype(BF16).reshape(4, 2, ROWS, 256)

    def back_step(t, carry):
        s = s_of(3 - t)

        def between(j):
            run_at(t, PLAN_BACK[j])

        attend_back(s, between)

        @pl.when(t < NS - 1)
        def _():
            attend_weight(s)
            credit_step(False)
            scatter_p(0, s, s_of(t))

        return carry

    lax.fori_loop(0, NS, back_step, 0)

    for step in (2, 1, 3, 0):
        i = (z + step) % NS
        rows = pl.ds(pl.multiple_of(i * CHUNK, CHUNK), CHUNK)
        normal, scale = norm_stats(X[i].astype(F32))
        grad = ACC2[rows, :]
        SG[0:1, :] += column_sum(grad * normal)
        SG[1:2, :] += column_sum(grad)
        N2[i] = (MID[rows, :] + norm_grad(normal, scale, grad, row(gain1))).astype(BF16)

    def sum_z(step):
        other = (z + step) % NS
        return remote(SG, SGR.at[z], sg_send.at[step], sg_recv.at[z], z_dev(other))

    def sum_z_wait():
        for step in range(1, NS):
            origin = (z + step) % NS
            remote(SGR.at[origin], SGR.at[origin], sg_send.at[step], sg_recv.at[origin], z_dev(origin)).wait_recv()
            sum_z(step).wait_send()
        SGR[pl.ds(z, 1)] = SG[...][None]
        SG[...] = (SGR[0] + SGR[1]) + (SGR[2] + SGR[3])

    def sum_copy(step, device):
        return remote(SG, SGR.at[step], sg_send.at[step], sg_recv.at[step], device)

    def sum_end(step, device):
        sum_copy(step, device).wait()
        SG[...] = SG[...] + SGR[step]

    for step in range(1, NS):
        sum_z(step).start()
    for step in (2, 1, 3, 0):
        back_send(1, N2, FR, (z + step) % NS)
    attend_weight(z)
    credit_step(False)
    scatter_p(0, z, s_of(3))
    run("T9 Z8 Q11")
    sum_z_wait()
    sum_copy(4, c_dev).start()
    run("T10")
    sum_end(4, c_dev)
    sum_copy(5, x_dev).start()
    run("R11 Z9")
    weight_sums[1] = scatter_sum(1)
    sum_end(5, x_dev)
    sum_copy(6, y_dev).start()
    weight_sums[2] = scatter_sum(2)
    run("Z10 T11")
    sum_end(6, y_dev)
    weight_sums[0] = scatter_sum(0)
    back_wait(0, FS, out)
    back_wait(1, N2, FR)

    def drain(i, carry):
        m = i // NS
        s = i % NS

        @pl.when((s <= z) & (z < NS - 1))
        def _():
            z_copy(m, s, 1).wait_send()

        @pl.when((s >= z) & (z > 0))
        def _():
            z_copy(m, s, 0).wait_send()

        for kind in range(5):
            plane_copy(kind, m, s).wait_send()
        rs_core(m, s, s).wait_send()
        rs_diag(XFWD, m, s, s).wait_send()
        rs_diag(YFWD, m, s, s).wait_send()
        rs_side(XOWN, m, s, s).wait_send()
        rs_side(YOWN, m, s, s).wait_send()

        @pl.when(s != z)
        def _():
            remote(G.at[m, s, k, c], RZ.at[m, 0], rz_send.at[m, s], rz_recv.at[m, 0], z_dev(pair)).wait_send()

        return carry

    lax.fori_loop(0, 3 * NS, drain, 0)
    for which, source, target in ((0, features, X), (1, cotangent, U)):
        for step in range(1, NS):
            row_copy(which, source, target, (z + step) % NS).wait_send()


def finish_kernel(
    rows, grads, weight_sums, sums,
    out, features_grad, gain1_grad, shift1_grad, project_grad, project_bias_grad, merge_grad, merge_bias_grad,
    gain2_grad, shift2_grad, expand_grad, expand_bias_grad, reduce_grad, reduce_bias_grad,
):
    out[...] = rows[...]
    features_grad[...] = grads[...].astype(F32)
    gain1_grad[...] = sums[0]
    shift1_grad[...] = sums[1]
    gain2_grad[...] = sums[2]
    shift2_grad[...] = sums[3]
    merge_bias_grad[...] = sums[4]
    reduce_bias_grad[...] = sums[5]
    for s in range(NS):
        expand_bias_grad[s * D : (s + 1) * D] = sums[6 + s]
        project_bias_grad[0:1, s * SEC : (s + 1) * SEC] = sums[10 + s : 11 + s, 0:SEC]
        project_bias_grad[1:2, s * SEC : (s + 1) * SEC] = sums[10 + s : 11 + s, 2 * SEC : 3 * SEC]
    for piece in range(3):
        project_grad[piece] = weight_sums[0, :, piece * SEC : (piece + 1) * SEC]
    merge_grad[...] = weight_sums[0, :, 3 * SEC :].T
    expand_grad[...] = weight_sums[1]
    reduce_grad[...] = weight_sums[2]


def block(features, packing, segment_ids, norm1_gain, norm1_shift, project_weight, project_bias, merge_weight, merge_bias,
          norm2_gain, norm2_shift, expand_weight, expand_bias, reduce_weight, reduce_bias, cotangent):
    vmem = pl.BlockSpec(memory_space=pltpu.VMEM)
    anywhere = pl.BlockSpec(memory_space=pl.ANY)
    shape = jax.ShapeDtypeStruct
    inner = pl.pallas_call(
        block_kernel,
        name="block",
        in_specs=[anywhere] + [vmem] * 14 + [anywhere],
        out_specs=[anywhere, anywhere, vmem, vmem],
        out_shape=[
            shape((NS, CHUNK, D), BF16),
            shape((NS, CHUNK, D), BF16),
            shape((3, ROWS, D), F32),
            shape((16, D), F32),
        ],
        scratch_shapes=[
            pltpu.VMEM((3, NS, 4, 2, ROWS, D), BF16),
            pltpu.VMEM((3, NS, 4, 2, ROWS, D), BF16),
            pltpu.VMEM((2, NS, 4, ROWS, D), BF16),
            pltpu.VMEM((2, NS, 2, HALF, D), BF16),
            pltpu.VMEM((2, NS, 2, ROWS, D), BF16),
            pltpu.VMEM((3, 2, ROWS, D), BF16),
            pltpu.VMEM((3, 2, ROWS, D), BF16),
            pltpu.VMEM((NS, CHUNK, D), BF16),
            pltpu.VMEM((NS, CHUNK, D), BF16),
            pltpu.VMEM((D, TOK), BF16),
            pltpu.VMEM((TOK, D), BF16),
            pltpu.VMEM((D, TOK), BF16),
            pltpu.VMEM((NS, CHUNK, D), BF16),
            pltpu.VMEM((D, TOK), BF16),
            pltpu.VMEM((NS, TOK, 640), BF16),
            pltpu.VMEM((NS, TOK, 256), BF16),
            pltpu.VMEM((TOK, D), F32),
            pltpu.VMEM((TOK, D), F32),
            pltpu.VMEM((TOK, D), F32),
            pltpu.VMEM((TOK, D), BF16),
            pltpu.VMEM((TOK, D), BF16),
            pltpu.VMEM((TOK, 256), BF16),
            pltpu.VMEM((TOK, TOK), F32),
            pltpu.VMEM((16, 1, TOK), F32),
            pltpu.VMEM((NS, 1, D), F32),
            pltpu.VMEM((NS, 1, D), F32),
            pltpu.VMEM((7, 16, D), F32),
            pltpu.VMEM((NS, CHUNK, D), BF16),
            pltpu.VMEM((ROWS, D), F32),
            pltpu.SemaphoreType.DMA((2, 3, NS)),
            pltpu.SemaphoreType.DMA((3, NS)),
            pltpu.SemaphoreType.DMA((5, 3, NS)),
            pltpu.SemaphoreType.DMA((5, 3, NS)),
            pltpu.SemaphoreType.DMA((5, 3, NS)),
            pltpu.SemaphoreType.DMA((5, 3, NS)),
            pltpu.SemaphoreType.DMA((3, NS)),
            pltpu.SemaphoreType.DMA((3, 2)),
            pltpu.SemaphoreType.DMA((3, 2)),
            pltpu.SemaphoreType.DMA((2, NS)),
            pltpu.SemaphoreType.DMA((2, NS)),
            pltpu.SemaphoreType.DMA((2, NS)),
            pltpu.SemaphoreType.DMA((2, NS)),
            pltpu.SemaphoreType.DMA((7,)),
            pltpu.SemaphoreType.DMA((7,)),
            pltpu.SemaphoreType.DMA((4,)),
            pltpu.SemaphoreType.REGULAR((3,)),
        ],
        compiler_params=pltpu.CompilerParams(collective_id=0, has_side_effects=True, vmem_limit_bytes=65 * 1000 * 1000),
    )(
        features, packing, segment_ids, norm1_gain, norm1_shift, project_weight, project_bias, merge_weight, merge_bias,
        norm2_gain, norm2_shift, expand_weight, expand_bias, reduce_weight.T, reduce_bias, cotangent,
    )
    results = pl.pallas_call(
        finish_kernel,
        name="finish",
        in_specs=[vmem] * 4,
        out_specs=[vmem] * 14,
        out_shape=[
            shape((NS, CHUNK, D), BF16),
            shape((NS, CHUNK, D), F32),
            shape((D,), F32),
            shape((D,), F32),
            shape((3, ROWS, SEC), F32),
            shape((2, D), F32),
            shape((SEC, ROWS), F32),
            shape((D,), F32),
            shape((D,), F32),
            shape((D,), F32),
            shape((ROWS, D), F32),
            shape((4 * D,), F32),
            shape((ROWS, D), F32),
            shape((D,), F32),
        ],
        compiler_params=pltpu.CompilerParams(vmem_limit_bytes=32 * 1024 * 1024),
    )(*inner)
    return tuple(results[:12]) + (results[12].T, results[13])


def norm_rows(values, gain, shift):
    center = values - jnp.mean(values, axis=-1, keepdims=True)
    spread = jnp.mean(center * center, axis=-1, keepdims=True)
    return center * lax.rsqrt(spread + EPSILON) * gain + shift


def exact_gelu(values):
    return jax.nn.gelu(values, approximate=False)


def swap_rows(values):
    return lax.all_to_all(values, "section", split_axis=0, concat_axis=1, tiled=True)[0]


def swap_back(values):
    return lax.all_to_all(values[None], "section", split_axis=1, concat_axis=0, tiled=True)


def whole(values, dp_axis, section_axis):
    values = lax.all_gather(values, "dp", axis=dp_axis, tiled=True)
    return lax.all_gather(values, "section", axis=section_axis, tiled=True)


def shard(values, dp_axis, section_axis):
    values = lax.psum_scatter(values, "section", scatter_dimension=section_axis, tiled=True)
    return lax.psum_scatter(values, "dp", scatter_dimension=dp_axis, tiled=True)


def body(
    features,
    packing,
    segment_ids,
    norm1_gain,
    norm1_shift,
    project_weight,
    project_bias,
    merge_weight,
    merge_bias,
    norm2_gain,
    norm2_shift,
    expand_weight,
    expand_bias,
    reduce_weight,
    reduce_bias,
    cotangent,
):
    length = packing.shape[2]
    width = features.shape[2]
    heads = width // HEAD_DIM
    scale = HEAD_DIM ** (-0.5)
    mine = lax.axis_index("section")
    order = lax.dynamic_index_in_dim(packing[:, 0], mine, 0, keepdims=False)
    packed_labels = lax.dynamic_index_in_dim(segment_ids[:, 0], mine, 0, keepdims=False)
    labels = jnp.zeros((length,), jnp.int32).at[order].set(packed_labels)
    allowed = labels[:, None] == labels[None, :]

    tokens = swap_rows(features).astype(F32)
    upstream = swap_rows(cotangent)
    project = whole(project_weight, 1, 2)
    merge = whole(merge_weight, 1, 0)
    expand = whole(expand_weight, 0, 1)
    reduce = whole(reduce_weight, 1, 0)

    normed = norm_rows(tokens, norm1_gain, norm1_shift).astype(BF16)
    projected = jnp.einsum("td,cde->cte", normed, project, preferred_element_type=F32)
    queries = (projected[0] + project_bias[0]).astype(BF16).reshape(length, heads, HEAD_DIM)
    keys = projected[1].astype(BF16).reshape(length, heads, HEAD_DIM)
    values = (projected[2] + project_bias[1]).astype(BF16).reshape(length, heads, HEAD_DIM)
    scores = jnp.einsum("qhd,khd->hqk", queries, keys, preferred_element_type=F32) * scale
    scores = jnp.where(allowed[None], scores, MASKED)
    peak = jnp.max(scores, axis=-1, keepdims=True)
    weights = jnp.exp(scores - peak)
    probs = weights / jnp.sum(weights, axis=-1, keepdims=True)
    low_probs = probs.astype(BF16)
    mixed = jnp.einsum("hqk,khd->qhd", low_probs, values, preferred_element_type=F32)
    mixed = mixed.reshape(length, width).astype(BF16)
    middle = tokens + (jnp.dot(mixed, merge, preferred_element_type=F32) + merge_bias)
    normed_two = norm_rows(middle, norm2_gain, norm2_shift).astype(BF16)
    hidden = jnp.dot(normed_two, expand, preferred_element_type=F32) + expand_bias
    active = exact_gelu(hidden).astype(BF16)
    second = jnp.dot(active, reduce, preferred_element_type=F32)
    output = swap_back((middle + (second + reduce_bias)).astype(BF16))

    wide_upstream = upstream.astype(F32)
    reduce_bias_grad = jnp.sum(wide_upstream, axis=0)
    reduce_grad = jnp.einsum("tf,td->fd", active, upstream, preferred_element_type=F32)
    grad_active = jnp.einsum("td,fd->tf", upstream, reduce, preferred_element_type=F32)
    _, gelu_back = jax.vjp(exact_gelu, hidden)
    grad_hidden = gelu_back(grad_active)[0].astype(BF16)
    expand_bias_grad = jnp.sum(grad_hidden.astype(F32), axis=0)
    expand_grad = jnp.einsum("td,tf->df", normed_two, grad_hidden, preferred_element_type=F32)
    grad_normed_two = jnp.einsum("tf,df->td", grad_hidden, expand, preferred_element_type=F32)
    _, norm_back = jax.vjp(norm_rows, middle, norm2_gain, norm2_shift)
    grad_from_norm, gain_two, shift_two = norm_back(grad_normed_two)
    grad_middle = wide_upstream + grad_from_norm
    grad_branch = grad_middle.astype(BF16)
    merge_bias_grad = jnp.sum(grad_branch.astype(F32), axis=0)
    merge_grad = jnp.einsum("te,td->ed", mixed, grad_branch, preferred_element_type=F32)
    grad_mixed = jnp.einsum("td,ed->te", grad_branch, merge, preferred_element_type=F32)
    grad_mixed = grad_mixed.astype(BF16).reshape(length, heads, HEAD_DIM)
    grad_probs = jnp.einsum("qhd,khd->hqk", grad_mixed, values, preferred_element_type=F32)
    inner = jnp.sum(probs * grad_probs, axis=-1, keepdims=True)
    grad_scores = (probs * (grad_probs - inner)).astype(BF16)
    grad_queries = jnp.einsum("hqk,khd->qhd", grad_scores, keys, preferred_element_type=F32) * scale
    grad_keys = jnp.einsum("hqk,qhd->khd", grad_scores, queries, preferred_element_type=F32) * scale
    grad_values = jnp.einsum("hqk,qhd->khd", low_probs, grad_mixed, preferred_element_type=F32)
    stacked = jnp.stack([grad_queries, grad_keys, grad_values])
    stacked = stacked.reshape(3, length, width).astype(BF16)
    wide = stacked.astype(F32)
    project_bias_grad = jnp.stack([jnp.sum(wide[0], axis=0), jnp.sum(wide[2], axis=0)])
    project_grad = jnp.einsum("td,cte->cde", normed, stacked, preferred_element_type=F32)
    grad_normed = jnp.einsum("cte,cde->td", stacked, project, preferred_element_type=F32)
    _, first_back = jax.vjp(norm_rows, tokens, norm1_gain, norm1_shift)
    grad_tokens, gain_one, shift_one = first_back(grad_normed)
    features_grad = swap_back(grad_middle + grad_tokens)

    summed = lax.psum(
        (
            gain_one,
            shift_one,
            project_bias_grad,
            merge_bias_grad,
            gain_two,
            shift_two,
            expand_bias_grad,
            reduce_bias_grad,
        ),
        ("dp", "section"),
    )
    return (
        output,
        features_grad,
        summed[0],
        summed[1],
        shard(project_grad, 1, 2),
        summed[2],
        shard(merge_grad, 1, 0),
        summed[3],
        summed[4],
        summed[5],
        shard(expand_grad, 0, 1),
        summed[6],
        shard(reduce_grad, 1, 0),
        summed[7],
    )


def solution(mesh):
    rows = P(None, ("dp", "section"), None)
    groups = P(None, "dp", None)
    project = P(None, "dp", "section")
    inward = P("section", "dp")
    outward = P("dp", "section")
    in_specs = (rows, groups, groups, P(), P(), project, P(), inward, P(), P(), P(), outward, P(), inward, P(), rows)
    out_specs = (rows, rows, P(), P(), project, P(), inward, P(), P(), P(), outward, P(), inward, P())
    fits = mesh.shape["dp"] == 8 and mesh.shape["section"] == NS
    return jax.shard_map(block if fits else body, mesh=mesh, in_specs=in_specs, out_specs=out_specs, check_vma=False)
```

```python
import functools

import jax
import jax.numpy as jnp
from jax import lax
from jax.experimental import pallas as pl
from jax.experimental.pallas import tpu as pltpu
from jax.sharding import PartitionSpec as P

HEAD_DIM = 64
EPSILON = 1e-06
MASKED = -1000000000.0
F32 = jnp.float32
BF16 = jnp.bfloat16
MESH_ID = pl.DeviceIdType.MESH

NS = 4
D = 768
TOK = 512
ROWS = 96
HALF = 48
SEC = 192
NT_DIMS = (((1,), (1,)), ((), ()))
TN_DIMS = (((0,), (0,)), ((), ()))
CORE, XOWN, YOWN, XFWD, YFWD = range(5)
CHUNK = 128

def norm_stats(values):
    center = values - jnp.mean(values, axis=-1, keepdims=True)
    spread = jnp.mean(center * center, axis=-1, keepdims=True)
    scale = lax.rsqrt(spread + EPSILON)
    return center * scale, scale


def norm_grad(normal, scale, grad, gain):
    scaled = grad * gain
    first = jnp.mean(scaled, axis=-1, keepdims=True)
    second = jnp.mean(scaled * normal, axis=-1, keepdims=True)
    return scale * (scaled - first - normal * second)


def dot(left, right, dims=(((1,), (0,)), ((), ()))):
    return lax.dot_general(left, right, dims, preferred_element_type=F32)


def row(values):
    return values[...].reshape(1, D)


def column_sum(values):
    return jnp.sum(values, axis=0, keepdims=True)


def block_kernel(
    features, packing, segments, gain1, shift1, project, project_bias, merge, merge_bias, gain2, shift2,
    expand, expand_bias, reduce, reduce_bias, cotangent,
    out, FR, weight_sums, SG,
    W, G, RC, RD, RE, RZ, RY, X, U, UT, N1, N1T, N2, N2T, QA, AT, MID, ACC1, ACC2, AC, GH, MASK, LSE, PB, EB, SGR, FS, TB,
    z_send, z_recv, g_send, g_recv, r_send, r_recv, rz_send, rz_recv, ry_recv, in_send, in_recv, out_send, out_recv,
    sg_send, sg_recv, local_sem, credit,
):
    dp = lax.axis_index("dp")
    z = lax.axis_index("section")
    c = dp % 2
    k = dp // 2
    xi = k % 2
    yi = k // 2
    kx = 2 * yi + (1 - xi)
    ky = 2 * (1 - yi) + xi
    kd = 3 - k
    x_dev = {"dp": 2 * kx + c, "section": z}
    y_dev = {"dp": 2 * ky + c, "section": z}
    c_dev = {"dp": 2 * k + (1 - c), "section": z}

    def z_dev(other):
        return {"dp": dp, "section": other}

    half = z // 2
    inner = ((z + 1) // 2) % 2 == 1
    outer = ((z + 1) // 2) % 2 == 0
    pair = z + 1 - 2 * (z % 2)
    start = (1 - half) * (z % 2) + half * (1 - z % 2)

    def s_of(t):
        base = (t // 2) * t + (1 - t // 2) * ((start + t) % 2)
        return half * 3 + (1 - 2 * half) * base

    def remote(src, dst, send, recv, device):
        return pltpu.make_async_remote_copy(
            src_ref=src, dst_ref=dst, send_sem=send, recv_sem=recv, device_id=device, device_id_type=MESH_ID
        )

    barrier = pltpu.get_barrier_semaphore()
    for device in (x_dev, y_dev, c_dev):
        pl.semaphore_signal(barrier, inc=1, device_id=device, device_id_type=MESH_ID)
    for step in range(1, NS):
        pl.semaphore_signal(barrier, inc=1, device_id=z_dev((z + step) % NS), device_id_type=MESH_ID)

    for piece in range(3):
        TB[:, piece * SEC : (piece + 1) * SEC] = project[piece].astype(F32)
    TB[:, 3 * SEC :] = merge[...].astype(F32).T
    W[0, pl.ds(z, 1), pl.ds(k, 1), pl.ds(c, 1)] = TB[...].astype(BF16)[None, None, None]
    W[1, pl.ds(z, 1), pl.ds(k, 1), pl.ds(c, 1)] = expand[...][None, None, None]
    W[2, pl.ds(z, 1), pl.ds(k, 1), pl.ds(c, 1)] = reduce[...][None, None, None]
    pl.semaphore_wait(barrier, 6)

    def z_copy(m, s, up):
        place = W.at[m, s, k, c]
        return remote(place, place, z_send.at[up, m, s], z_recv.at[m, s], z_dev(z + 2 * up - 1))

    def z_pass(m, s):
        @pl.when((s <= z) & (z < NS - 1))
        def _():
            z_copy(m, s, 1).start()

        @pl.when((s >= z) & (z > 0))
        def _():
            z_copy(m, s, 0).start()

    def plane_copy(kind, m, s, receive=False):
        rows = slice(None)
        if kind == CORE:
            place = W.at[m, s, :, (1 - c) if receive else c]
            return remote(place, place, g_send.at[kind, m, s], g_recv.at[kind, m, s], c_dev)
        if kind == XOWN:
            place = W.at[m, s, kx if receive else k, c]
            return remote(place, place, g_send.at[kind, m, s], g_recv.at[kind, m, s], x_dev)
        if kind == YOWN:
            place = W.at[m, s, ky if receive else k, c]
            return remote(place, place, g_send.at[kind, m, s], g_recv.at[kind, m, s], y_dev)
        if kind == XFWD:
            place = W.at[m, s, kd if receive else ky, c, pl.ds(0, HALF)]
            return remote(place, place, g_send.at[kind, m, s], g_recv.at[kind, m, s], x_dev)
        place = W.at[m, s, kd if receive else kx, c, pl.ds(HALF, HALF)]
        return remote(place, place, g_send.at[kind, m, s], g_recv.at[kind, m, s], y_dev)

    def guard(condition, action):
        if isinstance(condition, bool):
            if condition:
                action()
        else:
            pl.when(condition)(action)

    def place_of(i):
        if isinstance(i, int) and i < 3:
            return i, 0
        late = i // 6
        return late * (1 + i % 2), late * (i // 2 - 2) + (1 - late) * (i - 2)

    def gather_a(i):
        def action():
            m, t = place_of(i)
            s = s_of(t)
            if not isinstance(i, int) or i > 2:
                z_copy(m, s, 0).wait_recv()
                z_pass(m, s)
            plane_copy(XOWN, m, s).start()
            plane_copy(YOWN, m, s).start()

        guard(i <= 11, action)

    def gather_b(i):
        def action():
            m, t = place_of(i)
            s = s_of(t)
            plane_copy(YOWN, m, s, True).wait_recv()
            plane_copy(XFWD, m, s).start()
            plane_copy(XOWN, m, s, True).wait_recv()
            plane_copy(YFWD, m, s).start()

        guard(i <= 11, action)

    def gather_c(i):
        def action():
            m, t = place_of(i)
            s = s_of(t)
            plane_copy(XFWD, m, s, True).wait_recv()
            plane_copy(YFWD, m, s, True).wait_recv()
            plane_copy(CORE, m, s).start()

        guard(i <= 11, action)

    def gather_d(m, t):
        plane_copy(CORE, m, s_of(t), True).wait_recv()

    def pump(i):
        gather_a(i + 3)
        gather_b(i + 1)
        gather_c(i)

    def rs_core(m, s, at, receive=False):
        place = RC.at[m % 2, at]
        source = place if receive else G.at[m, s, :, 1 - c]
        return remote(source, place, r_send.at[CORE, m, s], r_recv.at[CORE, m, s], c_dev)

    def rs_diag(kind, m, s, at):
        which, device = (0, x_dev) if kind == XFWD else (1, y_dev)
        return remote(
            G.at[m, s, kd, c, pl.ds(which * HALF, HALF)], RD.at[m % 2, at, which],
            r_send.at[kind, m, s], r_recv.at[kind, m, s], device,
        )

    def rs_side(kind, m, s, at):
        which, device, block = (0, x_dev, kx) if kind == XOWN else (1, y_dev, ky)
        return remote(
            G.at[m, s, block, c], RE.at[m % 2, at, which], r_send.at[kind, m, s], r_recv.at[kind, m, s], device
        )

    def rs_near(m, s):
        near = s // 2 == z // 2
        place = G.at[m, s, k, c]

        @pl.when(near)
        def _():
            remote(place, RZ.at[m, 0], rz_send.at[m, s], rz_recv.at[m, 0], z_dev(pair)).start()

        @pl.when(jnp.logical_not(near) & outer)
        def _():
            remote(place, RY.at[m, s % 2], rz_send.at[m, s], ry_recv.at[m, s % 2], z_dev(pair)).start()

    def rs_far(m, s):
        @pl.when((s // 2 != z // 2) & inner)
        def _():
            place = G.at[m, s, k, c]
            buffer = RY.at[m, s % 2]
            remote(buffer, buffer, rz_send.at[m, s], ry_recv.at[m, s % 2], z_dev(pair)).wait_recv()
            add_into(place, buffer)
            remote(place, RZ.at[m, 1], rz_send.at[m, s], rz_recv.at[m, 1], z_dev(s)).start()

    def add_into(place, other):
        place[...] = place[...] + other[...]

    def scatter_place(r):
        if r < 8:
            return 2 - r % 2, s_of(r // 2), s_of(r // 2)
        return 0, s_of(11 - r), s_of(r - 8)

    def credit_give(at):
        for device, which in ((c_dev, 0), (x_dev, 1), (y_dev, 2)):
            pl.semaphore_signal(credit.at[which, at], inc=1, device_id=device, device_id_type=MESH_ID)

    def credit_take(at):
        for which in range(3):
            pl.semaphore_wait(credit.at[which, at], 1)

    def scatter_p(m, s, at):
        rs_core(m, s, at).start()

    def scatter_q(r):
        m, s, at = scatter_place(r)
        rs_core(m, s, at, True).wait_recv()
        for block in range(4):
            add_into(G.at[m, s, block, c], RC.at[m % 2, at, block])
        rs_diag(XFWD, m, s, at).start()
        rs_diag(YFWD, m, s, at).start()

    def scatter_r(r):
        m, s, at = scatter_place(r)
        rs_diag(XFWD, m, s, at).wait_recv()
        add_into(G.at[m, s, ky, c, pl.ds(0, HALF)], RD.at[m % 2, at, 0])
        rs_side(YOWN, m, s, at).start()
        rs_diag(YFWD, m, s, at).wait_recv()
        add_into(G.at[m, s, kx, c, pl.ds(HALF, HALF)], RD.at[m % 2, at, 1])
        rs_side(XOWN, m, s, at).start()

    def scatter_t(r):
        m, s, at = scatter_place(r)
        rs_side(XOWN, m, s, at).wait_recv()
        rs_side(YOWN, m, s, at).wait_recv()
        place = G.at[m, s, k, c]
        total = RE[m % 2, at, 0].astype(F32) + RE[m % 2, at, 1].astype(F32)
        place[...] = (place[...].astype(F32) + total).astype(BF16)
        if r in (0, 2, 4, 6):
            credit_give(r // 2)
        pl.when(s != z)(lambda: rs_near(m, s))

    def scatter_z(r):
        m, s, _ = scatter_place(r)
        rs_far(m, s)

    def scatter_sum(m):
        total = G[m, z, k, c].astype(F32)
        for which in range(2):
            remote(RZ.at[m, which], RZ.at[m, which], rz_send.at[m, z], rz_recv.at[m, which], z_dev(pair)).wait_recv()
            total = total + RZ[m, which].astype(F32)
        return total

    def row_copy(which, source, target, there):
        return remote(source.at[there], target.at[z], in_send.at[which, there], in_recv.at[which, z], z_dev(there))

    def rows_send(which, source, target):
        for there in range(NS):

            @pl.when(there != z)
            def _():
                row_copy(which, source, target, there).start()

        pltpu.make_async_copy(source.at[z], target.at[z], local_sem.at[which]).start()

    def rows_wait(which, source, target, t):
        origin = s_of(t)
        if t == 0:
            pltpu.make_async_copy(source.at[z], target.at[z], local_sem.at[which]).wait()
        else:
            remote(
                source.at[origin], target.at[origin], in_send.at[which, origin], in_recv.at[which, origin], z_dev(origin)
            ).wait_recv()
        return origin

    def back_send(which, source, target, there):
        @pl.when(there != z)
        def _():
            remote(
                source.at[there], target.at[z], out_send.at[which, there], out_recv.at[which, z], z_dev(there)
            ).start()

        @pl.when(there == z)
        def _():
            pltpu.make_async_copy(source.at[z], target.at[z], local_sem.at[2 + which]).start()

    def back_wait(which, source, target):
        for step in range(1, NS):
            other = (z + step) % NS
            remote(
                source.at[other], target.at[other], out_send.at[which, other], out_recv.at[which, other], z_dev(other)
            ).wait()
        pltpu.make_async_copy(source.at[z], target.at[z], local_sem.at[2 + which]).wait()

    def sum_z(step):
        other = (z + step) % NS
        return remote(SG, SGR.at[z], sg_send.at[step], sg_recv.at[z], z_dev(other))

    def sum_z_wait():
        for step in range(1, NS):
            origin = (z + step) % NS
            remote(SGR.at[origin], SGR.at[origin], sg_send.at[step], sg_recv.at[origin], z_dev(origin)).wait_recv()
            sum_z(step).wait_send()
        SGR[pl.ds(z, 1)] = SG[...][None]
        SG[...] = (SGR[0] + SGR[1]) + (SGR[2] + SGR[3])

    def sum_copy(step, device):
        return remote(SG, SGR.at[step], sg_send.at[step], sg_recv.at[step], device)

    def sum_end(step, device):
        sum_copy(step, device).wait()
        SG[...] = SG[...] + SGR[step]

    def rows_home():
        for step in (2, 1, 3, 0):
            back_send(1, N2, FR, (z + step) % NS)

    z_pass(0, z)

    @pl.when(inner)
    def _():
        z_pass(1, z)
        gather_a(0)
        gather_a(1)
        gather_a(3)
        z_pass(2, z)
        gather_a(8)
        gather_a(4)
        gather_a(2)
        gather_b(0)
        rows_send(0, features, X)
        gather_b(1)

    @pl.when(outer)
    def _():
        gather_a(0)
        gather_a(2)
        gather_a(1)
        gather_a(3)
        rows_send(0, features, X)
        gather_b(2)
        z_pass(1, z)
        gather_b(0)
        gather_a(7)
        gather_c(2)
        gather_b(1)
        gather_b(7)
        z_pass(2, z)

    order = packing[z]
    labels = segments[z].astype(F32)
    token = lax.broadcasted_iota(jnp.int32, (TOK, TOK), 0)
    token_labels = jnp.sum(jnp.where(token == order, labels, 0.0), axis=1, keepdims=True)
    kinds = lax.broadcasted_iota(jnp.int32, (TOK, 128), 1).astype(F32)
    one_hot = jnp.where(token_labels == kinds, 1.0, 0.0).astype(BF16)
    MASK[...] = (dot(one_hot, one_hot, NT_DIMS) - 1.0) * -MASKED
    AT[:, :, 0:64] = jnp.zeros((NS, TOK, 64), BF16)
    SG[...] = jnp.zeros_like(SG)
    PB[...] = jnp.zeros_like(PB)
    for s in range(NS):
        EB[s] = expand_bias[s * D : (s + 1) * D].reshape(1, D)
        PB[s, :, 0:SEC] = project_bias[0:1, s * SEC : (s + 1) * SEC]
        PB[s, :, 2 * SEC : 3 * SEC] = project_bias[1:2, s * SEC : (s + 1) * SEC]

    gather_b(3)

    @pl.when(inner)
    def _():
        gather_c(0)
        gather_a(5)
        gather_b(4)
        gather_c(1)
        gather_a(7)

    @pl.when(outer)
    def _():
        gather_c(3)
        gather_a(6)
        gather_a(8)
        gather_c(1)
        gather_a(4)
        gather_a(5)
        gather_c(0)

    for t in range(NS):
        i = rows_wait(0, features, X, t)
        rows = pl.ds(pl.multiple_of(i * CHUNK, CHUNK), CHUNK)
        normal, _ = norm_stats(X[i].astype(F32))
        normed = normal * row(gain1) + row(shift1)
        N1[rows, :] = normed.astype(BF16)
        N1T[:, rows] = normed.T.astype(BF16)

    def weight(m, s):
        return W[m, s].reshape(D, D)

    def weight_tile(m, s, n):
        return W[m, s, :, :, :, pl.ds(pl.multiple_of(n * 256, 256), 256)].reshape(D, 256)

    def weight_end(s):
        return W[0, s, :, :, :, 512:768].reshape(D, 256)

    def attend(s, between):
        for first, last in ((0, 256), (256, 512), (512, 640)):
            part = dot(N1[...], W[0, s, :, :, :, first:last].reshape(D, last - first))
            QA[s, :, first:last] = (part + PB[s, :, first:last]).astype(BF16)
        between()
        for j in range(3):
            keys = QA[s, :, SEC + 64 * j : SEC + 64 * j + 64]
            values = QA[s, :, 2 * SEC + 64 * j : 2 * SEC + 64 * j + 64]
            queries = QA[s, :, 64 * j : 64 * j + 64] * 0.125
            scores = dot(keys, queries, NT_DIMS) + MASK[...]
            peak = jnp.max(scores, axis=0, keepdims=True)
            weights = jnp.exp(scores - peak)
            total = jnp.sum(weights, axis=0, keepdims=True)
            LSE[s * 3 + j] = peak + jnp.log(total)
            mixed = dot(values, weights.astype(BF16), TN_DIMS) * (1.0 / total)
            AT[s, :, 64 + 64 * j : 128 + 64 * j] = mixed.T.astype(BF16)
        ACC1[...] += dot(AT[s], weight_end(s), NT_DIMS)

    ACC1[...] = jnp.zeros_like(ACC1)

    @pl.when(outer)
    def _():
        rows_send(1, cotangent, U)

    def attend_step(t, carry):

        @pl.when(t == 0)
        def _():
            gather_b(5)

            @pl.when(outer)
            def _():
                gather_b(4)
                gather_c(7)

        @pl.when(t == 1)
        def _():

            @pl.when(inner)
            def _():
                gather_c(3)
                rows_send(1, cotangent, U)
                gather_b(7)
                gather_a(11)

        @pl.when(t == 2)
        def _():

            @pl.when(inner)
            def _():
                gather_c(5)
                gather_c(4)

            @pl.when(outer)
            def _():
                gather_a(9)
                gather_c(5)
                gather_b(8)
                gather_c(6)

        @pl.when(t == 3)
        def _():

            @pl.when(inner)
            def _():
                gather_b(6)
                gather_c(7)
                gather_a(10)

        gather_d(0, t)

        def between():

            @pl.when(t == 0)
            def _():

                @pl.when(inner)
                def _():
                    gather_b(2)
                    gather_a(9)
                    gather_a(6)

            @pl.when(t == 1)
            def _():

                @pl.when(outer)
                def _():
                    gather_c(4)
                    gather_b(6)

            @pl.when(t == 2)
            def _():

                @pl.when(inner)
                def _():
                    gather_c(2)
                    gather_b(9)

            @pl.when(t == 3)
            def _():

                @pl.when(outer)
                def _():
                    gather_a(11)
                    gather_b(9)
                    gather_c(8)

        attend(s_of(t), between)
        return carry

    lax.fori_loop(0, NS, attend_step, 0)


    for i in range(NS):
        rows = slice(i * CHUNK, (i + 1) * CHUNK)
        middle = X[i].astype(F32) + (ACC1[rows, :] + row(merge_bias))
        MID[rows, :] = middle
        normal, _ = norm_stats(middle)
        normed = normal * row(gain2) + row(shift2)
        N2[i] = normed.astype(BF16)
        N2T[:, rows] = normed.T.astype(BF16)

    for t in range(NS):
        i = rows_wait(1, cotangent, U, t)
        upstream = U[i].astype(F32)
        UT[:, pl.ds(pl.multiple_of(i * CHUNK, CHUNK), CHUNK)] = upstream.T.astype(BF16)
        SG[5:6, :] += column_sum(upstream)
    ACC1[...] = jnp.zeros_like(ACC1)
    ACC2[...] = jnp.zeros_like(ACC2)

    @pl.when(inner)
    def _():
        gather_c(9)
        gather_b(8)
        gather_c(6)

    def feed(s, between):
        def tile_step(n, carry):
            lanes = pl.ds(pl.multiple_of(n * 256, 256), 256)
            hidden = dot(N2[...].reshape(TOK, D), weight_tile(1, s, n)) + EB[s, :, lanes]
            gate = 0.5 + 0.5 * lax.erf(hidden * 0.7071067811865476)
            active = (hidden * gate).astype(BF16)
            AC[:, lanes] = active
            slope = gate + hidden * (jnp.exp(-0.5 * hidden * hidden) * 0.3989422804014327)
            G[2, s, :, :, :, lanes] = dot(UT[...], active).astype(BF16).reshape(4, 2, ROWS, 256)
            grad_active = dot(U[...].reshape(TOK, D), weight_tile(2, s, n))
            grad_hidden = (grad_active * slope).astype(BF16)
            GH[:, lanes] = grad_hidden
            SG[pl.ds(6 + s, 1), lanes] = column_sum(grad_hidden.astype(F32))
            G[1, s, :, :, :, lanes] = dot(N2T[...], grad_hidden).astype(BF16).reshape(4, 2, ROWS, 256)
            return carry

        lax.fori_loop(0, 3, tile_step, 0, unroll=True)
        between()
        ACC1[...] += dot(AC[...], weight(2, s), NT_DIMS)
        ACC2[...] += dot(GH[...], weight(1, s), NT_DIMS)

    def feed_step(t, carry):
        s = s_of(t)

        def before():

            @pl.when(t == 0)
            def _():

                @pl.when(outer)
                def _():
                    gather_a(10)

            @pl.when(t == 1)
            def _():
                gather_b(10)

                @pl.when(inner)
                def _():
                    gather_c(8)

            @pl.when(t == 2)
            def _():
                gather_c(11)

                @pl.when(inner)
                def _():
                    scatter_q(0)
                    gather_c(10)

            @pl.when(t == 3)
            def _():
                scatter_q(2)

        def between():
            scatter_p(2, s, s)
            scatter_p(1, s, s)

            @pl.when(t == 0)
            def _():

                @pl.when(outer)
                def _():
                    gather_c(9)

                gather_b(11)

            @pl.when(t == 1)
            def _():

                @pl.when(outer)
                def _():
                    scatter_q(0)
                    gather_c(10)

            @pl.when(t == 2)
            def _():
                scatter_r(0)

            @pl.when(t == 3)
            def _():

                @pl.when(inner)
                def _():
                    scatter_q(4)

        before()
        gather_d(1, t)
        gather_d(2, t)
        feed(s, between)
        return carry

    lax.fori_loop(0, NS, feed_step, 0)

    for i in range(NS):
        rows = slice(i * CHUNK, (i + 1) * CHUNK)
        FS[i] = (MID[rows, :] + (ACC1[rows, :] + row(reduce_bias))).astype(BF16)
        back_send(0, FS, out, i)

    @pl.when(inner)
    def _():
        scatter_q(1)
        scatter_r(2)

    @pl.when(outer)
    def _():
        scatter_r(2)
        scatter_q(4)
        scatter_t(0)

    for i in range(NS):
        rows = slice(i * CHUNK, (i + 1) * CHUNK)
        normal, scale = norm_stats(MID[rows, :])
        grad = ACC2[rows, :]
        grad_middle = U[i].astype(F32) + norm_grad(normal, scale, grad, row(gain2))
        SG[2:3, :] += column_sum(grad * normal)
        SG[3:4, :] += column_sum(grad)
        grad_branch = grad_middle.astype(BF16)
        SG[4:5, :] += column_sum(grad_branch.astype(F32))
        MID[rows, :] = grad_middle
        AC[rows, :] = grad_branch
        UT[:, rows] = grad_branch.astype(F32).T.astype(BF16)
    ACC2[...] = jnp.zeros_like(ACC2)

    @pl.when(inner)
    def _():
        scatter_t(0)

    scatter_q(6)

    def attend_back(s, between):
        N1[:, 0:256] = dot(AC[...], weight_end(s)).astype(BF16)
        GH[:, 512:768] = jnp.zeros((TOK, 256), BF16)
        for j in range(3):
            keys = QA[s, :, SEC + 64 * j : SEC + 64 * j + 64]
            values = QA[s, :, 2 * SEC + 64 * j : 2 * SEC + 64 * j + 64]
            queries = QA[s, :, 64 * j : 64 * j + 64] * 0.125
            grad_mixed = N1[:, 64 + 64 * j : 128 + 64 * j]
            scores = dot(keys, queries, NT_DIMS) + MASK[...]
            probs = jnp.exp(scores - LSE[s * 3 + j])
            grad_probs = dot(values, grad_mixed, NT_DIMS)
            inner = jnp.sum(probs * grad_probs, axis=0, keepdims=True)
            grad_scores = (probs * (grad_probs - inner)).astype(BF16)
            grad_queries = dot(keys, grad_scores, TN_DIMS) * 0.125
            GH[:, 64 * j : 64 * j + 64] = grad_queries.T.astype(BF16)
            GH[:, SEC + 64 * j : SEC + 64 * j + 64] = dot(grad_scores, queries).astype(BF16)
            GH[:, 2 * SEC + 64 * j : 2 * SEC + 64 * j + 64] = dot(probs.astype(BF16), grad_mixed).astype(BF16)
        between()
        SG[pl.ds(10 + s, 1), :] = column_sum(GH[...].astype(F32))
        ACC2[...] += dot(GH[...], weight(0, s), NT_DIMS)

    def attend_weight(s):
        for n in range(3):
            lanes = slice(n * 256, n * 256 + 256)
            part = dot(N1T[...], GH[:, lanes])
            if n == 2:
                part += dot(UT[...], AT[s])
            G[0, s, :, :, :, lanes] = part.astype(BF16).reshape(4, 2, ROWS, 256)

    def back_step(t, carry):
        s = s_of(3 - t)

        def before():

            @pl.when(t == 1)
            def _():

                @pl.when(inner)
                def _():
                    scatter_r(6)

                @pl.when(outer)
                def _():
                    scatter_r(4)

                scatter_t(2)

            @pl.when(t == 2)
            def _():

                @pl.when(inner)
                def _():
                    scatter_r(1)

                @pl.when(outer)
                def _():
                    scatter_t(4)
                    scatter_r(5)
                    scatter_q(7)

            @pl.when(t == 3)
            def _():

                @pl.when(inner)
                def _():
                    scatter_z(4)
                    scatter_r(7)

                @pl.when(outer)
                def _():
                    scatter_r(7)
                    scatter_q(9)

        def between():

            @pl.when(t == 0)
            def _():
                scatter_q(5)

                @pl.when(inner)
                def _():
                    scatter_r(4)

            @pl.when(t == 1)
            def _():

                @pl.when(inner)
                def _():
                    scatter_q(7)
                    scatter_r(5)

                @pl.when(outer)
                def _():
                    scatter_r(6)

            @pl.when(t == 2)
            def _():

                @pl.when(inner)
                def _():
                    scatter_t(6)
                    scatter_t(4)

                @pl.when(outer)
                def _():
                    scatter_q(3)
                    scatter_q(1)
                    scatter_q(8)
                    scatter_t(6)

            @pl.when(t == 3)
            def _():

                @pl.when(inner)
                def _():
                    scatter_z(6)
                    scatter_q(10)

                @pl.when(outer)
                def _():
                    scatter_t(5)
                    scatter_r(8)

        before()
        attend_back(s, between)

        @pl.when(t < NS - 1)
        def _():
            attend_weight(s)
            credit_take(t)
            scatter_p(0, s, s_of(t))

        return carry

    lax.fori_loop(0, NS, back_step, 0)


    @pl.when(inner)
    def _():
        scatter_q(8)
        scatter_q(3)

    for step in (2, 1, 3, 0):
        i = (z + step) % NS
        rows = pl.ds(pl.multiple_of(i * CHUNK, CHUNK), CHUNK)
        normal, _ = norm_stats(X[i].astype(F32))
        grad = ACC2[rows, :]
        SG[0:1, :] += column_sum(grad * normal)
        SG[1:2, :] += column_sum(grad)
    for step in range(1, NS):
        sum_z(step).start()
    for step in (2, 1, 3, 0):
        i = (z + step) % NS
        rows = pl.ds(pl.multiple_of(i * CHUNK, CHUNK), CHUNK)
        normal, scale = norm_stats(X[i].astype(F32))
        N2[i] = (MID[rows, :] + norm_grad(normal, scale, ACC2[rows, :], row(gain1))).astype(BF16)

    @pl.when(inner)
    def _():
        scatter_r(10)
        scatter_t(7)

    @pl.when(outer)
    def _():
        scatter_t(7)
        scatter_r(9)
        scatter_q(10)

    attend_weight(z)
    credit_take(3)
    scatter_p(0, z, s_of(3))

    @pl.when(inner)
    def _():
        rows_home()
        scatter_q(11)
        scatter_r(11)
        scatter_t(10)
        scatter_t(1)
        sum_z_wait()
        scatter_r(8)
        sum_copy(4, c_dev).start()
        scatter_t(5)
        scatter_z(7)
        scatter_q(9)
        weight_sums[2] = scatter_sum(2)
        scatter_t(8)
        sum_end(4, c_dev)
        scatter_z(5)
        scatter_r(3)
        sum_copy(5, x_dev).start()
        scatter_z(8)
        scatter_r(9)
        scatter_t(3)
        scatter_t(9)
        scatter_t(11)
        sum_end(5, x_dev)
        scatter_z(9)
        scatter_z(10)
        sum_copy(6, y_dev).start()
        scatter_z(1)
        scatter_z(2)
        sum_end(6, y_dev)
        scatter_z(0)
        weight_sums[1] = scatter_sum(1)
        weight_sums[0] = scatter_sum(0)
        scatter_z(3)

    @pl.when(outer)
    def _():
        weight_sums[2] = scatter_sum(2)
        scatter_t(8)
        scatter_q(11)
        sum_z_wait()
        scatter_r(1)
        rows_home()
        scatter_r(11)
        sum_copy(4, c_dev).start()
        sum_end(4, c_dev)
        sum_copy(5, x_dev).start()
        scatter_r(3)
        scatter_r(10)
        sum_end(5, x_dev)
        scatter_t(9)
        scatter_t(1)
        scatter_t(3)
        sum_copy(6, y_dev).start()
        sum_end(6, y_dev)
        scatter_t(10)
        scatter_t(11)
        weight_sums[1] = scatter_sum(1)
        weight_sums[0] = scatter_sum(0)

    back_wait(0, FS, out)
    back_wait(1, N2, FR)

    def drain(i, carry):
        m = i // NS
        s = i % NS

        @pl.when((s <= z) & (z < NS - 1))
        def _():
            z_copy(m, s, 1).wait_send()

        @pl.when((s >= z) & (z > 0))
        def _():
            z_copy(m, s, 0).wait_send()

        for kind in range(5):
            plane_copy(kind, m, s).wait_send()
        rs_core(m, s, s).wait_send()
        rs_diag(XFWD, m, s, s).wait_send()
        rs_diag(YFWD, m, s, s).wait_send()
        rs_side(XOWN, m, s, s).wait_send()
        rs_side(YOWN, m, s, s).wait_send()

        @pl.when(s != z)
        def _():
            remote(G.at[m, s, k, c], RZ.at[m, 0], rz_send.at[m, s], rz_recv.at[m, 0], z_dev(pair)).wait_send()

        return carry

    lax.fori_loop(0, 3 * NS, drain, 0)
    for which, source, target in ((0, features, X), (1, cotangent, U)):
        for step in range(1, NS):
            row_copy(which, source, target, (z + step) % NS).wait_send()


def finish_kernel(
    rows, grads, weight_sums, sums,
    out, features_grad, gain1_grad, shift1_grad, project_grad, project_bias_grad, merge_grad, merge_bias_grad,
    gain2_grad, shift2_grad, expand_grad, expand_bias_grad, reduce_grad, reduce_bias_grad,
    low_rows, wide, carried, project_sums, small, sem_in, sem_out,
):
    first = pltpu.make_async_copy(sums, small, sem_in.at[0])
    second = pltpu.make_async_copy(weight_sums.at[0], project_sums, sem_in.at[1])
    in_copies = [pltpu.make_async_copy(grads.at[i], low_rows.at[i], sem_in.at[2 + i]) for i in range(NS)]
    through = [pltpu.make_async_copy(rows.at[i], carried.at[i], sem_in.at[6 + i]) for i in range(NS)]
    weight_copies = [
        pltpu.make_async_copy(weight_sums.at[1], expand_grad, sem_out.at[1]),
        pltpu.make_async_copy(weight_sums.at[2], reduce_grad, sem_out.at[2]),
    ]
    for copy in in_copies + through + weight_copies + [second, first]:
        copy.start()
    out_copies = [pltpu.make_async_copy(wide.at[i], features_grad.at[i], sem_out.at[3 + i]) for i in range(NS)]
    out_copies += [pltpu.make_async_copy(carried.at[i], out.at[i], sem_out.at[7 + i]) for i in range(NS)]
    for i in range(NS):
        in_copies[i].wait()
        wide[i] = low_rows[i].astype(F32)
        out_copies[i].start()
    for i in range(NS):
        through[i].wait()
        out_copies[NS + i].start()
    second.wait()
    for piece in range(3):
        project_grad[piece] = project_sums[:, piece * SEC : (piece + 1) * SEC]
    merge_grad[...] = project_sums[:, 3 * SEC :].T
    first.wait()
    gain1_grad[...] = small[0]
    shift1_grad[...] = small[1]
    gain2_grad[...] = small[2]
    shift2_grad[...] = small[3]
    merge_bias_grad[...] = small[4]
    reduce_bias_grad[...] = small[5]
    for s in range(NS):
        expand_bias_grad[s * D : (s + 1) * D] = small[6 + s]
        project_bias_grad[0:1, s * SEC : (s + 1) * SEC] = small[10 + s : 11 + s, 0:SEC]
        project_bias_grad[1:2, s * SEC : (s + 1) * SEC] = small[10 + s : 11 + s, 2 * SEC : 3 * SEC]
    for copy in weight_copies + out_copies:
        copy.wait()


def block(features, packing, segment_ids, norm1_gain, norm1_shift, project_weight, project_bias, merge_weight, merge_bias,
          norm2_gain, norm2_shift, expand_weight, expand_bias, reduce_weight, reduce_bias, cotangent):
    vmem = pl.BlockSpec(memory_space=pltpu.VMEM)
    anywhere = pl.BlockSpec(memory_space=pl.ANY)
    shape = jax.ShapeDtypeStruct
    inner = pl.pallas_call(
        block_kernel,
        name="block",
        in_specs=[anywhere] + [vmem] * 14 + [anywhere],
        out_specs=[anywhere, anywhere, vmem, vmem],
        out_shape=[
            shape((NS, CHUNK, D), BF16),
            shape((NS, CHUNK, D), BF16),
            shape((3, ROWS, D), F32),
            shape((16, D), F32),
        ],
        scratch_shapes=[
            pltpu.VMEM((3, NS, 4, 2, ROWS, D), BF16),
            pltpu.VMEM((3, NS, 4, 2, ROWS, D), BF16),
            pltpu.VMEM((2, NS, 4, ROWS, D), BF16),
            pltpu.VMEM((2, NS, 2, HALF, D), BF16),
            pltpu.VMEM((2, NS, 2, ROWS, D), BF16),
            pltpu.VMEM((3, 2, ROWS, D), BF16),
            pltpu.VMEM((3, 2, ROWS, D), BF16),
            pltpu.VMEM((NS, CHUNK, D), BF16),
            pltpu.VMEM((NS, CHUNK, D), BF16),
            pltpu.VMEM((D, TOK), BF16),
            pltpu.VMEM((TOK, D), BF16),
            pltpu.VMEM((D, TOK), BF16),
            pltpu.VMEM((NS, CHUNK, D), BF16),
            pltpu.VMEM((D, TOK), BF16),
            pltpu.VMEM((NS, TOK, 640), BF16),
            pltpu.VMEM((NS, TOK, 256), BF16),
            pltpu.VMEM((TOK, D), F32),
            pltpu.VMEM((TOK, D), F32),
            pltpu.VMEM((TOK, D), F32),
            pltpu.VMEM((TOK, D), BF16),
            pltpu.VMEM((TOK, D), BF16),
            pltpu.VMEM((TOK, TOK), F32),
            pltpu.VMEM((16, 1, TOK), F32),
            pltpu.VMEM((NS, 1, D), F32),
            pltpu.VMEM((NS, 1, D), F32),
            pltpu.VMEM((7, 16, D), F32),
            pltpu.VMEM((NS, CHUNK, D), BF16),
            pltpu.VMEM((ROWS, D), F32),
            pltpu.SemaphoreType.DMA((2, 3, NS)),
            pltpu.SemaphoreType.DMA((3, NS)),
            pltpu.SemaphoreType.DMA((5, 3, NS)),
            pltpu.SemaphoreType.DMA((5, 3, NS)),
            pltpu.SemaphoreType.DMA((5, 3, NS)),
            pltpu.SemaphoreType.DMA((5, 3, NS)),
            pltpu.SemaphoreType.DMA((3, NS)),
            pltpu.SemaphoreType.DMA((3, 2)),
            pltpu.SemaphoreType.DMA((3, 2)),
            pltpu.SemaphoreType.DMA((2, NS)),
            pltpu.SemaphoreType.DMA((2, NS)),
            pltpu.SemaphoreType.DMA((2, NS)),
            pltpu.SemaphoreType.DMA((2, NS)),
            pltpu.SemaphoreType.DMA((7,)),
            pltpu.SemaphoreType.DMA((7,)),
            pltpu.SemaphoreType.DMA((4,)),
            pltpu.SemaphoreType.REGULAR((3, NS)),
        ],
        compiler_params=pltpu.CompilerParams(collective_id=0, has_side_effects=True, vmem_limit_bytes=66 * 1000 * 1000),
    )(
        features, packing, segment_ids, norm1_gain, norm1_shift, project_weight, project_bias, merge_weight, merge_bias,
        norm2_gain, norm2_shift, expand_weight, expand_bias, reduce_weight.T, reduce_bias, cotangent,
    )
    results = pl.pallas_call(
        finish_kernel,
        name="finish",
        in_specs=[anywhere] * 4,
        out_specs=[anywhere] * 2 + [vmem] * 12,
        out_shape=[
            shape((NS, CHUNK, D), BF16),
            shape((NS, CHUNK, D), F32),
            shape((D,), F32),
            shape((D,), F32),
            shape((3, ROWS, SEC), F32),
            shape((2, D), F32),
            shape((SEC, ROWS), F32),
            shape((D,), F32),
            shape((D,), F32),
            shape((D,), F32),
            shape((ROWS, D), F32),
            shape((4 * D,), F32),
            shape((ROWS, D), F32),
            shape((D,), F32),
        ],
        scratch_shapes=[
            pltpu.VMEM((NS, CHUNK, D), BF16),
            pltpu.VMEM((NS, CHUNK, D), F32),
            pltpu.VMEM((NS, CHUNK, D), BF16),
            pltpu.VMEM((ROWS, D), F32),
            pltpu.VMEM((16, D), F32),
            pltpu.SemaphoreType.DMA((10,)),
            pltpu.SemaphoreType.DMA((11,)),
        ],
        compiler_params=pltpu.CompilerParams(vmem_limit_bytes=63 * 1000 * 1000),
    )(*inner)
    return tuple(results[:12]) + (results[12].T, results[13])


def norm_rows(values, gain, shift):
    center = values - jnp.mean(values, axis=-1, keepdims=True)
    spread = jnp.mean(center * center, axis=-1, keepdims=True)
    return center * lax.rsqrt(spread + EPSILON) * gain + shift


def exact_gelu(values):
    return jax.nn.gelu(values, approximate=False)


def swap_rows(values):
    return lax.all_to_all(values, "section", split_axis=0, concat_axis=1, tiled=True)[0]


def swap_back(values):
    return lax.all_to_all(values[None], "section", split_axis=1, concat_axis=0, tiled=True)


def whole(values, dp_axis, section_axis):
    values = lax.all_gather(values, "dp", axis=dp_axis, tiled=True)
    return lax.all_gather(values, "section", axis=section_axis, tiled=True)


def shard(values, dp_axis, section_axis):
    values = lax.psum_scatter(values, "section", scatter_dimension=section_axis, tiled=True)
    return lax.psum_scatter(values, "dp", scatter_dimension=dp_axis, tiled=True)


def body(
    features,
    packing,
    segment_ids,
    norm1_gain,
    norm1_shift,
    project_weight,
    project_bias,
    merge_weight,
    merge_bias,
    norm2_gain,
    norm2_shift,
    expand_weight,
    expand_bias,
    reduce_weight,
    reduce_bias,
    cotangent,
):
    length = packing.shape[2]
    width = features.shape[2]
    heads = width // HEAD_DIM
    scale = HEAD_DIM ** (-0.5)
    mine = lax.axis_index("section")
    order = lax.dynamic_index_in_dim(packing[:, 0], mine, 0, keepdims=False)
    packed_labels = lax.dynamic_index_in_dim(segment_ids[:, 0], mine, 0, keepdims=False)
    labels = jnp.zeros((length,), jnp.int32).at[order].set(packed_labels)
    allowed = labels[:, None] == labels[None, :]

    tokens = swap_rows(features).astype(F32)
    upstream = swap_rows(cotangent)
    project = whole(project_weight, 1, 2)
    merge = whole(merge_weight, 1, 0)
    expand = whole(expand_weight, 0, 1)
    reduce = whole(reduce_weight, 1, 0)

    normed = norm_rows(tokens, norm1_gain, norm1_shift).astype(BF16)
    projected = jnp.einsum("td,cde->cte", normed, project, preferred_element_type=F32)
    queries = (projected[0] + project_bias[0]).astype(BF16).reshape(length, heads, HEAD_DIM)
    keys = projected[1].astype(BF16).reshape(length, heads, HEAD_DIM)
    values = (projected[2] + project_bias[1]).astype(BF16).reshape(length, heads, HEAD_DIM)
    scores = jnp.einsum("qhd,khd->hqk", queries, keys, preferred_element_type=F32) * scale
    scores = jnp.where(allowed[None], scores, MASKED)
    peak = jnp.max(scores, axis=-1, keepdims=True)
    weights = jnp.exp(scores - peak)
    probs = weights / jnp.sum(weights, axis=-1, keepdims=True)
    low_probs = probs.astype(BF16)
    mixed = jnp.einsum("hqk,khd->qhd", low_probs, values, preferred_element_type=F32)
    mixed = mixed.reshape(length, width).astype(BF16)
    middle = tokens + (jnp.dot(mixed, merge, preferred_element_type=F32) + merge_bias)
    normed_two = norm_rows(middle, norm2_gain, norm2_shift).astype(BF16)
    hidden = jnp.dot(normed_two, expand, preferred_element_type=F32) + expand_bias
    active = exact_gelu(hidden).astype(BF16)
    second = jnp.dot(active, reduce, preferred_element_type=F32)
    output = swap_back((middle + (second + reduce_bias)).astype(BF16))

    wide_upstream = upstream.astype(F32)
    reduce_bias_grad = jnp.sum(wide_upstream, axis=0)
    reduce_grad = jnp.einsum("tf,td->fd", active, upstream, preferred_element_type=F32)
    grad_active = jnp.einsum("td,fd->tf", upstream, reduce, preferred_element_type=F32)
    _, gelu_back = jax.vjp(exact_gelu, hidden)
    grad_hidden = gelu_back(grad_active)[0].astype(BF16)
    expand_bias_grad = jnp.sum(grad_hidden.astype(F32), axis=0)
    expand_grad = jnp.einsum("td,tf->df", normed_two, grad_hidden, preferred_element_type=F32)
    grad_normed_two = jnp.einsum("tf,df->td", grad_hidden, expand, preferred_element_type=F32)
    _, norm_back = jax.vjp(norm_rows, middle, norm2_gain, norm2_shift)
    grad_from_norm, gain_two, shift_two = norm_back(grad_normed_two)
    grad_middle = wide_upstream + grad_from_norm
    grad_branch = grad_middle.astype(BF16)
    merge_bias_grad = jnp.sum(grad_branch.astype(F32), axis=0)
    merge_grad = jnp.einsum("te,td->ed", mixed, grad_branch, preferred_element_type=F32)
    grad_mixed = jnp.einsum("td,ed->te", grad_branch, merge, preferred_element_type=F32)
    grad_mixed = grad_mixed.astype(BF16).reshape(length, heads, HEAD_DIM)
    grad_probs = jnp.einsum("qhd,khd->hqk", grad_mixed, values, preferred_element_type=F32)
    inner = jnp.sum(probs * grad_probs, axis=-1, keepdims=True)
    grad_scores = (probs * (grad_probs - inner)).astype(BF16)
    grad_queries = jnp.einsum("hqk,khd->qhd", grad_scores, keys, preferred_element_type=F32) * scale
    grad_keys = jnp.einsum("hqk,qhd->khd", grad_scores, queries, preferred_element_type=F32) * scale
    grad_values = jnp.einsum("hqk,qhd->khd", low_probs, grad_mixed, preferred_element_type=F32)
    stacked = jnp.stack([grad_queries, grad_keys, grad_values])
    stacked = stacked.reshape(3, length, width).astype(BF16)
    wide = stacked.astype(F32)
    project_bias_grad = jnp.stack([jnp.sum(wide[0], axis=0), jnp.sum(wide[2], axis=0)])
    project_grad = jnp.einsum("td,cte->cde", normed, stacked, preferred_element_type=F32)
    grad_normed = jnp.einsum("cte,cde->td", stacked, project, preferred_element_type=F32)
    _, first_back = jax.vjp(norm_rows, tokens, norm1_gain, norm1_shift)
    grad_tokens, gain_one, shift_one = first_back(grad_normed)
    features_grad = swap_back(grad_middle + grad_tokens)

    summed = lax.psum(
        (
            gain_one,
            shift_one,
            project_bias_grad,
            merge_bias_grad,
            gain_two,
            shift_two,
            expand_bias_grad,
            reduce_bias_grad,
        ),
        ("dp", "section"),
    )
    return (
        output,
        features_grad,
        summed[0],
        summed[1],
        shard(project_grad, 1, 2),
        summed[2],
        shard(merge_grad, 1, 0),
        summed[3],
        summed[4],
        summed[5],
        shard(expand_grad, 0, 1),
        summed[6],
        shard(reduce_grad, 1, 0),
        summed[7],
    )


def solution(mesh):
    rows = P(None, ("dp", "section"), None)
    groups = P(None, "dp", None)
    project = P(None, "dp", "section")
    inward = P("section", "dp")
    outward = P("dp", "section")
    in_specs = (rows, groups, groups, P(), P(), project, P(), inward, P(), P(), P(), outward, P(), inward, P(), rows)
    out_specs = (rows, rows, P(), P(), project, P(), inward, P(), P(), P(), outward, P(), inward, P())
    fits = mesh.shape["dp"] == 8 and mesh.shape["section"] == NS
    return jax.shard_map(block if fits else body, mesh=mesh, in_specs=in_specs, out_specs=out_specs, check_vma=False)
```

```python
import functools

import jax
import jax.numpy as jnp
from jax import lax
from jax.experimental import pallas as pl
from jax.experimental.pallas import tpu as pltpu
from jax.sharding import PartitionSpec as P

HEAD_DIM = 64
EPSILON = 1e-06
MASKED = -1000000000.0
F32 = jnp.float32
BF16 = jnp.bfloat16
MESH_ID = pl.DeviceIdType.MESH

NS = 4
D = 768
TOK = 512
ROWS = 96
HALF = 48
SEC = 192
NT_DIMS = (((1,), (1,)), ((), ()))
TN_DIMS = (((0,), (0,)), ((), ()))
CORE, XOWN, YOWN, XFWD, YFWD = range(5)
CHUNK = 128

def norm_stats(values):
    center = values - jnp.mean(values, axis=-1, keepdims=True)
    spread = jnp.mean(center * center, axis=-1, keepdims=True)
    scale = lax.rsqrt(spread + EPSILON)
    return center * scale, scale


def norm_grad(normal, scale, grad, gain):
    scaled = grad * gain
    first = jnp.mean(scaled, axis=-1, keepdims=True)
    second = jnp.mean(scaled * normal, axis=-1, keepdims=True)
    return scale * (scaled - first - normal * second)


def dot(left, right, dims=(((1,), (0,)), ((), ()))):
    return lax.dot_general(left, right, dims, preferred_element_type=F32)


def row(values):
    return values[...].reshape(1, D)


def column_sum(values):
    return jnp.sum(values, axis=0, keepdims=True)


def block_kernel(
    features, packing_in, segments_in, gain1_in, shift1_in, project_in, project_bias_in, merge_in,
    merge_bias_in, gain2_in, shift2_in, expand_in, expand_bias_in, reduce_in, reduce_bias_in, cotangent,
    out, FR, weight_sums, SG,
    W, G, RC, RD, RE, RZ, RY, X, U, UT, N1, N1T, N2, N2T, QA, AT, MID, ACC1, ACC2, AC, GH, MASK, LSE, PB, EB, SGR, FS, TB,
    z_send, z_recv, g_send, g_recv, r_send, r_recv, rz_send, rz_recv, ry_recv, in_send, in_recv, out_send, out_recv,
    sg_send, sg_recv, local_sem, credit,
    packing, segments, gain1, shift1, project, project_bias, merge, merge_bias, gain2,
    shift2, expand, expand_bias, reduce, reduce_bias, arg_sem,
):
    dp = lax.axis_index("dp")
    z = lax.axis_index("section")
    c = dp % 2
    k = dp // 2
    xi = k % 2
    yi = k // 2
    kx = 2 * yi + (1 - xi)
    ky = 2 * (1 - yi) + xi
    kd = 3 - k
    x_dev = {"dp": 2 * kx + c, "section": z}
    y_dev = {"dp": 2 * ky + c, "section": z}
    c_dev = {"dp": 2 * k + (1 - c), "section": z}

    def z_dev(other):
        return {"dp": dp, "section": other}

    half = z // 2
    inner = ((z + 1) // 2) % 2 == 1
    outer = ((z + 1) // 2) % 2 == 0
    pair = z + 1 - 2 * (z % 2)
    start = (1 - half) * (z % 2) + half * (1 - z % 2)

    def s_of(t):
        base = (t // 2) * t + (1 - t // 2) * ((start + t) % 2)
        return half * 3 + (1 - 2 * half) * base

    def remote(src, dst, send, recv, device):
        return pltpu.make_async_remote_copy(
            src_ref=src, dst_ref=dst, send_sem=send, recv_sem=recv, device_id=device, device_id_type=MESH_ID
        )

    barrier = pltpu.get_barrier_semaphore()
    for device in (x_dev, y_dev, c_dev):
        pl.semaphore_signal(barrier, inc=1, device_id=device, device_id_type=MESH_ID)
    for step in range(1, NS):
        pl.semaphore_signal(barrier, inc=1, device_id=z_dev((z + step) % NS), device_id_type=MESH_ID)

    arguments = (
        (packing_in, packing),
        (segments_in, segments),
        (gain1_in, gain1),
        (shift1_in, shift1),
        (project_in, project),
        (project_bias_in, project_bias),
        (merge_in, merge),
        (merge_bias_in, merge_bias),
        (gain2_in, gain2),
        (shift2_in, shift2),
        (expand_in, expand),
        (expand_bias_in, expand_bias),
        (reduce_in, reduce),
        (reduce_bias_in, reduce_bias),
    )
    for i, (source, target) in enumerate(arguments):
        pltpu.make_async_copy(source, target, arg_sem.at[i]).start()
    for i, (source, target) in enumerate(arguments):
        pltpu.make_async_copy(source, target, arg_sem.at[i]).wait()

    for piece in range(3):
        TB[:, piece * SEC : (piece + 1) * SEC] = project[piece].astype(F32)
    TB[:, 3 * SEC :] = merge[...].astype(F32).T
    W[0, pl.ds(z, 1), pl.ds(k, 1), pl.ds(c, 1)] = TB[...].astype(BF16)[None, None, None]
    W[1, pl.ds(z, 1), pl.ds(k, 1), pl.ds(c, 1)] = expand[...][None, None, None]
    W[2, pl.ds(z, 1), pl.ds(k, 1), pl.ds(c, 1)] = reduce[...][None, None, None]
    pl.semaphore_wait(barrier, 6)

    def z_copy(m, s, up):
        place = W.at[m, s, k, c]
        return remote(place, place, z_send.at[up], z_recv.at[m, s], z_dev(z + 2 * up - 1))

    def z_pass(m, s):
        @pl.when((s <= z) & (z < NS - 1))
        def _():
            z_copy(m, s, 1).start()

        @pl.when((s >= z) & (z > 0))
        def _():
            z_copy(m, s, 0).start()

    def plane_copy(kind, m, s, receive=False):
        rows = slice(None)
        if kind == CORE:
            place = W.at[m, s, :, (1 - c) if receive else c]
            return remote(place, place, g_send.at[kind], g_recv.at[kind, m, s], c_dev)
        if kind == XOWN:
            place = W.at[m, s, kx if receive else k, c]
            return remote(place, place, g_send.at[kind], g_recv.at[kind, m, s], x_dev)
        if kind == YOWN:
            place = W.at[m, s, ky if receive else k, c]
            return remote(place, place, g_send.at[kind], g_recv.at[kind, m, s], y_dev)
        if kind == XFWD:
            place = W.at[m, s, kd if receive else ky, c, pl.ds(0, HALF)]
            return remote(place, place, g_send.at[kind], g_recv.at[kind, m, s], x_dev)
        place = W.at[m, s, kd if receive else kx, c, pl.ds(HALF, HALF)]
        return remote(place, place, g_send.at[kind], g_recv.at[kind, m, s], y_dev)

    def guard(condition, action):
        if isinstance(condition, bool):
            if condition:
                action()
        else:
            pl.when(condition)(action)

    def place_of(i):
        if isinstance(i, int) and i < 3:
            return i, 0
        late = i // 6
        return late * (1 + i % 2), late * (i // 2 - 2) + (1 - late) * (i - 2)

    def gather_a(i):
        def action():
            m, t = place_of(i)
            s = s_of(t)
            if not isinstance(i, int) or i > 2:
                z_copy(m, s, 0).wait_recv()
                z_pass(m, s)
            plane_copy(XOWN, m, s).start()
            plane_copy(YOWN, m, s).start()

        guard(i <= 11, action)

    def gather_b(i):
        def action():
            m, t = place_of(i)
            s = s_of(t)
            plane_copy(YOWN, m, s, True).wait_recv()
            plane_copy(XFWD, m, s).start()
            plane_copy(XOWN, m, s, True).wait_recv()
            plane_copy(YFWD, m, s).start()

        guard(i <= 11, action)

    def gather_c(i):
        def action():
            m, t = place_of(i)
            s = s_of(t)
            plane_copy(XFWD, m, s, True).wait_recv()
            plane_copy(YFWD, m, s, True).wait_recv()
            plane_copy(CORE, m, s).start()

        guard(i <= 11, action)

    def gather_d(m, t):
        plane_copy(CORE, m, s_of(t), True).wait_recv()

    def pump(i):
        gather_a(i + 3)
        gather_b(i + 1)
        gather_c(i)

    def rs_core(m, s, at, receive=False):
        place = RC.at[m % 2, at]
        source = place if receive else G.at[m, s, :, 1 - c]
        return remote(source, place, r_send.at[CORE], r_recv.at[CORE, m, s], c_dev)

    def rs_diag(kind, m, s, at):
        which, device = (0, x_dev) if kind == XFWD else (1, y_dev)
        return remote(
            G.at[m, s, kd, c, pl.ds(which * HALF, HALF)], RD.at[m % 2, at, which],
            r_send.at[kind], r_recv.at[kind, m, s], device,
        )

    def rs_side(kind, m, s, at):
        which, device, block = (0, x_dev, kx) if kind == XOWN else (1, y_dev, ky)
        return remote(
            G.at[m, s, block, c], RE.at[m % 2, at, which], r_send.at[kind], r_recv.at[kind, m, s], device
        )

    def rs_near(m, s):
        near = s // 2 == z // 2
        place = G.at[m, s, k, c]

        @pl.when(near)
        def _():
            remote(place, RZ.at[m, 0], rz_send.at[0], rz_recv.at[m, 0], z_dev(pair)).start()

        @pl.when(jnp.logical_not(near) & outer)
        def _():
            remote(place, RY.at[m, s % 2], rz_send.at[0], ry_recv.at[m, s % 2], z_dev(pair)).start()

    def rs_far(m, s):
        @pl.when((s // 2 != z // 2) & inner)
        def _():
            place = G.at[m, s, k, c]
            buffer = RY.at[m, s % 2]
            remote(buffer, buffer, rz_send.at[0], ry_recv.at[m, s % 2], z_dev(pair)).wait_recv()
            add_into(place, buffer)
            remote(place, RZ.at[m, 1], rz_send.at[0], rz_recv.at[m, 1], z_dev(s)).start()

    def add_into(place, other):
        place[...] = place[...] + other[...]

    def scatter_place(r):
        if r < 8:
            return 2 - r % 2, s_of(r // 2), s_of(r // 2)
        return 0, s_of(11 - r), s_of(r - 8)

    def credit_give(at):
        for device, which in ((c_dev, 0), (x_dev, 1), (y_dev, 2)):
            pl.semaphore_signal(credit.at[which, at], inc=1, device_id=device, device_id_type=MESH_ID)

    def credit_take(at):
        for which in range(3):
            pl.semaphore_wait(credit.at[which, at], 1)

    def scatter_p(m, s, at):
        rs_core(m, s, at).start()

    def scatter_q(r):
        m, s, at = scatter_place(r)
        rs_core(m, s, at, True).wait_recv()
        for block in range(4):
            add_into(G.at[m, s, block, c], RC.at[m % 2, at, block])
        rs_diag(XFWD, m, s, at).start()
        rs_diag(YFWD, m, s, at).start()

    def scatter_r(r):
        m, s, at = scatter_place(r)
        rs_diag(XFWD, m, s, at).wait_recv()
        add_into(G.at[m, s, ky, c, pl.ds(0, HALF)], RD.at[m % 2, at, 0])
        rs_side(YOWN, m, s, at).start()
        rs_diag(YFWD, m, s, at).wait_recv()
        add_into(G.at[m, s, kx, c, pl.ds(HALF, HALF)], RD.at[m % 2, at, 1])
        rs_side(XOWN, m, s, at).start()

    def scatter_t(r):
        m, s, at = scatter_place(r)
        rs_side(XOWN, m, s, at).wait_recv()
        rs_side(YOWN, m, s, at).wait_recv()
        place = G.at[m, s, k, c]
        total = RE[m % 2, at, 0].astype(F32) + RE[m % 2, at, 1].astype(F32)
        place[...] = (place[...].astype(F32) + total).astype(BF16)
        if r in (0, 2, 4, 6):
            credit_give(r // 2)
        pl.when(s != z)(lambda: rs_near(m, s))

    def scatter_z(r):
        m, s, _ = scatter_place(r)
        rs_far(m, s)

    def scatter_sum(m):
        total = G[m, z, k, c].astype(F32)
        for which in range(2):
            remote(RZ.at[m, which], RZ.at[m, which], rz_send.at[0], rz_recv.at[m, which], z_dev(pair)).wait_recv()
            total = total + RZ[m, which].astype(F32)
        return total

    def row_copy(which, source, target, there):
        return remote(source.at[there], target.at[z], in_send.at[which, there], in_recv.at[which, z], z_dev(there))

    def row_send(which, source, target, t):
        row_copy(which, source, target, s_of(t)).start()

    def rows_wait(which, source, target, t):
        origin = s_of(t)
        if t == 0:
            pltpu.make_async_copy(source.at[z], target.at[z], local_sem.at[which]).wait()
        else:
            remote(
                source.at[origin], target.at[origin], in_send.at[which, origin], in_recv.at[which, origin], z_dev(origin)
            ).wait_recv()
        return origin

    def back_send(which, source, target, there):
        remote(source.at[there], target.at[z], out_send.at[which, there], out_recv.at[which, z], z_dev(there)).start()

    def back_keep(which, source, target):
        pltpu.make_async_copy(source.at[z], target.at[z], local_sem.at[2 + which]).start()

    def back_wait(which, source, target):
        for step in range(1, NS):
            other = (z + step) % NS
            remote(
                source.at[other], target.at[other], out_send.at[which, other], out_recv.at[which, other], z_dev(other)
            ).wait()
        pltpu.make_async_copy(source.at[z], target.at[z], local_sem.at[2 + which]).wait()

    def sum_z(step):
        other = (z + step) % NS
        return remote(SG, SGR.at[z], sg_send.at[step], sg_recv.at[z], z_dev(other))

    def sum_z_wait():
        for step in range(1, NS):
            origin = (z + step) % NS
            remote(SGR.at[origin], SGR.at[origin], sg_send.at[step], sg_recv.at[origin], z_dev(origin)).wait_recv()
            sum_z(step).wait_send()
        SGR[pl.ds(z, 1)] = SG[...][None]
        SG[...] = (SGR[0] + SGR[1]) + (SGR[2] + SGR[3])

    def sum_copy(step, device):
        return remote(SG, SGR.at[step], sg_send.at[step], sg_recv.at[step], device)

    def sum_end(step, device):
        sum_copy(step, device).wait()
        SG[...] = SG[...] + SGR[step]

    def z_near(m):
        z_copy(m, z, 1 - z % 2).start()

    def z_far(m):
        z_copy(m, z, z % 2).start()

    for which, source, target in ((0, features, X), (1, cotangent, U)):
        pltpu.make_async_copy(source.at[z], target.at[z], local_sem.at[which]).start()

    @pl.when(inner)
    def _():
        z_near(1)
        z_far(1)
        z_far(0)
        row_send(1, cotangent, U, 1)
        gather_a(0)
        z_far(2)
        z_near(0)
        gather_a(2)
        gather_a(1)
        gather_a(3)
        z_near(2)
        gather_b(2)
        gather_a(4)
        row_send(0, features, X, 2)
        gather_b(0)
        gather_a(5)
        gather_c(0)
        row_send(0, features, X, 3)
        gather_b(3)
        row_send(0, features, X, 1)
        gather_b(4)
        gather_b(1)

    @pl.when(outer)
    def _():
        z_near(0)
        gather_a(0)
        gather_a(2)
        row_send(1, cotangent, U, 1)
        gather_b(0)
        gather_a(1)
        z_near(2)
        gather_a(6)
        row_send(0, features, X, 2)
        row_send(0, features, X, 1)
        z_near(1)
        gather_c(0)
        gather_b(6)
        gather_a(3)
        gather_a(7)
        gather_a(4)
        row_send(0, features, X, 3)

    order = packing[z]
    labels = segments[z].astype(F32)
    token = lax.broadcasted_iota(jnp.int32, (TOK, TOK), 0)
    token_labels = jnp.sum(jnp.where(token == order, labels, 0.0), axis=1, keepdims=True)
    kinds = lax.broadcasted_iota(jnp.int32, (TOK, 128), 1).astype(F32)
    one_hot = jnp.where(token_labels == kinds, 1.0, 0.0).astype(BF16)
    MASK[...] = (dot(one_hot, one_hot, NT_DIMS) - 1.0) * -MASKED
    AT[:, :, 0:64] = jnp.zeros((NS, TOK, 64), BF16)
    SG[...] = jnp.zeros_like(SG)
    PB[...] = jnp.zeros_like(PB)
    for s in range(NS):
        EB[s] = expand_bias[s * D : (s + 1) * D].reshape(1, D)
        PB[s, :, 0:SEC] = project_bias[0:1, s * SEC : (s + 1) * SEC]
        PB[s, :, 2 * SEC : 3 * SEC] = project_bias[1:2, s * SEC : (s + 1) * SEC]

    @pl.when(inner)
    def _():
        gather_a(7)
        gather_c(3)

    @pl.when(outer)
    def _():
        gather_b(2)
        gather_a(5)
        gather_b(3)
        gather_b(4)
        gather_b(1)

    for t in range(NS):
        i = rows_wait(0, features, X, t)
        rows = pl.ds(pl.multiple_of(i * CHUNK, CHUNK), CHUNK)
        normal, _ = norm_stats(X[i].astype(F32))
        normed = normal * row(gain1) + row(shift1)
        N1[rows, :] = normed.astype(BF16)
        N1T[:, rows] = normed.T.astype(BF16)

    def weight(m, s):
        return W[m, s].reshape(D, D)

    def weight_tile(m, s, n):
        return W[m, s, :, :, :, pl.ds(pl.multiple_of(n * 256, 256), 256)].reshape(D, 256)

    def weight_end(s):
        return W[0, s, :, :, :, 512:768].reshape(D, 256)

    def attend(s, between):
        for first, last in ((0, 256), (256, 512), (512, 640)):
            part = dot(N1[...], W[0, s, :, :, :, first:last].reshape(D, last - first))
            QA[s, :, first:last] = (part + PB[s, :, first:last]).astype(BF16)
        between()
        for j in range(3):
            keys = QA[s, :, SEC + 64 * j : SEC + 64 * j + 64]
            values = QA[s, :, 2 * SEC + 64 * j : 2 * SEC + 64 * j + 64]
            queries = QA[s, :, 64 * j : 64 * j + 64] * 0.125
            scores = dot(keys, queries, NT_DIMS) + MASK[...]
            peak = jnp.max(scores, axis=0, keepdims=True)
            weights = jnp.exp(scores - peak)
            total = jnp.sum(weights, axis=0, keepdims=True)
            LSE[s * 3 + j] = peak + jnp.log(total)
            mixed = dot(values, weights.astype(BF16), TN_DIMS) * (1.0 / total)
            AT[s, :, 64 + 64 * j : 128 + 64 * j] = mixed.T.astype(BF16)
        ACC1[...] += dot(AT[s], weight_end(s), NT_DIMS)

    ACC1[...] = jnp.zeros_like(ACC1)

    @pl.when(outer)
    def _():
        gather_b(5)

    def attend_step(t, carry):

        @pl.when(t == 0)
        def _():

            @pl.when(inner)
            def _():
                gather_a(6)
                gather_c(1)
                gather_a(9)
                gather_c(2)

            @pl.when(outer)
            def _():
                gather_c(3)

        @pl.when(t == 1)
        def _():

            @pl.when(inner)
            def _():
                gather_b(5)

        @pl.when(t == 2)
        def _():

            @pl.when(inner)
            def _():
                row_send(1, cotangent, U, 2)
                gather_c(4)
                gather_a(8)
                gather_b(6)
                gather_a(10)
                gather_b(7)
                gather_c(5)

            @pl.when(outer)
            def _():
                gather_a(9)

        @pl.when(t == 3)
        def _():

            @pl.when(inner)
            def _():
                gather_a(11)
                row_send(1, cotangent, U, 3)

            @pl.when(outer)
            def _():
                gather_a(8)
                gather_c(6)

        gather_d(0, t)

        def between():

            @pl.when(t == 0)
            def _():

                @pl.when(outer)
                def _():
                    row_send(1, cotangent, U, 2)
                    gather_b(7)
                    gather_c(4)

            @pl.when(t == 1)
            def _():

                @pl.when(outer)
                def _():
                    gather_c(2)
                    gather_c(5)

            @pl.when(t == 3)
            def _():

                @pl.when(outer)
                def _():
                    gather_b(9)
                    gather_c(1)

        attend(s_of(t), between)
        return carry

    lax.fori_loop(0, NS, attend_step, 0)


    @pl.when(inner)
    def _():
        gather_c(6)

    @pl.when(outer)
    def _():
        row_send(1, cotangent, U, 3)
        gather_a(10)
        gather_b(8)
        gather_c(7)

    for i in range(NS):
        rows = slice(i * CHUNK, (i + 1) * CHUNK)
        middle = X[i].astype(F32) + (ACC1[rows, :] + row(merge_bias))
        MID[rows, :] = middle
        normal, _ = norm_stats(middle)
        normed = normal * row(gain2) + row(shift2)
        N2[i] = normed.astype(BF16)
        N2T[:, rows] = normed.T.astype(BF16)

    @pl.when(inner)
    def _():
        gather_b(8)

    @pl.when(outer)
    def _():
        gather_a(11)
        gather_c(9)

    for t in range(NS):
        i = rows_wait(1, cotangent, U, t)
        upstream = U[i].astype(F32)
        UT[:, pl.ds(pl.multiple_of(i * CHUNK, CHUNK), CHUNK)] = upstream.T.astype(BF16)
        SG[5:6, :] += column_sum(upstream)
    ACC1[...] = jnp.zeros_like(ACC1)
    ACC2[...] = jnp.zeros_like(ACC2)

    @pl.when(inner)
    def _():
        gather_b(9)

    def feed(s, between):
        def tile_step(n, carry):
            lanes = pl.ds(pl.multiple_of(n * 256, 256), 256)
            hidden = dot(N2[...].reshape(TOK, D), weight_tile(1, s, n)) + EB[s, :, lanes]
            gate = 0.5 + 0.5 * lax.erf(hidden * 0.7071067811865476)
            active = (hidden * gate).astype(BF16)
            AC[:, lanes] = active
            slope = gate + hidden * (jnp.exp(-0.5 * hidden * hidden) * 0.3989422804014327)
            G[2, s, :, :, :, lanes] = dot(UT[...], active).astype(BF16).reshape(4, 2, ROWS, 256)
            grad_active = dot(U[...].reshape(TOK, D), weight_tile(2, s, n))
            grad_hidden = (grad_active * slope).astype(BF16)
            GH[:, lanes] = grad_hidden
            SG[pl.ds(6 + s, 1), lanes] = column_sum(grad_hidden.astype(F32))
            G[1, s, :, :, :, lanes] = dot(N2T[...], grad_hidden).astype(BF16).reshape(4, 2, ROWS, 256)
            return carry

        lax.fori_loop(0, 3, tile_step, 0, unroll=True)
        between()
        ACC1[...] += dot(AC[...], weight(2, s), NT_DIMS)
        ACC2[...] += dot(GH[...], weight(1, s), NT_DIMS)

    def feed_step(t, carry):
        s = s_of(t)

        def before():

            @pl.when(t == 0)
            def _():

                @pl.when(inner)
                def _():
                    gather_c(7)

            @pl.when(t == 1)
            def _():

                @pl.when(inner)
                def _():
                    gather_b(10)
                    gather_b(11)
                    gather_c(9)
                    gather_c(8)

                @pl.when(outer)
                def _():
                    gather_c(8)
                    gather_b(11)
                    gather_b(10)

            @pl.when(t == 2)
            def _():
                scatter_q(0)
                gather_c(11)
                gather_c(10)

            @pl.when(t == 3)
            def _():

                @pl.when(outer)
                def _():
                    scatter_q(2)

        def between():
            scatter_p(2, s, s)
            scatter_p(1, s, s)

            @pl.when(t == 2)
            def _():

                @pl.when(inner)
                def _():
                    scatter_q(2)

                scatter_r(0)

            @pl.when(t == 3)
            def _():

                @pl.when(outer)
                def _():
                    scatter_q(5)

        before()
        gather_d(1, t)
        gather_d(2, t)
        feed(s, between)
        return carry

    lax.fori_loop(0, NS, feed_step, 0)

    for i in range(NS):
        rows = slice(i * CHUNK, (i + 1) * CHUNK)
        FS[i] = (MID[rows, :] + (ACC1[rows, :] + row(reduce_bias))).astype(BF16)
    back_keep(0, FS, out)
    back_send(0, FS, out, s_of(2))

    @pl.when(inner)
    def _():
        scatter_t(0)

    @pl.when(outer)
    def _():
        scatter_r(2)
        scatter_r(5)
        back_send(0, FS, out, s_of(3))
        scatter_t(0)
        scatter_q(4)

    for i in range(NS):
        rows = slice(i * CHUNK, (i + 1) * CHUNK)
        normal, scale = norm_stats(MID[rows, :])
        grad = ACC2[rows, :]
        grad_middle = U[i].astype(F32) + norm_grad(normal, scale, grad, row(gain2))
        SG[2:3, :] += column_sum(grad * normal)
        SG[3:4, :] += column_sum(grad)
        grad_branch = grad_middle.astype(BF16)
        SG[4:5, :] += column_sum(grad_branch.astype(F32))
        MID[rows, :] = grad_middle
        AC[rows, :] = grad_branch
        UT[:, rows] = grad_branch.astype(F32).T.astype(BF16)
    ACC2[...] = jnp.zeros_like(ACC2)

    @pl.when(inner)
    def _():
        back_send(0, FS, out, s_of(1))
        scatter_q(6)

    def attend_back(s, between):
        N1[:, 0:256] = dot(AC[...], weight_end(s)).astype(BF16)
        GH[:, 512:768] = jnp.zeros((TOK, 256), BF16)
        for j in range(3):
            keys = QA[s, :, SEC + 64 * j : SEC + 64 * j + 64]
            values = QA[s, :, 2 * SEC + 64 * j : 2 * SEC + 64 * j + 64]
            queries = QA[s, :, 64 * j : 64 * j + 64] * 0.125
            grad_mixed = N1[:, 64 + 64 * j : 128 + 64 * j]
            scores = dot(keys, queries, NT_DIMS) + MASK[...]
            probs = jnp.exp(scores - LSE[s * 3 + j])
            grad_probs = dot(values, grad_mixed, NT_DIMS)
            inner = jnp.sum(probs * grad_probs, axis=0, keepdims=True)
            grad_scores = (probs * (grad_probs - inner)).astype(BF16)
            grad_queries = dot(keys, grad_scores, TN_DIMS) * 0.125
            GH[:, 64 * j : 64 * j + 64] = grad_queries.T.astype(BF16)
            GH[:, SEC + 64 * j : SEC + 64 * j + 64] = dot(grad_scores, queries).astype(BF16)
            GH[:, 2 * SEC + 64 * j : 2 * SEC + 64 * j + 64] = dot(probs.astype(BF16), grad_mixed).astype(BF16)
        between()
        SG[pl.ds(10 + s, 1), :] = column_sum(GH[...].astype(F32))
        ACC2[...] += dot(GH[...], weight(0, s), NT_DIMS)

    def attend_weight(s):
        for n in range(3):
            lanes = slice(n * 256, n * 256 + 256)
            part = dot(N1T[...], GH[:, lanes])
            if n == 2:
                part += dot(UT[...], AT[s])
            G[0, s, :, :, :, lanes] = part.astype(BF16).reshape(4, 2, ROWS, 256)

    def back_step(t, carry):
        s = s_of(3 - t)

        def before():

            @pl.when(t == 0)
            def _():

                @pl.when(inner)
                def _():
                    scatter_q(4)
                    scatter_r(2)

            @pl.when(t == 1)
            def _():

                @pl.when(inner)
                def _():
                    scatter_r(6)
                    scatter_r(4)

                @pl.when(outer)
                def _():
                    scatter_r(4)
                    scatter_q(6)
                    scatter_t(2)
                    scatter_q(7)

            @pl.when(t == 2)
            def _():

                @pl.when(outer)
                def _():
                    scatter_r(6)
                    scatter_t(5)

            @pl.when(t == 3)
            def _():

                @pl.when(outer)
                def _():
                    scatter_r(7)
                    scatter_t(6)

        def between():

            @pl.when(t == 0)
            def _():

                @pl.when(outer)
                def _():
                    back_send(0, FS, out, s_of(1))

            @pl.when(t == 1)
            def _():

                @pl.when(inner)
                def _():
                    scatter_t(2)

                scatter_q(8)

            @pl.when(t == 2)
            def _():

                @pl.when(inner)
                def _():
                    back_send(0, FS, out, s_of(3))
                    scatter_t(4)
                    scatter_r(8)
                    scatter_t(6)
                    scatter_z(0)

                @pl.when(outer)
                def _():
                    scatter_t(4)
                    scatter_r(8)

            @pl.when(t == 3)
            def _():

                @pl.when(outer)
                def _():
                    scatter_t(8)
                    scatter_q(9)

        before()
        attend_back(s, between)

        @pl.when(t < NS - 1)
        def _():
            attend_weight(s)
            credit_take(t)
            scatter_p(0, s, s_of(t))

        return carry

    lax.fori_loop(0, NS, back_step, 0)


    for step in (2, 1, 3, 0):
        i = (z + step) % NS
        rows = pl.ds(pl.multiple_of(i * CHUNK, CHUNK), CHUNK)
        normal, _ = norm_stats(X[i].astype(F32))
        grad = ACC2[rows, :]
        SG[0:1, :] += column_sum(grad * normal)
        SG[1:2, :] += column_sum(grad)
    for step in range(1, NS):
        sum_z(step).start()
    for step in (2, 1, 3, 0):
        i = (z + step) % NS
        rows = pl.ds(pl.multiple_of(i * CHUNK, CHUNK), CHUNK)
        normal, scale = norm_stats(X[i].astype(F32))
        N2[i] = (MID[rows, :] + norm_grad(normal, scale, ACC2[rows, :], row(gain1))).astype(BF16)
    back_keep(1, N2, FR)

    @pl.when(inner)
    def _():
        scatter_q(5)
        scatter_q(10)
        back_send(1, N2, FR, s_of(2))
        back_send(1, N2, FR, s_of(3))
        scatter_q(7)
        scatter_r(10)
        back_send(1, N2, FR, s_of(1))

    @pl.when(outer)
    def _():
        scatter_q(10)
        back_send(1, N2, FR, s_of(2))
        scatter_t(7)

    attend_weight(z)
    credit_take(3)
    scatter_p(0, z, s_of(3))

    @pl.when(inner)
    def _():
        scatter_z(4)
        scatter_r(5)
        scatter_q(9)
        scatter_z(6)
        scatter_q(3)
        scatter_r(9)
        sum_z_wait()
        scatter_q(11)
        scatter_t(8)
        scatter_t(10)
        scatter_r(3)
        scatter_q(1)
        scatter_r(7)
        sum_copy(4, c_dev).start()
        sum_end(4, c_dev)
        scatter_z(8)
        weight_sums[2] = scatter_sum(2)
        scatter_t(5)
        scatter_r(1)
        scatter_t(7)
        scatter_z(7)
        scatter_r(11)
        scatter_t(1)
        scatter_t(9)
        sum_copy(5, x_dev).start()
        scatter_z(10)
        scatter_z(5)
        scatter_t(3)
        scatter_z(1)
        sum_end(5, x_dev)
        scatter_z(9)
        scatter_t(11)
        sum_copy(6, y_dev).start()
        sum_end(6, y_dev)
        weight_sums[1] = scatter_sum(1)
        scatter_z(3)
        weight_sums[0] = scatter_sum(0)
        scatter_z(2)

    @pl.when(outer)
    def _():
        scatter_q(3)
        back_send(1, N2, FR, s_of(3))
        scatter_r(9)
        scatter_r(10)
        sum_z_wait()
        scatter_q(11)
        scatter_t(9)
        sum_copy(4, c_dev).start()
        scatter_q(1)
        scatter_r(3)
        sum_end(4, c_dev)
        weight_sums[2] = scatter_sum(2)
        scatter_r(11)
        scatter_t(10)
        sum_copy(5, x_dev).start()
        sum_end(5, x_dev)
        sum_copy(6, y_dev).start()
        back_send(1, N2, FR, s_of(1))
        scatter_t(3)
        scatter_r(1)
        scatter_t(11)
        scatter_t(1)
        weight_sums[1] = scatter_sum(1)
        sum_end(6, y_dev)
        weight_sums[0] = scatter_sum(0)

    back_wait(0, FS, out)
    back_wait(1, N2, FR)

    def gone(blocks, send, receive, device):
        remote(blocks, blocks, send, receive, device).wait_send()

    pair_dev = z_dev(pair)

    @pl.when(outer)
    def _():
        gone(W.at[:, 0, k, c], z_send.at[1 - z % 2], z_recv.at[0, 0], pair_dev)

    @pl.when(inner)
    def _():
        gone(W.at[:, 0:3, k, c], z_send.at[1 - z % 2], z_recv.at[0, 0], pair_dev)
        gone(W.at[:, 0:2, k, c], z_send.at[z % 2], z_recv.at[0, 0], z_dev(NS - 1 - z))

    gone(W.at[:, :, :, c], g_send.at[CORE], g_recv.at[CORE, 0, 0], c_dev)
    gone(W.at[:, :, k, c], g_send.at[XOWN], g_recv.at[XOWN, 0, 0], x_dev)
    gone(W.at[:, :, k, c], g_send.at[YOWN], g_recv.at[YOWN, 0, 0], y_dev)
    gone(W.at[:, :, k, c, pl.ds(0, HALF)], g_send.at[XFWD], g_recv.at[XFWD, 0, 0], x_dev)
    gone(W.at[:, :, k, c, pl.ds(0, HALF)], g_send.at[YFWD], g_recv.at[YFWD, 0, 0], y_dev)
    gone(G.at[:, :, :, c], r_send.at[CORE], r_recv.at[CORE, 0, 0], c_dev)
    gone(G.at[:, :, k, c], r_send.at[XOWN], r_recv.at[XOWN, 0, 0], x_dev)
    gone(G.at[:, :, k, c], r_send.at[YOWN], r_recv.at[YOWN, 0, 0], y_dev)
    gone(G.at[:, :, k, c, pl.ds(0, HALF)], r_send.at[XFWD], r_recv.at[XFWD, 0, 0], x_dev)
    gone(G.at[:, :, k, c, pl.ds(0, HALF)], r_send.at[YFWD], r_recv.at[YFWD, 0, 0], y_dev)
    gone(G.at[:, 0:3, k, c], rz_send.at[0], rz_recv.at[0, 0], pair_dev)
    for which, source, target in ((0, features, X), (1, cotangent, U)):
        for step in range(1, NS):
            row_copy(which, source, target, (z + step) % NS).wait_send()


def finish_kernel(
    rows, grads, weight_sums, sums,
    out, features_grad, gain1_grad, shift1_grad, project_grad, project_bias_grad, merge_grad, merge_bias_grad,
    gain2_grad, shift2_grad, expand_grad, expand_bias_grad, reduce_grad, reduce_bias_grad,
    low_rows, wide, carried, project_sums, small, sem_in, sem_out,
):
    first = pltpu.make_async_copy(sums, small, sem_in.at[0])
    second = pltpu.make_async_copy(weight_sums.at[0], project_sums, sem_in.at[1])
    in_copies = [pltpu.make_async_copy(grads.at[i], low_rows.at[i], sem_in.at[2 + i]) for i in range(NS)]
    through = [pltpu.make_async_copy(rows.at[i], carried.at[i], sem_in.at[6 + i]) for i in range(NS)]
    weight_copies = [
        pltpu.make_async_copy(weight_sums.at[1], expand_grad, sem_out.at[1]),
        pltpu.make_async_copy(weight_sums.at[2], reduce_grad, sem_out.at[2]),
    ]
    for copy in in_copies + through + weight_copies + [second, first]:
        copy.start()
    out_copies = [pltpu.make_async_copy(wide.at[i], features_grad.at[i], sem_out.at[3 + i]) for i in range(NS)]
    out_copies += [pltpu.make_async_copy(carried.at[i], out.at[i], sem_out.at[7 + i]) for i in range(NS)]
    for i in range(NS):
        in_copies[i].wait()
        wide[i] = low_rows[i].astype(F32)
        out_copies[i].start()
    for i in range(NS):
        through[i].wait()
        out_copies[NS + i].start()
    second.wait()
    for piece in range(3):
        project_grad[piece] = project_sums[:, piece * SEC : (piece + 1) * SEC]
    merge_grad[...] = project_sums[:, 3 * SEC :].T
    first.wait()
    gain1_grad[...] = small[0]
    shift1_grad[...] = small[1]
    gain2_grad[...] = small[2]
    shift2_grad[...] = small[3]
    merge_bias_grad[...] = small[4]
    reduce_bias_grad[...] = small[5]
    for s in range(NS):
        expand_bias_grad[s * D : (s + 1) * D] = small[6 + s]
        project_bias_grad[0:1, s * SEC : (s + 1) * SEC] = small[10 + s : 11 + s, 0:SEC]
        project_bias_grad[1:2, s * SEC : (s + 1) * SEC] = small[10 + s : 11 + s, 2 * SEC : 3 * SEC]
    for copy in weight_copies + out_copies:
        copy.wait()


def block(features, packing, segment_ids, norm1_gain, norm1_shift, project_weight, project_bias, merge_weight, merge_bias,
          norm2_gain, norm2_shift, expand_weight, expand_bias, reduce_weight, reduce_bias, cotangent):
    vmem = pl.BlockSpec(memory_space=pltpu.VMEM)
    anywhere = pl.BlockSpec(memory_space=pl.ANY)
    shape = jax.ShapeDtypeStruct
    inner = pl.pallas_call(
        block_kernel,
        name="block",
        in_specs=[anywhere] * 16,
        out_specs=[anywhere, anywhere, vmem, vmem],
        out_shape=[
            shape((NS, CHUNK, D), BF16),
            shape((NS, CHUNK, D), BF16),
            shape((3, ROWS, D), F32),
            shape((16, D), F32),
        ],
        scratch_shapes=[
            pltpu.VMEM((3, NS, 4, 2, ROWS, D), BF16),
            pltpu.VMEM((3, NS, 4, 2, ROWS, D), BF16),
            pltpu.VMEM((2, NS, 4, ROWS, D), BF16),
            pltpu.VMEM((2, NS, 2, HALF, D), BF16),
            pltpu.VMEM((2, NS, 2, ROWS, D), BF16),
            pltpu.VMEM((3, 2, ROWS, D), BF16),
            pltpu.VMEM((3, 2, ROWS, D), BF16),
            pltpu.VMEM((NS, CHUNK, D), BF16),
            pltpu.VMEM((NS, CHUNK, D), BF16),
            pltpu.VMEM((D, TOK), BF16),
            pltpu.VMEM((TOK, D), BF16),
            pltpu.VMEM((D, TOK), BF16),
            pltpu.VMEM((NS, CHUNK, D), BF16),
            pltpu.VMEM((D, TOK), BF16),
            pltpu.VMEM((NS, TOK, 640), BF16),
            pltpu.VMEM((NS, TOK, 256), BF16),
            pltpu.VMEM((TOK, D), F32),
            pltpu.VMEM((TOK, D), F32),
            pltpu.VMEM((TOK, D), F32),
            pltpu.VMEM((TOK, D), BF16),
            pltpu.VMEM((TOK, D), BF16),
            pltpu.VMEM((TOK, TOK), F32),
            pltpu.VMEM((16, 1, TOK), F32),
            pltpu.VMEM((NS, 1, D), F32),
            pltpu.VMEM((NS, 1, D), F32),
            pltpu.VMEM((7, 16, D), F32),
            pltpu.VMEM((NS, CHUNK, D), BF16),
            pltpu.VMEM((ROWS, D), F32),
            pltpu.SemaphoreType.DMA((2,)),
            pltpu.SemaphoreType.DMA((3, NS)),
            pltpu.SemaphoreType.DMA((5,)),
            pltpu.SemaphoreType.DMA((5, 3, NS)),
            pltpu.SemaphoreType.DMA((5,)),
            pltpu.SemaphoreType.DMA((5, 3, NS)),
            pltpu.SemaphoreType.DMA((1,)),
            pltpu.SemaphoreType.DMA((3, 2)),
            pltpu.SemaphoreType.DMA((3, 2)),
            pltpu.SemaphoreType.DMA((2, NS)),
            pltpu.SemaphoreType.DMA((2, NS)),
            pltpu.SemaphoreType.DMA((2, NS)),
            pltpu.SemaphoreType.DMA((2, NS)),
            pltpu.SemaphoreType.DMA((7,)),
            pltpu.SemaphoreType.DMA((7,)),
            pltpu.SemaphoreType.DMA((4,)),
            pltpu.SemaphoreType.REGULAR((3, NS)),
            pltpu.VMEM((NS, 1, TOK), jnp.int32),
            pltpu.VMEM((NS, 1, TOK), jnp.int32),
            pltpu.VMEM((D,), F32),
            pltpu.VMEM((D,), F32),
            pltpu.VMEM((3, ROWS, SEC), BF16),
            pltpu.VMEM((2, D), F32),
            pltpu.VMEM((SEC, ROWS), BF16),
            pltpu.VMEM((D,), F32),
            pltpu.VMEM((D,), F32),
            pltpu.VMEM((D,), F32),
            pltpu.VMEM((ROWS, D), BF16),
            pltpu.VMEM((4 * D,), F32),
            pltpu.VMEM((ROWS, D), BF16),
            pltpu.VMEM((D,), F32),
            pltpu.SemaphoreType.DMA((14,)),
        ],
        compiler_params=pltpu.CompilerParams(collective_id=0, has_side_effects=True, vmem_limit_bytes=66 * 1000 * 1000),
    )(
        features, packing, segment_ids, norm1_gain, norm1_shift, project_weight, project_bias, merge_weight, merge_bias,
        norm2_gain, norm2_shift, expand_weight, expand_bias, reduce_weight.T, reduce_bias, cotangent,
    )
    results = pl.pallas_call(
        finish_kernel,
        name="finish",
        in_specs=[anywhere] * 4,
        out_specs=[anywhere] * 2 + [vmem] * 12,
        out_shape=[
            shape((NS, CHUNK, D), BF16),
            shape((NS, CHUNK, D), F32),
            shape((D,), F32),
            shape((D,), F32),
            shape((3, ROWS, SEC), F32),
            shape((2, D), F32),
            shape((SEC, ROWS), F32),
            shape((D,), F32),
            shape((D,), F32),
            shape((D,), F32),
            shape((ROWS, D), F32),
            shape((4 * D,), F32),
            shape((ROWS, D), F32),
            shape((D,), F32),
        ],
        scratch_shapes=[
            pltpu.VMEM((NS, CHUNK, D), BF16),
            pltpu.VMEM((NS, CHUNK, D), F32),
            pltpu.VMEM((NS, CHUNK, D), BF16),
            pltpu.VMEM((ROWS, D), F32),
            pltpu.VMEM((16, D), F32),
            pltpu.SemaphoreType.DMA((10,)),
            pltpu.SemaphoreType.DMA((11,)),
        ],
        compiler_params=pltpu.CompilerParams(vmem_limit_bytes=63 * 1000 * 1000),
    )(*inner)
    return tuple(results[:12]) + (results[12].T, results[13])


def norm_rows(values, gain, shift):
    center = values - jnp.mean(values, axis=-1, keepdims=True)
    spread = jnp.mean(center * center, axis=-1, keepdims=True)
    return center * lax.rsqrt(spread + EPSILON) * gain + shift


def exact_gelu(values):
    return jax.nn.gelu(values, approximate=False)


def swap_rows(values):
    return lax.all_to_all(values, "section", split_axis=0, concat_axis=1, tiled=True)[0]


def swap_back(values):
    return lax.all_to_all(values[None], "section", split_axis=1, concat_axis=0, tiled=True)


def whole(values, dp_axis, section_axis):
    values = lax.all_gather(values, "dp", axis=dp_axis, tiled=True)
    return lax.all_gather(values, "section", axis=section_axis, tiled=True)


def shard(values, dp_axis, section_axis):
    values = lax.psum_scatter(values, "section", scatter_dimension=section_axis, tiled=True)
    return lax.psum_scatter(values, "dp", scatter_dimension=dp_axis, tiled=True)


def body(
    features,
    packing,
    segment_ids,
    norm1_gain,
    norm1_shift,
    project_weight,
    project_bias,
    merge_weight,
    merge_bias,
    norm2_gain,
    norm2_shift,
    expand_weight,
    expand_bias,
    reduce_weight,
    reduce_bias,
    cotangent,
):
    length = packing.shape[2]
    width = features.shape[2]
    heads = width // HEAD_DIM
    scale = HEAD_DIM ** (-0.5)
    mine = lax.axis_index("section")
    order = lax.dynamic_index_in_dim(packing[:, 0], mine, 0, keepdims=False)
    packed_labels = lax.dynamic_index_in_dim(segment_ids[:, 0], mine, 0, keepdims=False)
    labels = jnp.zeros((length,), jnp.int32).at[order].set(packed_labels)
    allowed = labels[:, None] == labels[None, :]

    tokens = swap_rows(features).astype(F32)
    upstream = swap_rows(cotangent)
    project = whole(project_weight, 1, 2)
    merge = whole(merge_weight, 1, 0)
    expand = whole(expand_weight, 0, 1)
    reduce = whole(reduce_weight, 1, 0)

    normed = norm_rows(tokens, norm1_gain, norm1_shift).astype(BF16)
    projected = jnp.einsum("td,cde->cte", normed, project, preferred_element_type=F32)
    queries = (projected[0] + project_bias[0]).astype(BF16).reshape(length, heads, HEAD_DIM)
    keys = projected[1].astype(BF16).reshape(length, heads, HEAD_DIM)
    values = (projected[2] + project_bias[1]).astype(BF16).reshape(length, heads, HEAD_DIM)
    scores = jnp.einsum("qhd,khd->hqk", queries, keys, preferred_element_type=F32) * scale
    scores = jnp.where(allowed[None], scores, MASKED)
    peak = jnp.max(scores, axis=-1, keepdims=True)
    weights = jnp.exp(scores - peak)
    probs = weights / jnp.sum(weights, axis=-1, keepdims=True)
    low_probs = probs.astype(BF16)
    mixed = jnp.einsum("hqk,khd->qhd", low_probs, values, preferred_element_type=F32)
    mixed = mixed.reshape(length, width).astype(BF16)
    middle = tokens + (jnp.dot(mixed, merge, preferred_element_type=F32) + merge_bias)
    normed_two = norm_rows(middle, norm2_gain, norm2_shift).astype(BF16)
    hidden = jnp.dot(normed_two, expand, preferred_element_type=F32) + expand_bias
    active = exact_gelu(hidden).astype(BF16)
    second = jnp.dot(active, reduce, preferred_element_type=F32)
    output = swap_back((middle + (second + reduce_bias)).astype(BF16))

    wide_upstream = upstream.astype(F32)
    reduce_bias_grad = jnp.sum(wide_upstream, axis=0)
    reduce_grad = jnp.einsum("tf,td->fd", active, upstream, preferred_element_type=F32)
    grad_active = jnp.einsum("td,fd->tf", upstream, reduce, preferred_element_type=F32)
    _, gelu_back = jax.vjp(exact_gelu, hidden)
    grad_hidden = gelu_back(grad_active)[0].astype(BF16)
    expand_bias_grad = jnp.sum(grad_hidden.astype(F32), axis=0)
    expand_grad = jnp.einsum("td,tf->df", normed_two, grad_hidden, preferred_element_type=F32)
    grad_normed_two = jnp.einsum("tf,df->td", grad_hidden, expand, preferred_element_type=F32)
    _, norm_back = jax.vjp(norm_rows, middle, norm2_gain, norm2_shift)
    grad_from_norm, gain_two, shift_two = norm_back(grad_normed_two)
    grad_middle = wide_upstream + grad_from_norm
    grad_branch = grad_middle.astype(BF16)
    merge_bias_grad = jnp.sum(grad_branch.astype(F32), axis=0)
    merge_grad = jnp.einsum("te,td->ed", mixed, grad_branch, preferred_element_type=F32)
    grad_mixed = jnp.einsum("td,ed->te", grad_branch, merge, preferred_element_type=F32)
    grad_mixed = grad_mixed.astype(BF16).reshape(length, heads, HEAD_DIM)
    grad_probs = jnp.einsum("qhd,khd->hqk", grad_mixed, values, preferred_element_type=F32)
    inner = jnp.sum(probs * grad_probs, axis=-1, keepdims=True)
    grad_scores = (probs * (grad_probs - inner)).astype(BF16)
    grad_queries = jnp.einsum("hqk,khd->qhd", grad_scores, keys, preferred_element_type=F32) * scale
    grad_keys = jnp.einsum("hqk,qhd->khd", grad_scores, queries, preferred_element_type=F32) * scale
    grad_values = jnp.einsum("hqk,qhd->khd", low_probs, grad_mixed, preferred_element_type=F32)
    stacked = jnp.stack([grad_queries, grad_keys, grad_values])
    stacked = stacked.reshape(3, length, width).astype(BF16)
    wide = stacked.astype(F32)
    project_bias_grad = jnp.stack([jnp.sum(wide[0], axis=0), jnp.sum(wide[2], axis=0)])
    project_grad = jnp.einsum("td,cte->cde", normed, stacked, preferred_element_type=F32)
    grad_normed = jnp.einsum("cte,cde->td", stacked, project, preferred_element_type=F32)
    _, first_back = jax.vjp(norm_rows, tokens, norm1_gain, norm1_shift)
    grad_tokens, gain_one, shift_one = first_back(grad_normed)
    features_grad = swap_back(grad_middle + grad_tokens)

    summed = lax.psum(
        (
            gain_one,
            shift_one,
            project_bias_grad,
            merge_bias_grad,
            gain_two,
            shift_two,
            expand_bias_grad,
            reduce_bias_grad,
        ),
        ("dp", "section"),
    )
    return (
        output,
        features_grad,
        summed[0],
        summed[1],
        shard(project_grad, 1, 2),
        summed[2],
        shard(merge_grad, 1, 0),
        summed[3],
        summed[4],
        summed[5],
        shard(expand_grad, 0, 1),
        summed[6],
        shard(reduce_grad, 1, 0),
        summed[7],
    )


def solution(mesh):
    rows = P(None, ("dp", "section"), None)
    groups = P(None, "dp", None)
    project = P(None, "dp", "section")
    inward = P("section", "dp")
    outward = P("dp", "section")
    in_specs = (rows, groups, groups, P(), P(), project, P(), inward, P(), P(), P(), outward, P(), inward, P(), rows)
    out_specs = (rows, rows, P(), P(), project, P(), inward, P(), P(), P(), outward, P(), inward, P())
    fits = mesh.shape["dp"] == 8 and mesh.shape["section"] == NS
    return jax.shard_map(block if fits else body, mesh=mesh, in_specs=in_specs, out_specs=out_specs, check_vma=False)
```

```python
import functools

import jax
import jax.numpy as jnp
from jax import lax
from jax.experimental import pallas as pl
from jax.experimental.pallas import tpu as pltpu
from jax.sharding import PartitionSpec as P

HEAD_DIM = 64
EPSILON = 1e-06
MASKED = -1000000000.0
F32 = jnp.float32
BF16 = jnp.bfloat16
MESH_ID = pl.DeviceIdType.MESH

NS = 4
D = 768
TOK = 512
ROWS = 96
HALF = 48
SEC = 192
NT_DIMS = (((1,), (1,)), ((), ()))
TN_DIMS = (((0,), (0,)), ((), ()))
CORE, XOWN, YOWN, XFWD, YFWD = range(5)
CHUNK = 128

def norm_stats(values):
    center = values - jnp.mean(values, axis=-1, keepdims=True)
    spread = jnp.mean(center * center, axis=-1, keepdims=True)
    scale = lax.rsqrt(spread + EPSILON)
    return center * scale, scale


def norm_grad(normal, scale, grad, gain):
    scaled = grad * gain
    first = jnp.mean(scaled, axis=-1, keepdims=True)
    second = jnp.mean(scaled * normal, axis=-1, keepdims=True)
    return scale * (scaled - first - normal * second)


def dot(left, right, dims=(((1,), (0,)), ((), ()))):
    return lax.dot_general(left, right, dims, preferred_element_type=F32)


def row(values):
    return values[...].reshape(1, D)


def column_sum(values):
    return jnp.sum(values, axis=0, keepdims=True)


def block_kernel(
    features, packing_in, segments_in, gain1_in, shift1_in, project_in, project_bias_in, merge_in,
    merge_bias_in, gain2_in, shift2_in, expand_in, expand_bias_in, reduce_in, reduce_bias_in, cotangent,
    out, FR, weight_out, sum_out,
    W, G, RC, RD, RE, RZ, RY, X, U, UT, N1, N1T, N2, N2T, QA, AT, MID, ACC1, ACC2, AC, GH, MASK, LSE, PB, EB, SGR, FS, TB,
    z_send, z_recv, g_send, g_recv, r_send, r_recv, rz_send, rz_recv, ry_recv, in_send, in_recv, out_send, out_recv,
    sg_send, sg_recv, local_sem, credit,
    packing, segments, gain1, shift1, project, project_bias, merge, merge_bias, gain2,
    shift2, expand, expand_bias, reduce, reduce_bias, arg_sem, weight_sums, SG, sum_sem,
):
    dp = lax.axis_index("dp")
    z = lax.axis_index("section")
    c = dp % 2
    k = dp // 2
    xi = k % 2
    yi = k // 2
    kx = 2 * yi + (1 - xi)
    ky = 2 * (1 - yi) + xi
    kd = 3 - k
    x_dev = {"dp": 2 * kx + c, "section": z}
    y_dev = {"dp": 2 * ky + c, "section": z}
    c_dev = {"dp": 2 * k + (1 - c), "section": z}

    def z_dev(other):
        return {"dp": dp, "section": other}

    half = z // 2
    inner = ((z + 1) // 2) % 2 == 1
    outer = ((z + 1) // 2) % 2 == 0
    pair = z + 1 - 2 * (z % 2)
    start = (1 - half) * (z % 2) + half * (1 - z % 2)

    def s_of(t):
        base = (t // 2) * t + (1 - t // 2) * ((start + t) % 2)
        return half * 3 + (1 - 2 * half) * base

    def remote(src, dst, send, recv, device):
        return pltpu.make_async_remote_copy(
            src_ref=src, dst_ref=dst, send_sem=send, recv_sem=recv, device_id=device, device_id_type=MESH_ID
        )

    barrier = pltpu.get_barrier_semaphore()
    for device in (x_dev, y_dev, c_dev):
        pl.semaphore_signal(barrier, inc=1, device_id=device, device_id_type=MESH_ID)
    for step in range(1, NS):
        pl.semaphore_signal(barrier, inc=1, device_id=z_dev((z + step) % NS), device_id_type=MESH_ID)

    arguments = (
        (packing_in, packing),
        (segments_in, segments),
        (gain1_in, gain1),
        (shift1_in, shift1),
        (project_in, project),
        (project_bias_in, project_bias),
        (merge_in, merge),
        (merge_bias_in, merge_bias),
        (gain2_in, gain2),
        (shift2_in, shift2),
        (expand_in, expand),
        (expand_bias_in, expand_bias),
        (reduce_in, reduce),
        (reduce_bias_in, reduce_bias),
    )
    for i, (source, target) in enumerate(arguments):
        pltpu.make_async_copy(source, target, arg_sem.at[i]).start()
    for i, (source, target) in enumerate(arguments):
        pltpu.make_async_copy(source, target, arg_sem.at[i]).wait()

    for piece in range(3):
        TB[:, piece * SEC : (piece + 1) * SEC] = project[piece].astype(F32)
    TB[:, 3 * SEC :] = merge[...].astype(F32).T
    W[0, pl.ds(z, 1), pl.ds(k, 1), pl.ds(c, 1)] = TB[...].astype(BF16)[None, None, None]
    W[1, pl.ds(z, 1), pl.ds(k, 1), pl.ds(c, 1)] = expand[...][None, None, None]
    W[2, pl.ds(z, 1), pl.ds(k, 1), pl.ds(c, 1)] = reduce[...][None, None, None]
    pl.semaphore_wait(barrier, 6)

    def z_copy(m, s, up):
        place = W.at[m, s, k, c]
        return remote(place, place, z_send.at[up], z_recv.at[m, s], z_dev(z + 2 * up - 1))

    def z_pass(m, s):
        @pl.when((s <= z) & (z < NS - 1))
        def _():
            z_copy(m, s, 1).start()

        @pl.when((s >= z) & (z > 0))
        def _():
            z_copy(m, s, 0).start()

    def plane_copy(kind, m, s, receive=False):
        rows = slice(None)
        if kind == CORE:
            place = W.at[m, s, :, (1 - c) if receive else c]
            return remote(place, place, g_send.at[kind], g_recv.at[kind, m, s], c_dev)
        if kind == XOWN:
            place = W.at[m, s, kx if receive else k, c]
            return remote(place, place, g_send.at[kind], g_recv.at[kind, m, s], x_dev)
        if kind == YOWN:
            place = W.at[m, s, ky if receive else k, c]
            return remote(place, place, g_send.at[kind], g_recv.at[kind, m, s], y_dev)
        if kind == XFWD:
            place = W.at[m, s, kd if receive else ky, c, pl.ds(0, HALF)]
            return remote(place, place, g_send.at[kind], g_recv.at[kind, m, s], x_dev)
        place = W.at[m, s, kd if receive else kx, c, pl.ds(HALF, HALF)]
        return remote(place, place, g_send.at[kind], g_recv.at[kind, m, s], y_dev)

    def guard(condition, action):
        if isinstance(condition, bool):
            if condition:
                action()
        else:
            pl.when(condition)(action)

    def place_of(i):
        if isinstance(i, int) and i < 3:
            return i, 0
        late = i // 6
        return late * (1 + i % 2), late * (i // 2 - 2) + (1 - late) * (i - 2)

    def gather_a(i):
        def action():
            m, t = place_of(i)
            s = s_of(t)
            if not isinstance(i, int) or i > 2:
                z_copy(m, s, 0).wait_recv()
                z_pass(m, s)
            plane_copy(XOWN, m, s).start()
            plane_copy(YOWN, m, s).start()

        guard(i <= 11, action)

    def gather_b(i):
        def action():
            m, t = place_of(i)
            s = s_of(t)
            plane_copy(YOWN, m, s, True).wait_recv()
            plane_copy(XFWD, m, s).start()
            plane_copy(XOWN, m, s, True).wait_recv()
            plane_copy(YFWD, m, s).start()

        guard(i <= 11, action)

    def gather_c(i):
        def action():
            m, t = place_of(i)
            s = s_of(t)
            plane_copy(XFWD, m, s, True).wait_recv()
            plane_copy(YFWD, m, s, True).wait_recv()
            plane_copy(CORE, m, s).start()

        guard(i <= 11, action)

    def gather_d(m, t):
        plane_copy(CORE, m, s_of(t), True).wait_recv()

    def pump(i):
        gather_a(i + 3)
        gather_b(i + 1)
        gather_c(i)

    def rs_core(m, s, at, receive=False):
        place = RC.at[m % 2, at]
        source = place if receive else G.at[m, s, :, 1 - c]
        return remote(source, place, r_send.at[CORE], r_recv.at[CORE, m, s], c_dev)

    def rs_diag(kind, m, s, at):
        which, device = (0, x_dev) if kind == XFWD else (1, y_dev)
        return remote(
            G.at[m, s, kd, c, pl.ds(which * HALF, HALF)], RD.at[m % 2, at, which],
            r_send.at[kind], r_recv.at[kind, m, s], device,
        )

    def rs_side(kind, m, s, at):
        which, device, block = (0, x_dev, kx) if kind == XOWN else (1, y_dev, ky)
        return remote(
            G.at[m, s, block, c], RE.at[m % 2, at, which], r_send.at[kind], r_recv.at[kind, m, s], device
        )

    def rs_near(m, s):
        near = s // 2 == z // 2
        place = G.at[m, s, k, c]

        @pl.when(near)
        def _():
            remote(place, RZ.at[m, 0], rz_send.at[0], rz_recv.at[m, 0], z_dev(pair)).start()

        @pl.when(jnp.logical_not(near) & outer)
        def _():
            remote(place, RY.at[m, s % 2], rz_send.at[0], ry_recv.at[m, s % 2], z_dev(pair)).start()

    def rs_far(m, s):
        @pl.when((s // 2 != z // 2) & inner)
        def _():
            place = G.at[m, s, k, c]
            buffer = RY.at[m, s % 2]
            remote(buffer, buffer, rz_send.at[0], ry_recv.at[m, s % 2], z_dev(pair)).wait_recv()
            add_into(place, buffer)
            remote(place, RZ.at[m, 1], rz_send.at[0], rz_recv.at[m, 1], z_dev(s)).start()

    def add_into(place, other):
        place[...] = place[...] + other[...]

    def scatter_place(r):
        if r < 8:
            return 2 - r % 2, s_of(r // 2), s_of(r // 2)
        return 0, s_of(11 - r), s_of(r - 8)

    def credit_give(at):
        for device, which in ((c_dev, 0), (x_dev, 1), (y_dev, 2)):
            pl.semaphore_signal(credit.at[which, at], inc=1, device_id=device, device_id_type=MESH_ID)

    def credit_take(at):
        for which in range(3):
            pl.semaphore_wait(credit.at[which, at], 1)

    def scatter_p(m, s, at):
        rs_core(m, s, at).start()

    def scatter_q(r):
        m, s, at = scatter_place(r)
        rs_core(m, s, at, True).wait_recv()
        for block in range(4):
            add_into(G.at[m, s, block, c], RC.at[m % 2, at, block])
        rs_diag(XFWD, m, s, at).start()
        rs_diag(YFWD, m, s, at).start()

    def scatter_r(r):
        m, s, at = scatter_place(r)
        rs_diag(XFWD, m, s, at).wait_recv()
        add_into(G.at[m, s, ky, c, pl.ds(0, HALF)], RD.at[m % 2, at, 0])
        rs_side(YOWN, m, s, at).start()
        rs_diag(YFWD, m, s, at).wait_recv()
        add_into(G.at[m, s, kx, c, pl.ds(HALF, HALF)], RD.at[m % 2, at, 1])
        rs_side(XOWN, m, s, at).start()

    def scatter_t(r):
        m, s, at = scatter_place(r)
        rs_side(XOWN, m, s, at).wait_recv()
        rs_side(YOWN, m, s, at).wait_recv()
        place = G.at[m, s, k, c]
        total = RE[m % 2, at, 0].astype(F32) + RE[m % 2, at, 1].astype(F32)
        place[...] = (place[...].astype(F32) + total).astype(BF16)
        if r in (0, 2, 4, 6):
            credit_give(r // 2)
        pl.when(s != z)(lambda: rs_near(m, s))

    def scatter_z(r):
        m, s, _ = scatter_place(r)
        rs_far(m, s)

    def scatter_sum(m):
        total = G[m, z, k, c].astype(F32)
        for which in range(2):
            remote(RZ.at[m, which], RZ.at[m, which], rz_send.at[0], rz_recv.at[m, which], z_dev(pair)).wait_recv()
            total = total + RZ[m, which].astype(F32)
        return total

    def row_copy(which, source, target, there):
        return remote(source.at[there], target.at[z], in_send.at[which, there], in_recv.at[which, z], z_dev(there))

    def row_send(which, source, target, t):
        row_copy(which, source, target, s_of(t)).start()

    def rows_wait(which, source, target, t):
        origin = s_of(t)
        if t == 0:
            pltpu.make_async_copy(source.at[z], target.at[z], local_sem.at[which]).wait()
        else:
            remote(
                source.at[origin], target.at[origin], in_send.at[which, origin], in_recv.at[which, origin], z_dev(origin)
            ).wait_recv()
        return origin

    def back_send(which, source, target, there):
        remote(source.at[there], target.at[z], out_send.at[which, there], out_recv.at[which, z], z_dev(there)).start()

    def back_keep(which, source, target):
        pltpu.make_async_copy(source.at[z], target.at[z], local_sem.at[2 + which]).start()

    def back_wait(which, source, target):
        for step in range(1, NS):
            other = (z + step) % NS
            remote(
                source.at[other], target.at[other], out_send.at[which, other], out_recv.at[which, other], z_dev(other)
            ).wait()
        pltpu.make_async_copy(source.at[z], target.at[z], local_sem.at[2 + which]).wait()

    def sum_z(step):
        other = (z + step) % NS
        return remote(SG, SGR.at[z], sg_send.at[step], sg_recv.at[z], z_dev(other))

    def sum_z_wait():
        for step in range(1, NS):
            origin = (z + step) % NS
            remote(SGR.at[origin], SGR.at[origin], sg_send.at[step], sg_recv.at[origin], z_dev(origin)).wait_recv()
            sum_z(step).wait_send()
        SGR[pl.ds(z, 1)] = SG[...][None]
        SG[...] = (SGR[0] + SGR[1]) + (SGR[2] + SGR[3])

    def sum_leave(m):
        return pltpu.make_async_copy(weight_sums.at[m], weight_out.at[m], sum_sem.at[m])

    def keep_sum(m):
        weight_sums[m] = scatter_sum(m)
        sum_leave(m).start()

    def sum_copy(step, device):
        return remote(SG, SGR.at[step], sg_send.at[step], sg_recv.at[step], device)

    def sum_end(step, device):
        sum_copy(step, device).wait()
        SG[...] = SG[...] + SGR[step]

    def z_near(m):
        z_copy(m, z, 1 - z % 2).start()

    def z_far(m):
        z_copy(m, z, z % 2).start()

    for which, source, target in ((0, features, X), (1, cotangent, U)):
        pltpu.make_async_copy(source.at[z], target.at[z], local_sem.at[which]).start()

    @pl.when(inner)
    def _():
        z_near(1)
        z_far(1)
        z_far(0)
        row_send(1, cotangent, U, 1)
        gather_a(0)
        z_far(2)
        z_near(0)
        gather_a(2)
        gather_a(1)
        gather_a(3)
        z_near(2)
        gather_b(2)
        gather_a(4)
        row_send(0, features, X, 2)
        gather_b(0)
        gather_a(5)
        gather_c(0)
        row_send(0, features, X, 3)
        gather_b(3)
        row_send(0, features, X, 1)
        gather_b(4)
        gather_b(1)

    @pl.when(outer)
    def _():
        z_near(0)
        gather_a(0)
        gather_a(2)
        row_send(1, cotangent, U, 1)
        gather_b(0)
        gather_a(1)
        z_near(2)
        gather_a(6)
        row_send(0, features, X, 2)
        row_send(0, features, X, 1)
        z_near(1)
        gather_c(0)
        gather_b(6)
        gather_a(3)
        gather_a(7)
        gather_a(4)
        row_send(0, features, X, 3)

    order = packing[z]
    labels = segments[z].astype(F32)
    token = lax.broadcasted_iota(jnp.int32, (TOK, TOK), 0)
    token_labels = jnp.sum(jnp.where(token == order, labels, 0.0), axis=1, keepdims=True)
    kinds = lax.broadcasted_iota(jnp.int32, (TOK, 128), 1).astype(F32)
    one_hot = jnp.where(token_labels == kinds, 1.0, 0.0).astype(BF16)
    MASK[...] = (dot(one_hot, one_hot, NT_DIMS) - 1.0) * -MASKED
    AT[:, :, 0:64] = jnp.zeros((NS, TOK, 64), BF16)
    SG[...] = jnp.zeros_like(SG)
    PB[...] = jnp.zeros_like(PB)
    for s in range(NS):
        EB[s] = expand_bias[s * D : (s + 1) * D].reshape(1, D)
        PB[s, :, 0:SEC] = project_bias[0:1, s * SEC : (s + 1) * SEC]
        PB[s, :, 2 * SEC : 3 * SEC] = project_bias[1:2, s * SEC : (s + 1) * SEC]

    @pl.when(inner)
    def _():
        gather_a(7)
        gather_c(3)

    @pl.when(outer)
    def _():
        gather_b(2)
        gather_a(5)
        gather_b(3)
        gather_b(4)
        gather_b(1)

    for t in range(NS):
        i = rows_wait(0, features, X, t)
        rows = pl.ds(pl.multiple_of(i * CHUNK, CHUNK), CHUNK)
        normal, _ = norm_stats(X[i].astype(F32))
        normed = normal * row(gain1) + row(shift1)
        N1[rows, :] = normed.astype(BF16)
        N1T[:, rows] = normed.T.astype(BF16)

    def weight(m, s):
        return W[m, s].reshape(D, D)

    def weight_tile(m, s, n):
        return W[m, s, :, :, :, pl.ds(pl.multiple_of(n * 256, 256), 256)].reshape(D, 256)

    def weight_end(s):
        return W[0, s, :, :, :, 512:768].reshape(D, 256)

    def attend(s, between):
        for first, last in ((0, 256), (256, 512), (512, 640)):
            part = dot(N1[...], W[0, s, :, :, :, first:last].reshape(D, last - first))
            QA[s, :, first:last] = (part + PB[s, :, first:last]).astype(BF16)
        between()
        for j in range(3):
            keys = QA[s, :, SEC + 64 * j : SEC + 64 * j + 64]
            values = QA[s, :, 2 * SEC + 64 * j : 2 * SEC + 64 * j + 64]
            queries = QA[s, :, 64 * j : 64 * j + 64] * 0.125
            scores = dot(keys, queries, NT_DIMS) + MASK[...]
            peak = jnp.max(scores, axis=0, keepdims=True)
            weights = jnp.exp(scores - peak)
            total = jnp.sum(weights, axis=0, keepdims=True)
            LSE[s * 3 + j] = peak + jnp.log(total)
            mixed = dot(values, weights.astype(BF16), TN_DIMS) * (1.0 / total)
            AT[s, :, 64 + 64 * j : 128 + 64 * j] = mixed.T.astype(BF16)
        ACC1[...] += dot(AT[s], weight_end(s), NT_DIMS)

    ACC1[...] = jnp.zeros_like(ACC1)

    @pl.when(outer)
    def _():
        gather_b(5)

    def attend_step(t, carry):

        @pl.when(t == 0)
        def _():

            @pl.when(inner)
            def _():
                gather_a(6)
                gather_c(1)
                gather_a(9)
                gather_c(2)

            @pl.when(outer)
            def _():
                gather_c(3)

        @pl.when(t == 1)
        def _():

            @pl.when(inner)
            def _():
                gather_b(5)

        @pl.when(t == 2)
        def _():

            @pl.when(inner)
            def _():
                row_send(1, cotangent, U, 2)
                gather_c(4)
                gather_a(8)
                gather_b(6)
                gather_a(10)
                gather_b(7)
                gather_c(5)

            @pl.when(outer)
            def _():
                gather_a(9)

        @pl.when(t == 3)
        def _():

            @pl.when(inner)
            def _():
                gather_a(11)
                row_send(1, cotangent, U, 3)

            @pl.when(outer)
            def _():
                gather_a(8)
                gather_c(6)

        gather_d(0, t)

        def between():

            @pl.when(t == 0)
            def _():

                @pl.when(outer)
                def _():
                    row_send(1, cotangent, U, 2)
                    gather_b(7)
                    gather_c(4)

            @pl.when(t == 1)
            def _():

                @pl.when(outer)
                def _():
                    gather_c(2)
                    gather_c(5)

            @pl.when(t == 3)
            def _():

                @pl.when(outer)
                def _():
                    gather_b(9)
                    gather_c(1)

        attend(s_of(t), between)
        return carry

    lax.fori_loop(0, NS, attend_step, 0)


    @pl.when(inner)
    def _():
        gather_c(6)

    @pl.when(outer)
    def _():
        row_send(1, cotangent, U, 3)
        gather_a(10)
        gather_b(8)
        gather_c(7)

    for i in range(NS):
        rows = slice(i * CHUNK, (i + 1) * CHUNK)
        middle = X[i].astype(F32) + (ACC1[rows, :] + row(merge_bias))
        MID[rows, :] = middle
        normal, _ = norm_stats(middle)
        normed = normal * row(gain2) + row(shift2)
        N2[i] = normed.astype(BF16)
        N2T[:, rows] = normed.T.astype(BF16)

    @pl.when(inner)
    def _():
        gather_b(8)

    @pl.when(outer)
    def _():
        gather_a(11)
        gather_c(9)

    for t in range(NS):
        i = rows_wait(1, cotangent, U, t)
        upstream = U[i].astype(F32)
        UT[:, pl.ds(pl.multiple_of(i * CHUNK, CHUNK), CHUNK)] = upstream.T.astype(BF16)
        SG[5:6, :] += column_sum(upstream)
    ACC1[...] = jnp.zeros_like(ACC1)
    ACC2[...] = jnp.zeros_like(ACC2)

    @pl.when(inner)
    def _():
        gather_b(9)

    def feed(s, between):
        def tile_step(n, carry):
            lanes = pl.ds(pl.multiple_of(n * 256, 256), 256)
            hidden = dot(N2[...].reshape(TOK, D), weight_tile(1, s, n)) + EB[s, :, lanes]
            gate = 0.5 + 0.5 * lax.erf(hidden * 0.7071067811865476)
            active = (hidden * gate).astype(BF16)
            AC[:, lanes] = active
            slope = gate + hidden * (jnp.exp(-0.5 * hidden * hidden) * 0.3989422804014327)
            G[2, s, :, :, :, lanes] = dot(UT[...], active).astype(BF16).reshape(4, 2, ROWS, 256)
            grad_active = dot(U[...].reshape(TOK, D), weight_tile(2, s, n))
            grad_hidden = (grad_active * slope).astype(BF16)
            GH[:, lanes] = grad_hidden
            SG[pl.ds(6 + s, 1), lanes] = column_sum(grad_hidden.astype(F32))
            G[1, s, :, :, :, lanes] = dot(N2T[...], grad_hidden).astype(BF16).reshape(4, 2, ROWS, 256)
            return carry

        lax.fori_loop(0, 3, tile_step, 0, unroll=True)
        between()
        ACC1[...] += dot(AC[...], weight(2, s), NT_DIMS)
        ACC2[...] += dot(GH[...], weight(1, s), NT_DIMS)

    def feed_step(t, carry):
        s = s_of(t)

        def before():

            @pl.when(t == 0)
            def _():

                @pl.when(inner)
                def _():
                    gather_c(7)

            @pl.when(t == 1)
            def _():

                @pl.when(inner)
                def _():
                    gather_b(10)
                    gather_b(11)
                    gather_c(9)
                    gather_c(8)

                @pl.when(outer)
                def _():
                    gather_c(8)
                    gather_b(11)
                    gather_b(10)

            @pl.when(t == 2)
            def _():
                scatter_q(0)
                gather_c(11)
                gather_c(10)

            @pl.when(t == 3)
            def _():

                @pl.when(outer)
                def _():
                    scatter_q(2)

        def between():
            scatter_p(2, s, s)
            scatter_p(1, s, s)

            @pl.when(t == 2)
            def _():

                @pl.when(inner)
                def _():
                    scatter_q(2)

                scatter_r(0)

            @pl.when(t == 3)
            def _():

                @pl.when(outer)
                def _():
                    scatter_q(5)

        before()
        gather_d(1, t)
        gather_d(2, t)
        feed(s, between)
        return carry

    lax.fori_loop(0, NS, feed_step, 0)

    for i in range(NS):
        rows = slice(i * CHUNK, (i + 1) * CHUNK)
        FS[i] = (MID[rows, :] + (ACC1[rows, :] + row(reduce_bias))).astype(BF16)
    back_keep(0, FS, out)
    back_send(0, FS, out, s_of(2))

    @pl.when(inner)
    def _():
        scatter_t(0)

    @pl.when(outer)
    def _():
        scatter_r(2)
        scatter_r(5)
        back_send(0, FS, out, s_of(3))
        scatter_t(0)
        scatter_q(4)

    for i in range(NS):
        rows = slice(i * CHUNK, (i + 1) * CHUNK)
        normal, scale = norm_stats(MID[rows, :])
        grad = ACC2[rows, :]
        grad_middle = U[i].astype(F32) + norm_grad(normal, scale, grad, row(gain2))
        SG[2:3, :] += column_sum(grad * normal)
        SG[3:4, :] += column_sum(grad)
        grad_branch = grad_middle.astype(BF16)
        SG[4:5, :] += column_sum(grad_branch.astype(F32))
        MID[rows, :] = grad_middle
        AC[rows, :] = grad_branch
        UT[:, rows] = grad_branch.astype(F32).T.astype(BF16)
    ACC2[...] = jnp.zeros_like(ACC2)

    @pl.when(inner)
    def _():
        back_send(0, FS, out, s_of(1))
        scatter_q(6)

    def attend_back(s, between):
        N1[:, 0:256] = dot(AC[...], weight_end(s)).astype(BF16)
        GH[:, 512:768] = jnp.zeros((TOK, 256), BF16)
        for j in range(3):
            keys = QA[s, :, SEC + 64 * j : SEC + 64 * j + 64]
            values = QA[s, :, 2 * SEC + 64 * j : 2 * SEC + 64 * j + 64]
            queries = QA[s, :, 64 * j : 64 * j + 64] * 0.125
            grad_mixed = N1[:, 64 + 64 * j : 128 + 64 * j]
            scores = dot(keys, queries, NT_DIMS) + MASK[...]
            probs = jnp.exp(scores - LSE[s * 3 + j])
            grad_probs = dot(values, grad_mixed, NT_DIMS)
            inner = jnp.sum(probs * grad_probs, axis=0, keepdims=True)
            grad_scores = (probs * (grad_probs - inner)).astype(BF16)
            grad_queries = dot(keys, grad_scores, TN_DIMS) * 0.125
            GH[:, 64 * j : 64 * j + 64] = grad_queries.T.astype(BF16)
            GH[:, SEC + 64 * j : SEC + 64 * j + 64] = dot(grad_scores, queries).astype(BF16)
            GH[:, 2 * SEC + 64 * j : 2 * SEC + 64 * j + 64] = dot(probs.astype(BF16), grad_mixed).astype(BF16)
        between()
        SG[pl.ds(10 + s, 1), :] = column_sum(GH[...].astype(F32))
        ACC2[...] += dot(GH[...], weight(0, s), NT_DIMS)

    def attend_weight(s):
        for n in range(3):
            lanes = slice(n * 256, n * 256 + 256)
            part = dot(N1T[...], GH[:, lanes])
            if n == 2:
                part += dot(UT[...], AT[s])
            G[0, s, :, :, :, lanes] = part.astype(BF16).reshape(4, 2, ROWS, 256)

    def back_step(t, carry):
        s = s_of(3 - t)

        def before():

            @pl.when(t == 0)
            def _():

                @pl.when(inner)
                def _():
                    scatter_q(4)
                    scatter_r(2)

            @pl.when(t == 1)
            def _():

                @pl.when(inner)
                def _():
                    scatter_r(6)
                    scatter_r(4)

                @pl.when(outer)
                def _():
                    scatter_r(4)
                    scatter_q(6)
                    scatter_t(2)
                    scatter_q(7)

            @pl.when(t == 2)
            def _():

                @pl.when(outer)
                def _():
                    scatter_r(6)
                    scatter_t(5)

            @pl.when(t == 3)
            def _():

                @pl.when(outer)
                def _():
                    scatter_r(7)
                    scatter_t(6)

        def between():

            @pl.when(t == 0)
            def _():

                @pl.when(outer)
                def _():
                    back_send(0, FS, out, s_of(1))

            @pl.when(t == 1)
            def _():

                @pl.when(inner)
                def _():
                    scatter_t(2)

                scatter_q(8)

            @pl.when(t == 2)
            def _():

                @pl.when(inner)
                def _():
                    back_send(0, FS, out, s_of(3))
                    scatter_t(4)
                    scatter_r(8)
                    scatter_t(6)
                    scatter_z(0)

                @pl.when(outer)
                def _():
                    scatter_t(4)
                    scatter_r(8)

            @pl.when(t == 3)
            def _():

                @pl.when(outer)
                def _():
                    scatter_t(8)
                    scatter_q(9)

        before()
        attend_back(s, between)

        @pl.when(t < NS - 1)
        def _():
            attend_weight(s)
            credit_take(t)
            scatter_p(0, s, s_of(t))

        return carry

    lax.fori_loop(0, NS, back_step, 0)


    for step in (2, 1, 3, 0):
        i = (z + step) % NS
        rows = pl.ds(pl.multiple_of(i * CHUNK, CHUNK), CHUNK)
        normal, _ = norm_stats(X[i].astype(F32))
        grad = ACC2[rows, :]
        SG[0:1, :] += column_sum(grad * normal)
        SG[1:2, :] += column_sum(grad)
    for step in range(1, NS):
        sum_z(step).start()
    for step in (2, 1, 3, 0):
        i = (z + step) % NS
        rows = pl.ds(pl.multiple_of(i * CHUNK, CHUNK), CHUNK)
        normal, scale = norm_stats(X[i].astype(F32))
        N2[i] = (MID[rows, :] + norm_grad(normal, scale, ACC2[rows, :], row(gain1))).astype(BF16)
    back_keep(1, N2, FR)

    @pl.when(inner)
    def _():
        scatter_q(5)
        scatter_q(10)
        back_send(1, N2, FR, s_of(2))
        back_send(1, N2, FR, s_of(3))
        scatter_q(7)
        scatter_r(10)
        back_send(1, N2, FR, s_of(1))

    @pl.when(outer)
    def _():
        scatter_q(10)
        back_send(1, N2, FR, s_of(2))
        scatter_t(7)

    attend_weight(z)
    credit_take(3)
    scatter_p(0, z, s_of(3))

    @pl.when(inner)
    def _():
        scatter_z(4)
        scatter_r(5)
        scatter_q(9)
        scatter_z(6)
        scatter_q(3)
        scatter_r(9)
        sum_z_wait()
        scatter_q(11)
        scatter_t(8)
        scatter_t(10)
        scatter_r(3)
        scatter_q(1)
        scatter_r(7)
        sum_copy(4, c_dev).start()
        sum_end(4, c_dev)
        scatter_z(8)
        keep_sum(2)
        scatter_t(5)
        scatter_r(1)
        scatter_t(7)
        scatter_z(7)
        scatter_r(11)
        scatter_t(1)
        scatter_t(9)
        sum_copy(5, x_dev).start()
        scatter_z(10)
        scatter_z(5)
        scatter_t(3)
        scatter_z(1)
        sum_end(5, x_dev)
        scatter_z(9)
        scatter_t(11)
        sum_copy(6, y_dev).start()
        sum_end(6, y_dev)
        keep_sum(1)
        scatter_z(3)
        keep_sum(0)
        scatter_z(2)

    @pl.when(outer)
    def _():
        scatter_q(3)
        back_send(1, N2, FR, s_of(3))
        scatter_r(9)
        scatter_r(10)
        sum_z_wait()
        scatter_q(11)
        scatter_t(9)
        sum_copy(4, c_dev).start()
        scatter_q(1)
        scatter_r(3)
        sum_end(4, c_dev)
        keep_sum(2)
        scatter_r(11)
        scatter_t(10)
        sum_copy(5, x_dev).start()
        sum_end(5, x_dev)
        sum_copy(6, y_dev).start()
        back_send(1, N2, FR, s_of(1))
        scatter_t(3)
        scatter_r(1)
        scatter_t(11)
        scatter_t(1)
        keep_sum(1)
        sum_end(6, y_dev)
        keep_sum(0)

    small = pltpu.make_async_copy(SG, sum_out, sum_sem.at[3])
    small.start()
    back_wait(0, FS, out)
    back_wait(1, N2, FR)

    def gone(blocks, send, receive, device):
        remote(blocks, blocks, send, receive, device).wait_send()

    pair_dev = z_dev(pair)

    @pl.when(outer)
    def _():
        gone(W.at[:, 0, k, c], z_send.at[1 - z % 2], z_recv.at[0, 0], pair_dev)

    @pl.when(inner)
    def _():
        gone(W.at[:, 0:3, k, c], z_send.at[1 - z % 2], z_recv.at[0, 0], pair_dev)
        gone(W.at[:, 0:2, k, c], z_send.at[z % 2], z_recv.at[0, 0], z_dev(NS - 1 - z))

    gone(W.at[:, :, :, c], g_send.at[CORE], g_recv.at[CORE, 0, 0], c_dev)
    gone(W.at[:, :, k, c], g_send.at[XOWN], g_recv.at[XOWN, 0, 0], x_dev)
    gone(W.at[:, :, k, c], g_send.at[YOWN], g_recv.at[YOWN, 0, 0], y_dev)
    gone(W.at[:, :, k, c, pl.ds(0, HALF)], g_send.at[XFWD], g_recv.at[XFWD, 0, 0], x_dev)
    gone(W.at[:, :, k, c, pl.ds(0, HALF)], g_send.at[YFWD], g_recv.at[YFWD, 0, 0], y_dev)
    gone(G.at[:, :, :, c], r_send.at[CORE], r_recv.at[CORE, 0, 0], c_dev)
    gone(G.at[:, :, k, c], r_send.at[XOWN], r_recv.at[XOWN, 0, 0], x_dev)
    gone(G.at[:, :, k, c], r_send.at[YOWN], r_recv.at[YOWN, 0, 0], y_dev)
    gone(G.at[:, :, k, c, pl.ds(0, HALF)], r_send.at[XFWD], r_recv.at[XFWD, 0, 0], x_dev)
    gone(G.at[:, :, k, c, pl.ds(0, HALF)], r_send.at[YFWD], r_recv.at[YFWD, 0, 0], y_dev)
    gone(G.at[:, 0:3, k, c], rz_send.at[0], rz_recv.at[0, 0], pair_dev)
    for which, source, target in ((0, features, X), (1, cotangent, U)):
        for step in range(1, NS):
            row_copy(which, source, target, (z + step) % NS).wait_send()
    for m in range(3):
        sum_leave(m).wait()
    small.wait()


def finish_kernel(
    rows, grads, weight_sums, sums,
    out, features_grad, gain1_grad, shift1_grad, project_grad, project_bias_grad, merge_grad, merge_bias_grad,
    gain2_grad, shift2_grad, expand_grad, expand_bias_grad, reduce_grad, reduce_bias_grad,
    low_rows, wide, carried, project_sums, small, sem_in, sem_out,
):
    first = pltpu.make_async_copy(sums, small, sem_in.at[0])
    second = pltpu.make_async_copy(weight_sums.at[0], project_sums, sem_in.at[1])
    in_copies = [pltpu.make_async_copy(grads.at[i], low_rows.at[i], sem_in.at[2 + i]) for i in range(NS)]
    through = [pltpu.make_async_copy(rows.at[i], carried.at[i], sem_in.at[6 + i]) for i in range(NS)]
    weight_copies = [
        pltpu.make_async_copy(weight_sums.at[1], expand_grad, sem_out.at[1]),
        pltpu.make_async_copy(weight_sums.at[2], reduce_grad, sem_out.at[2]),
    ]
    for copy in in_copies + through + weight_copies + [second, first]:
        copy.start()
    out_copies = [pltpu.make_async_copy(wide.at[i], features_grad.at[i], sem_out.at[3 + i]) for i in range(NS)]
    out_copies += [pltpu.make_async_copy(carried.at[i], out.at[i], sem_out.at[7 + i]) for i in range(NS)]
    for i in range(NS):
        in_copies[i].wait()
        wide[i] = low_rows[i].astype(F32)
        out_copies[i].start()
    for i in range(NS):
        through[i].wait()
        out_copies[NS + i].start()
    second.wait()
    for piece in range(3):
        project_grad[piece] = project_sums[:, piece * SEC : (piece + 1) * SEC]
    merge_grad[...] = project_sums[:, 3 * SEC :].T
    first.wait()
    gain1_grad[...] = small[0]
    shift1_grad[...] = small[1]
    gain2_grad[...] = small[2]
    shift2_grad[...] = small[3]
    merge_bias_grad[...] = small[4]
    reduce_bias_grad[...] = small[5]
    for s in range(NS):
        expand_bias_grad[s * D : (s + 1) * D] = small[6 + s]
        project_bias_grad[0:1, s * SEC : (s + 1) * SEC] = small[10 + s : 11 + s, 0:SEC]
        project_bias_grad[1:2, s * SEC : (s + 1) * SEC] = small[10 + s : 11 + s, 2 * SEC : 3 * SEC]
    for copy in weight_copies + out_copies:
        copy.wait()


def block(features, packing, segment_ids, norm1_gain, norm1_shift, project_weight, project_bias, merge_weight, merge_bias,
          norm2_gain, norm2_shift, expand_weight, expand_bias, reduce_weight, reduce_bias, cotangent):
    vmem = pl.BlockSpec(memory_space=pltpu.VMEM)
    anywhere = pl.BlockSpec(memory_space=pl.ANY)
    shape = jax.ShapeDtypeStruct
    inner = pl.pallas_call(
        block_kernel,
        name="block",
        in_specs=[anywhere] * 16,
        out_specs=[anywhere] * 4,
        out_shape=[
            shape((NS, CHUNK, D), BF16),
            shape((NS, CHUNK, D), BF16),
            shape((3, ROWS, D), F32),
            shape((16, D), F32),
        ],
        scratch_shapes=[
            pltpu.VMEM((3, NS, 4, 2, ROWS, D), BF16),
            pltpu.VMEM((3, NS, 4, 2, ROWS, D), BF16),
            pltpu.VMEM((2, NS, 4, ROWS, D), BF16),
            pltpu.VMEM((2, NS, 2, HALF, D), BF16),
            pltpu.VMEM((2, NS, 2, ROWS, D), BF16),
            pltpu.VMEM((3, 2, ROWS, D), BF16),
            pltpu.VMEM((3, 2, ROWS, D), BF16),
            pltpu.VMEM((NS, CHUNK, D), BF16),
            pltpu.VMEM((NS, CHUNK, D), BF16),
            pltpu.VMEM((D, TOK), BF16),
            pltpu.VMEM((TOK, D), BF16),
            pltpu.VMEM((D, TOK), BF16),
            pltpu.VMEM((NS, CHUNK, D), BF16),
            pltpu.VMEM((D, TOK), BF16),
            pltpu.VMEM((NS, TOK, 640), BF16),
            pltpu.VMEM((NS, TOK, 256), BF16),
            pltpu.VMEM((TOK, D), F32),
            pltpu.VMEM((TOK, D), F32),
            pltpu.VMEM((TOK, D), F32),
            pltpu.VMEM((TOK, D), BF16),
            pltpu.VMEM((TOK, D), BF16),
            pltpu.VMEM((TOK, TOK), F32),
            pltpu.VMEM((16, 1, TOK), F32),
            pltpu.VMEM((NS, 1, D), F32),
            pltpu.VMEM((NS, 1, D), F32),
            pltpu.VMEM((7, 16, D), F32),
            pltpu.VMEM((NS, CHUNK, D), BF16),
            pltpu.VMEM((ROWS, D), F32),
            pltpu.SemaphoreType.DMA((2,)),
            pltpu.SemaphoreType.DMA((3, NS)),
            pltpu.SemaphoreType.DMA((5,)),
            pltpu.SemaphoreType.DMA((5, 3, NS)),
            pltpu.SemaphoreType.DMA((5,)),
            pltpu.SemaphoreType.DMA((5, 3, NS)),
            pltpu.SemaphoreType.DMA((1,)),
            pltpu.SemaphoreType.DMA((3, 2)),
            pltpu.SemaphoreType.DMA((3, 2)),
            pltpu.SemaphoreType.DMA((2, NS)),
            pltpu.SemaphoreType.DMA((2, NS)),
            pltpu.SemaphoreType.DMA((2, NS)),
            pltpu.SemaphoreType.DMA((2, NS)),
            pltpu.SemaphoreType.DMA((7,)),
            pltpu.SemaphoreType.DMA((7,)),
            pltpu.SemaphoreType.DMA((4,)),
            pltpu.SemaphoreType.REGULAR((3, NS)),
            pltpu.VMEM((NS, 1, TOK), jnp.int32),
            pltpu.VMEM((NS, 1, TOK), jnp.int32),
            pltpu.VMEM((D,), F32),
            pltpu.VMEM((D,), F32),
            pltpu.VMEM((3, ROWS, SEC), BF16),
            pltpu.VMEM((2, D), F32),
            pltpu.VMEM((SEC, ROWS), BF16),
            pltpu.VMEM((D,), F32),
            pltpu.VMEM((D,), F32),
            pltpu.VMEM((D,), F32),
            pltpu.VMEM((ROWS, D), BF16),
            pltpu.VMEM((4 * D,), F32),
            pltpu.VMEM((ROWS, D), BF16),
            pltpu.VMEM((D,), F32),
            pltpu.SemaphoreType.DMA((14,)),
            pltpu.VMEM((3, ROWS, D), F32),
            pltpu.VMEM((16, D), F32),
            pltpu.SemaphoreType.DMA((4,)),
        ],
        compiler_params=pltpu.CompilerParams(collective_id=0, has_side_effects=True, vmem_limit_bytes=66 * 1000 * 1000),
    )(
        features, packing, segment_ids, norm1_gain, norm1_shift, project_weight, project_bias, merge_weight, merge_bias,
        norm2_gain, norm2_shift, expand_weight, expand_bias, reduce_weight.T, reduce_bias, cotangent,
    )
    results = pl.pallas_call(
        finish_kernel,
        name="finish",
        in_specs=[anywhere] * 4,
        out_specs=[anywhere] * 2 + [vmem] * 12,
        out_shape=[
            shape((NS, CHUNK, D), BF16),
            shape((NS, CHUNK, D), F32),
            shape((D,), F32),
            shape((D,), F32),
            shape((3, ROWS, SEC), F32),
            shape((2, D), F32),
            shape((SEC, ROWS), F32),
            shape((D,), F32),
            shape((D,), F32),
            shape((D,), F32),
            shape((ROWS, D), F32),
            shape((4 * D,), F32),
            shape((ROWS, D), F32),
            shape((D,), F32),
        ],
        scratch_shapes=[
            pltpu.VMEM((NS, CHUNK, D), BF16),
            pltpu.VMEM((NS, CHUNK, D), F32),
            pltpu.VMEM((NS, CHUNK, D), BF16),
            pltpu.VMEM((ROWS, D), F32),
            pltpu.VMEM((16, D), F32),
            pltpu.SemaphoreType.DMA((10,)),
            pltpu.SemaphoreType.DMA((11,)),
        ],
        compiler_params=pltpu.CompilerParams(vmem_limit_bytes=63 * 1000 * 1000),
    )(*inner)
    return tuple(results[:12]) + (results[12].T, results[13])


def norm_rows(values, gain, shift):
    center = values - jnp.mean(values, axis=-1, keepdims=True)
    spread = jnp.mean(center * center, axis=-1, keepdims=True)
    return center * lax.rsqrt(spread + EPSILON) * gain + shift


def exact_gelu(values):
    return jax.nn.gelu(values, approximate=False)


def swap_rows(values):
    return lax.all_to_all(values, "section", split_axis=0, concat_axis=1, tiled=True)[0]


def swap_back(values):
    return lax.all_to_all(values[None], "section", split_axis=1, concat_axis=0, tiled=True)


def whole(values, dp_axis, section_axis):
    values = lax.all_gather(values, "dp", axis=dp_axis, tiled=True)
    return lax.all_gather(values, "section", axis=section_axis, tiled=True)


def shard(values, dp_axis, section_axis):
    values = lax.psum_scatter(values, "section", scatter_dimension=section_axis, tiled=True)
    return lax.psum_scatter(values, "dp", scatter_dimension=dp_axis, tiled=True)


def body(
    features,
    packing,
    segment_ids,
    norm1_gain,
    norm1_shift,
    project_weight,
    project_bias,
    merge_weight,
    merge_bias,
    norm2_gain,
    norm2_shift,
    expand_weight,
    expand_bias,
    reduce_weight,
    reduce_bias,
    cotangent,
):
    length = packing.shape[2]
    width = features.shape[2]
    heads = width // HEAD_DIM
    scale = HEAD_DIM ** (-0.5)
    mine = lax.axis_index("section")
    order = lax.dynamic_index_in_dim(packing[:, 0], mine, 0, keepdims=False)
    packed_labels = lax.dynamic_index_in_dim(segment_ids[:, 0], mine, 0, keepdims=False)
    labels = jnp.zeros((length,), jnp.int32).at[order].set(packed_labels)
    allowed = labels[:, None] == labels[None, :]

    tokens = swap_rows(features).astype(F32)
    upstream = swap_rows(cotangent)
    project = whole(project_weight, 1, 2)
    merge = whole(merge_weight, 1, 0)
    expand = whole(expand_weight, 0, 1)
    reduce = whole(reduce_weight, 1, 0)

    normed = norm_rows(tokens, norm1_gain, norm1_shift).astype(BF16)
    projected = jnp.einsum("td,cde->cte", normed, project, preferred_element_type=F32)
    queries = (projected[0] + project_bias[0]).astype(BF16).reshape(length, heads, HEAD_DIM)
    keys = projected[1].astype(BF16).reshape(length, heads, HEAD_DIM)
    values = (projected[2] + project_bias[1]).astype(BF16).reshape(length, heads, HEAD_DIM)
    scores = jnp.einsum("qhd,khd->hqk", queries, keys, preferred_element_type=F32) * scale
    scores = jnp.where(allowed[None], scores, MASKED)
    peak = jnp.max(scores, axis=-1, keepdims=True)
    weights = jnp.exp(scores - peak)
    probs = weights / jnp.sum(weights, axis=-1, keepdims=True)
    low_probs = probs.astype(BF16)
    mixed = jnp.einsum("hqk,khd->qhd", low_probs, values, preferred_element_type=F32)
    mixed = mixed.reshape(length, width).astype(BF16)
    middle = tokens + (jnp.dot(mixed, merge, preferred_element_type=F32) + merge_bias)
    normed_two = norm_rows(middle, norm2_gain, norm2_shift).astype(BF16)
    hidden = jnp.dot(normed_two, expand, preferred_element_type=F32) + expand_bias
    active = exact_gelu(hidden).astype(BF16)
    second = jnp.dot(active, reduce, preferred_element_type=F32)
    output = swap_back((middle + (second + reduce_bias)).astype(BF16))

    wide_upstream = upstream.astype(F32)
    reduce_bias_grad = jnp.sum(wide_upstream, axis=0)
    reduce_grad = jnp.einsum("tf,td->fd", active, upstream, preferred_element_type=F32)
    grad_active = jnp.einsum("td,fd->tf", upstream, reduce, preferred_element_type=F32)
    _, gelu_back = jax.vjp(exact_gelu, hidden)
    grad_hidden = gelu_back(grad_active)[0].astype(BF16)
    expand_bias_grad = jnp.sum(grad_hidden.astype(F32), axis=0)
    expand_grad = jnp.einsum("td,tf->df", normed_two, grad_hidden, preferred_element_type=F32)
    grad_normed_two = jnp.einsum("tf,df->td", grad_hidden, expand, preferred_element_type=F32)
    _, norm_back = jax.vjp(norm_rows, middle, norm2_gain, norm2_shift)
    grad_from_norm, gain_two, shift_two = norm_back(grad_normed_two)
    grad_middle = wide_upstream + grad_from_norm
    grad_branch = grad_middle.astype(BF16)
    merge_bias_grad = jnp.sum(grad_branch.astype(F32), axis=0)
    merge_grad = jnp.einsum("te,td->ed", mixed, grad_branch, preferred_element_type=F32)
    grad_mixed = jnp.einsum("td,ed->te", grad_branch, merge, preferred_element_type=F32)
    grad_mixed = grad_mixed.astype(BF16).reshape(length, heads, HEAD_DIM)
    grad_probs = jnp.einsum("qhd,khd->hqk", grad_mixed, values, preferred_element_type=F32)
    inner = jnp.sum(probs * grad_probs, axis=-1, keepdims=True)
    grad_scores = (probs * (grad_probs - inner)).astype(BF16)
    grad_queries = jnp.einsum("hqk,khd->qhd", grad_scores, keys, preferred_element_type=F32) * scale
    grad_keys = jnp.einsum("hqk,qhd->khd", grad_scores, queries, preferred_element_type=F32) * scale
    grad_values = jnp.einsum("hqk,qhd->khd", low_probs, grad_mixed, preferred_element_type=F32)
    stacked = jnp.stack([grad_queries, grad_keys, grad_values])
    stacked = stacked.reshape(3, length, width).astype(BF16)
    wide = stacked.astype(F32)
    project_bias_grad = jnp.stack([jnp.sum(wide[0], axis=0), jnp.sum(wide[2], axis=0)])
    project_grad = jnp.einsum("td,cte->cde", normed, stacked, preferred_element_type=F32)
    grad_normed = jnp.einsum("cte,cde->td", stacked, project, preferred_element_type=F32)
    _, first_back = jax.vjp(norm_rows, tokens, norm1_gain, norm1_shift)
    grad_tokens, gain_one, shift_one = first_back(grad_normed)
    features_grad = swap_back(grad_middle + grad_tokens)

    summed = lax.psum(
        (
            gain_one,
            shift_one,
            project_bias_grad,
            merge_bias_grad,
            gain_two,
            shift_two,
            expand_bias_grad,
            reduce_bias_grad,
        ),
        ("dp", "section"),
    )
    return (
        output,
        features_grad,
        summed[0],
        summed[1],
        shard(project_grad, 1, 2),
        summed[2],
        shard(merge_grad, 1, 0),
        summed[3],
        summed[4],
        summed[5],
        shard(expand_grad, 0, 1),
        summed[6],
        shard(reduce_grad, 1, 0),
        summed[7],
    )


def solution(mesh):
    rows = P(None, ("dp", "section"), None)
    groups = P(None, "dp", None)
    project = P(None, "dp", "section")
    inward = P("section", "dp")
    outward = P("dp", "section")
    in_specs = (rows, groups, groups, P(), P(), project, P(), inward, P(), P(), P(), outward, P(), inward, P(), rows)
    out_specs = (rows, rows, P(), P(), project, P(), inward, P(), P(), P(), outward, P(), inward, P())
    fits = mesh.shape["dp"] == 8 and mesh.shape["section"] == NS
    return jax.shard_map(block if fits else body, mesh=mesh, in_specs=in_specs, out_specs=out_specs, check_vma=False)
```
